32 devices in a mesh: seq: 4 (over x, core), fsdp: 8 (over z, y).
Axes of the slice: x: 2, y: 2, z: 4, core: 2. Of those that a mesh axis runs over, the one named last changes fastest.
Arguments:
- tokens_in: bfloat16 [16, 512, 1024], P('fsdp', 'seq'), may hold values from -6 to 6
- cotangent: bfloat16 [16, 512, 1024], P('fsdp', 'seq'), may hold values from -6 to 6
- query_weight: bfloat16 [1024, 1024], P('fsdp'), may hold values from -0.1875 to 0.1875
- key_weight: bfloat16 [1024, 1024], P('fsdp'), may hold values from -0.1875 to 0.1875
- value_weight: bfloat16 [1024, 1024], P('fsdp'), may hold values from -0.1875 to 0.1875
- out_weight: bfloat16 [1024, 1024], P('fsdp'), may hold values from -1.5 to 1.5
- up_weight: bfloat16 [1024, 4096], P('fsdp'), may hold values from -0.1875 to 0.1875
- down_weight: bfloat16 [4096, 1024], P('fsdp'), may hold values from -0.09375 to 0.09375
- query_bias: bfloat16 [1024], P('fsdp'), may hold values from -4 to 4
- value_bias: bfloat16 [1024], P('fsdp'), may hold values from -0.75 to 0.75
- out_bias: bfloat16 [1024], P('fsdp'), may hold values from -4 to 4
- up_bias: bfloat16 [4096], P('fsdp'), may hold values from -4 to 4
- down_bias: bfloat16 [1024], P('fsdp'), may hold values from -4 to 4
- first_gain: bfloat16 [1024], P('fsdp'), may hold values from 0.25 to 1.75
- first_shift: bfloat16 [1024], P('fsdp'), may hold values from -4 to 4
- second_gain: bfloat16 [1024], P('fsdp'), may hold values from 0.25 to 1.75
- second_shift: bfloat16 [1024], P('fsdp'), may hold values from -4 to 4
Outputs:
- layer_out: bfloat16 [16, 512, 1024], P('fsdp', 'seq')
- input_grad: float32 [16, 512, 1024], P('fsdp', 'seq')
- query_weight_grad: float32 [1024, 1024], P('fsdp')
- key_weight_grad: float32 [1024, 1024], P('fsdp')
- value_weight_grad: float32 [1024, 1024], P('fsdp')
- out_weight_grad: float32 [1024, 1024], P('fsdp')
- up_weight_grad: float32 [1024, 4096], P('fsdp')
- down_weight_grad: float32 [4096, 1024], P('fsdp')
- query_bias_grad: float32 [1024], P('fsdp')
- value_bias_grad: float32 [1024], P('fsdp')
- out_bias_grad: float32 [1024], P('fsdp')
- up_bias_grad: float32 [4096], P('fsdp')
- down_bias_grad: float32 [1024], P('fsdp')
- first_gain_grad: float32 [1024], P('fsdp')
- first_shift_grad: float32 [1024], P('fsdp')
- second_gain_grad: float32 [1024], P('fsdp')
- second_shift_grad: float32 [1024], P('fsdp')
The draws below stay inside these ranges and needn't reach their ends.
All inputs are finite; a program needn't handle non-finite values.
Results may differ from the reference program's by a relative error of at most 0.018.
Values may be sent and summed in bfloat16 or wider, within the bound.
No kernel may reach another device: no remote copies, remote signals or barrier semaphores. Data moves between devices by JAX's collectives and lax.ppermute only.
A program may use at most 192 MiB of HBM per device.

```python
import math
import jax
import jax.numpy as jnp
from jax import lax

D = 1024
H = 16
FF = 4096
HD = 64
LEN = 512
SEQS = 16


def block_levels(own_key, shape, shards, least, largest):
    def one(position, shards_of):
        draws = jax.random.uniform(jax.random.fold_in(jax.random.fold_in(own_key, 6), position), (shards_of,), jnp.float32, least / len(shards), largest / len(shards))
        return jnp.repeat(jnp.exp(draws), shape[position] // shards_of).reshape((-1,) + (1,) * (len(shape) - position - 1))

    factor_of = one(*shards[0])
    for cut in shards[1:]:
        factor_of = factor_of * one(*cut)
    return factor_of


def noise(rng, dims, scale, most, shards=(), kind=jnp.bfloat16):
    level = block_levels(rng, dims, shards, -0.22, 0.18) if shards else 1.0
    array = jax.random.normal(rng, dims, jnp.float32) * scale * level
    return jnp.minimum(jnp.maximum(array, -most), most).astype(kind)


def setup_inputs(seed: int = 0) -> dict:
    arg_keys = jax.random.split(jax.random.key(seed), 18)
    return {
        "tokens_in": noise(arg_keys[0], (SEQS, LEN, D), 1.0, 6.0, ((0, 8), (1, 4))),
        "cotangent": noise(arg_keys[1], (SEQS, LEN, D), 1.0, 6.0, ((0, 8), (1, 4))),
        "query_weight": noise(arg_keys[2], (D, D), D ** -0.5, 0.1875, ((0, 8),)),
        "key_weight": noise(arg_keys[3], (D, D), D ** -0.5, 0.1875, ((0, 8),)),
        "value_weight": noise(arg_keys[4], (D, D), D ** -0.5, 0.1875, ((0, 8),)),
        "out_weight": noise(arg_keys[5], (D, D), (D // 64) ** -0.5, 1.5, ((0, 8),)),
        "up_weight": noise(arg_keys[6], (D, FF), D ** -0.5, 0.1875, ((0, 8),)),
        "down_weight": noise(arg_keys[7], (FF, D), FF ** -0.5, 0.09375, ((0, 8),)),
        "query_bias": noise(arg_keys[8], (D,), 0.3, 4.0, ((0, 8),)),
        "value_bias": noise(arg_keys[9], (D,), 0.05, 0.75, ((0, 8),)),
        "out_bias": noise(arg_keys[10], (D,), 0.3, 4.0, ((0, 8),)),
        "up_bias": noise(arg_keys[11], (FF,), 0.3, 4.0, ((0, 8),)),
        "down_bias": noise(arg_keys[12], (D,), 0.3, 4.0, ((0, 8),)),
        "first_gain": jnp.clip(1.0 + 0.15 * jax.random.normal(arg_keys[13], (D,), jnp.float32), 0.25, 1.75).astype(jnp.bfloat16),
        "first_shift": noise(arg_keys[14], (D,), 0.3, 4.0, ((0, 8),)),
        "second_gain": jnp.clip(1.0 + 0.15 * jax.random.normal(arg_keys[15], (D,), jnp.float32), 0.25, 1.75).astype(jnp.bfloat16),
        "second_shift": noise(arg_keys[16], (D,), 0.3, 4.0, ((0, 8),)),
    }


EPSILON = 1e-05
HIGHEST = lax.Precision.HIGHEST

@jax.custom_vjp
def low(v):
    return lax.optimization_barrier(v.astype(jnp.bfloat16)).astype(jnp.float32)

@jax.custom_vjp
def low_back(v):
    return v

def low_keep(v):
    return (low(v), None)

def low_pass(kept, grad):
    return (grad,)

def back_keep(v):
    return (v, None)

def back_low(kept, grad):
    return (low(grad),)
low.defvjp(low_keep, low_pass)
low_back.defvjp(back_keep, back_low)

def layer_norm(hidden, gain, shift):
    average = lax.optimization_barrier(jnp.mean(hidden, -1, keepdims=True))
    centered = hidden - average
    spread = lax.optimization_barrier(jnp.mean(centered * centered, -1, keepdims=True))
    return centered * lax.rsqrt(spread + EPSILON) * gain + shift

def product(left_side, right_side):
    return jnp.dot(left_side, right_side, precision=HIGHEST)

def attend_sequence(triple):
    query_heads, key_heads, value_heads = triple
    scaling = 1.0 / math.sqrt(HD)
    scores = low_back(jnp.einsum('qhd,khd->hqk', query_heads, key_heads, precision=HIGHEST) * scaling)
    attention = jax.nn.softmax(scores, axis=-1)
    return jnp.einsum('hqk,khd->qhd', low(attention), value_heads, precision=HIGHEST)

def forward(sequences, params):
    query_weight, key_weight, value_weight, out_weight, up_weight, down_weight, query_bias, value_bias, out_bias, up_bias, down_bias, first_gain, first_shift, second_gain, second_shift = params
    number = sequences.shape[0]
    token_rows = sequences.reshape(number * LEN, D)
    query_rows = low(low_back(product(token_rows, query_weight) + query_bias))
    key_rows = low(low_back(product(token_rows, key_weight)))
    value_rows = low(low_back(product(token_rows, value_weight) + value_bias))
    shaped = (query_rows.reshape(number, LEN, H, HD), key_rows.reshape(number, LEN, H, HD), value_rows.reshape(number, LEN, H, HD))
    mixture = lax.map(jax.checkpoint(attend_sequence), shaped)
    mixture_rows = low(low_back(mixture.reshape(number * LEN, D)))
    attn_sum = token_rows + low_back(product(mixture_rows, out_weight) + out_bias)
    normed_first = layer_norm(attn_sum, first_gain, first_shift)
    up_rows = low_back(product(low(normed_first), up_weight) + up_bias)
    gelu_rows = low(jax.nn.gelu(up_rows, approximate=False))
    ffn_sum = normed_first + low_back(product(gelu_rows, down_weight) + down_bias)
    return layer_norm(ffn_sum, second_gain, second_shift).reshape(number, LEN, D)

def reference(tokens_in, cotangent, query_weight, key_weight, value_weight, out_weight, up_weight, down_weight, query_bias, value_bias, out_bias, up_bias, down_bias, first_gain, first_shift, second_gain, second_shift):
    params = tuple((weight.astype(jnp.float32) for weight in (query_weight, key_weight, value_weight, out_weight, up_weight, down_weight, query_bias, value_bias, out_bias, up_bias, down_bias, first_gain, first_shift, second_gain, second_shift)))
    group_size = math.gcd(SEQS, max(1, 4096 // LEN))
    blocks_in = tokens_in.astype(jnp.float32).reshape(SEQS // group_size, group_size, LEN, D)
    blocks_cot = cotangent.astype(jnp.float32).reshape(SEQS // group_size, group_size, LEN, D)

    def scan_step(summed, paired):
        block_in, block_cot = paired
        layer_block, pullback = jax.vjp(forward, block_in, params)
        block_grad, param_grads = pullback(block_cot)
        return (jax.tree.map(jnp.add, summed, param_grads), (layer_block.astype(jnp.bfloat16), block_grad))
    initial = tuple((jnp.zeros_like(weight) for weight in params))
    summed, (layer_blocks, grad_blocks) = lax.scan(scan_step, initial, (blocks_in, blocks_cot))
    return (layer_blocks.reshape(SEQS, LEN, D), grad_blocks.reshape(SEQS, LEN, D), summed[0], summed[1], summed[2], summed[3], summed[4], summed[5], summed[6], summed[7], summed[8], summed[9], summed[10], summed[11], summed[12], summed[13], summed[14])
```

```python
import functools
import math

import jax
import jax.numpy as jnp
from jax import lax
from jax.experimental import pallas as pl
from jax.experimental.pallas import tpu as pltpu
from jax.sharding import Mesh, PartitionSpec as P

HD = 64
EPSILON = 1e-05
F32 = jnp.float32
BF16 = jnp.bfloat16
SEQ = ("x", "c")
FSDP = ("z", "y")
SEQ_N = 4
VEC = 16
ROW_QB, ROW_VB, ROW_OB, ROW_DB, ROW_G1, ROW_S1, ROW_G2, ROW_S2, ROW_UB = range(9)
VMEM = pltpu.VMEM
ANY = pl.ANY


def dot(a, b):
    return lax.dot_general(a, b, (((1,), (0,)), ((), ())), preferred_element_type=F32)


def dot_nt(a, b):
    return lax.dot_general(a, b, (((1,), (1,)), ((), ())), preferred_element_type=F32)


def dot_tn(a, b):
    return lax.dot_general(a, b, (((0,), (0,)), ((), ())), preferred_element_type=F32)


def struct(shape, dtype):
    return jax.ShapeDtypeStruct(shape, dtype)


def nbytes(tree):
    return sum(math.prod(a.shape) * a.dtype.itemsize for a in jax.tree.leaves(tree))


def whole(space=VMEM):
    return pl.BlockSpec(memory_space=space)


def call(kernel, outs, args, *, name, grid=None, in_specs=None, out_specs=None, scratch=(), flops=0, trans=0):
    if in_specs is None:
        in_specs = [whole() for _ in args]
    if out_specs is None:
        out_specs = jax.tree.map(lambda _: whole(), outs)
    kwargs = {} if grid is None else {"grid": grid}
    return pl.pallas_call(
        kernel,
        out_shape=outs,
        in_specs=in_specs,
        out_specs=out_specs,
        scratch_shapes=list(scratch),
        compiler_params=pltpu.CompilerParams(vmem_limit_bytes=56 << 20),
        cost_estimate=pl.CostEstimate(
            flops=flops, bytes_accessed=nbytes(args) + nbytes(outs), transcendentals=trans
        ),
        name=name,
        **kwargs,
    )(*args)


def seq_swap(value, k):
    return lax.ppermute(value, SEQ, [(i, i ^ k) for i in range(SEQ_N)])


def gather_seq(value):
    far = seq_swap(value, 2)
    near = seq_swap(value, 1)
    return [value, near, far, seq_swap(far, 1)]


def reduce_seq(parts):
    near0 = seq_swap(parts[1], 1)
    near2 = seq_swap(parts[3], 1)
    onward = (parts[2].astype(F32) + near2.astype(F32)).astype(BF16)
    return [parts[0], near0, seq_swap(onward, 2)]


def exchange_seq(parts):
    return [parts[0]] + [seq_swap(parts[r], r) for r in (1, 2, 3)]


def fsdp_swap(value, k, count):
    return lax.ppermute(value, FSDP, [(i, i ^ k) for i in range(count)])


def early_pack_kernel(ids, wq, wk, wv, wo, vec, out, sems):
    s = ids[0]
    n = wq.shape[0]
    c = wq.shape[1] // SEQ_N
    cols = pl.ds(pl.multiple_of(s * c, c), c)
    copies = [
        pltpu.make_async_copy(w.at[:, cols], out.at[pl.ds(0, n), pl.ds(i * c, c)], sems.at[i])
        for i, w in enumerate((wq, wk, wv, wo))
    ]
    copies.append(
        pltpu.make_async_copy(vec, out.at[pl.ds(n, VEC), pl.ds(0, n)], sems.at[SEQ_N])
    )
    for copy in copies:
        copy.start()
    for copy in copies:
        copy.wait()


def late_pack_kernel(fs, ids, up, down, out, sems):
    s = ids[0]
    n = up.shape[0]
    w = up.shape[1] // fs // SEQ_N
    copies = []
    for j in range(fs):
        cols = pl.ds(pl.multiple_of((j * SEQ_N + s) * w, w), w)
        copies.append(
            pltpu.make_async_copy(
                up.at[:, cols], out.at[pl.ds(0, n), pl.ds(j * w, w)], sems.at[j]
            )
        )
    rows = pl.ds(pl.multiple_of(s * w, w), w)
    copies.append(pltpu.make_async_copy(down.at[rows, :], out.at[pl.ds(n, w), :], sems.at[fs]))
    for copy in copies:
        copy.start()
    for copy in copies:
        copy.wait()


def pack_weights(ids, s, fs, wq, wk, wv, wo, up, down, vectors):
    n, d = wq.shape
    up_bias = vectors.pop("up_bias")
    rows = jnp.stack([vectors[k] for k in sorted(vectors)], 0)
    rows = jnp.concatenate([rows, up_bias.reshape(SEQ_N, n)], 0)
    vec = jnp.pad(rows, ((0, VEC - rows.shape[0]), (0, 0)))
    w = up.shape[1] // fs // SEQ_N
    c = d // SEQ_N
    if n % 128 == 0:
        early = call(
            early_pack_kernel,
            struct((n + VEC, d), BF16),
            (ids, wq, wk, wv, wo, vec),
            name="early_pack",
            in_specs=[whole(pltpu.SMEM)] + [whole(ANY)] * 5,
            out_specs=whole(ANY),
            scratch=[pltpu.SemaphoreType.DMA((SEQ_N + 1,))],
        )
        late = call(
            functools.partial(late_pack_kernel, fs),
            struct((n + w, d), BF16),
            (ids, up, down),
            name="late_pack",
            in_specs=[whole(pltpu.SMEM)] + [whole(ANY)] * 2,
            out_specs=whole(ANY),
            scratch=[pltpu.SemaphoreType.DMA((fs + 1,))],
        )
        return early, late
    four = [lax.dynamic_slice(m, (0, s * c), (n, c)) for m in (wq, wk, wv, wo)]
    early = jnp.concatenate(
        [jnp.concatenate(four, 1), jnp.pad(vec, ((0, 0), (0, d - n)))], 0
    )
    mine = lax.dynamic_index_in_dim(up.reshape(n, fs, SEQ_N, w), s, 2, keepdims=False)
    late = jnp.concatenate(
        [mine.reshape(n, fs * w), lax.dynamic_slice(down, (s * w, 0), (w, d))], 0
    )
    return early, late


def assemble_kernel(fs, ids, *refs):
    pieces, (wqkv, wo, vec, held, sems) = refs[:fs], refs[fs:]
    f = ids[1]
    n = pieces[0].shape[0] - VEC
    c3 = wqkv.shape[1]
    c = wo.shape[1]
    copies, vecs = [], []
    for g in range(fs):
        place = pl.multiple_of((f ^ g) * n, n)
        vecs.append(
            pltpu.make_async_copy(
                pieces[g].at[pl.ds(n, VEC), pl.ds(0, n)], held.at[g], sems.at[g, 0]
            )
        )
        copies.append(
            pltpu.make_async_copy(
                pieces[g].at[pl.ds(0, n), pl.ds(0, c3)], wqkv.at[pl.ds(place, n), :], sems.at[g, 1]
            )
        )
        copies.append(
            pltpu.make_async_copy(
                pieces[g].at[pl.ds(0, n), pl.ds(c3, c)], wo.at[pl.ds(place, n), :], sems.at[g, 2]
            )
        )
    for copy in vecs + copies:
        copy.start()
    for g in range(fs):
        vecs[g].wait()
        vec[:, pl.ds(pl.multiple_of((f ^ g) * n, n), n)] = held[g].astype(F32)
    for copy in copies:
        copy.wait()


def gather_early(ids, early, fs):
    n = early.shape[0] - VEC
    d = early.shape[1]
    c = d // SEQ_N
    if fs == 8 and n % 128 == 0:
        pieces = [None] * fs
        pieces[0] = early
        for g in (2, 4, 6):
            pieces[g] = fsdp_swap(early, g, fs)
        for g in (0, 2, 4, 6):
            pieces[g + 1] = fsdp_swap(pieces[g], 1, fs)
        outs = (struct((d, 3 * c), BF16), struct((d, c), BF16), struct((VEC, d), F32))
        return call(
            functools.partial(assemble_kernel, fs),
            outs,
            (ids, *pieces),
            name="assemble",
            in_specs=[whole(pltpu.SMEM)] + [whole(ANY)] * fs,
            out_specs=(whole(ANY), whole(ANY), whole()),
            scratch=[VMEM((fs, VEC, n), BF16), pltpu.SemaphoreType.DMA((fs, 3))],
        )
    full = lax.all_gather(early, FSDP)
    weights = full[:, :n].reshape(d, d)
    vec = full[:, n:, :n].transpose(1, 0, 2).reshape(VEC, d).astype(F32)
    return weights[:, : 3 * c], weights[:, 3 * c :], vec


def attend_kernel(ids, x0, x1, x2, x3, w, vec, qkv, lse, m0, m1, m2, m3, held, mix):
    c = w.shape[1] // 3
    heads = c // HD
    block = x0.shape[1]
    length = SEQ_N * block
    for r, x in enumerate((x0, x1, x2, x3)):
        held[r * block : (r + 1) * block, :] = x[0]
    cols = pl.ds(pl.multiple_of(ids[0] * c, c), c)
    for part in range(3):
        acc = dot(held[...], w[:, part * c : (part + 1) * c])
        if part != 1:
            row = ROW_QB if part == 0 else ROW_VB
            acc = acc + vec[row : row + 1, cols]
        qkv[0, :, part * c : (part + 1) * c] = acc.astype(BF16)
    scale = 1.0 / math.sqrt(HD)
    for h in range(heads):
        at = h * HD
        query = (qkv[0, :, at : at + HD].astype(F32) * scale).astype(BF16)
        key = qkv[0, :, c + at : c + at + HD]
        value = qkv[0, :, 2 * c + at : 2 * c + at + HD]
        scores = dot_nt(key, query)
        highest = jnp.max(scores, 0, keepdims=True)
        raised = jnp.exp(scores - highest)
        summed = jnp.sum(raised, 0, keepdims=True)
        lse[0, h : h + 1, :] = highest + jnp.log(summed)
        low = (raised * (1.0 / summed)).astype(BF16)
        mix[at : at + HD, :] = dot_tn(value, low)
    mixture = mix[...].T.astype(BF16)
    for r, m in enumerate((m0, m1, m2, m3)):
        m[0] = mixture[r * block : (r + 1) * block, :]


def attend(ids, blocks, wqkv, vec):
    nb, block, d = blocks[0].shape
    c = wqkv.shape[1] // 3
    length = SEQ_N * block
    heads = c // HD
    one = lambda shape: pl.BlockSpec((1,) + shape, lambda b: (b,) + (0,) * len(shape))
    fixed = lambda shape: pl.BlockSpec(shape, lambda b: (0,) * len(shape))
    outs = (
        struct((nb, length, 3 * c), BF16),
        struct((nb, heads, length), F32),
    ) + (struct((nb, block, c), BF16),) * SEQ_N
    return call(
        attend_kernel,
        outs,
        (ids, *blocks, wqkv, vec),
        name="attend",
        grid=(nb,),
        in_specs=[whole(pltpu.SMEM)]
        + [one((block, d))] * SEQ_N
        + [fixed(wqkv.shape), fixed(vec.shape)],
        out_specs=(one((length, 3 * c)), one((heads, length))) + (one((block, c)),) * SEQ_N,
        scratch=[VMEM((length, d), BF16), VMEM((c, length), F32)],
        flops=2 * nb * length * (3 * c * d + 2 * length * c),
        trans=nb * heads * length * length,
    )


def attend_back_kernel(qkv, lse, h0, h1, h2, h3, w, back, sums, r0, r1, r2, r3, held, turned):
    c = w.shape[1] // 3
    heads = c // HD
    block = h0.shape[1]
    for r, h in enumerate((h0, h1, h2, h3)):
        held[r * block : (r + 1) * block, :] = h[0]
    scale = 1.0 / math.sqrt(HD)
    for h in range(heads):
        at = h * HD
        query = (qkv[0, :, at : at + HD].astype(F32) * scale).astype(BF16)
        key = qkv[0, :, c + at : c + at + HD]
        value = qkv[0, :, 2 * c + at : 2 * c + at + HD]
        grad = held[:, at : at + HD]
        scores = dot_nt(key, query)
        attention = jnp.exp(scores - lse[0, h : h + 1, :])
        attention_grad = dot_nt(value, grad)
        inner = jnp.sum(attention * attention_grad, 0, keepdims=True)
        low = (attention * (attention_grad - inner)).astype(BF16)
        turned[at : at + HD, :] = dot_tn(key, low) * scale
        back[0, :, c + at : c + at + HD] = dot(low, query).astype(BF16)
        back[0, :, 2 * c + at : 2 * c + at + HD] = dot(attention.astype(BF16), grad).astype(BF16)
    back[0, :, 0:c] = turned[...].T.astype(BF16)
    whole_back = back[0]
    total = jnp.sum(whole_back.astype(F32), 0, keepdims=True)

    @pl.when(pl.program_id(0) == 0)
    def _():
        sums[...] = jnp.zeros_like(sums)

    sums[0:1, :] += total
    for r, out in enumerate((r0, r1, r2, r3)):
        out[0] = dot_nt(back[0, r * block : (r + 1) * block, :], w[...]).astype(BF16)


def attend_back(qkv, lse, grads, wqkv):
    nb, length, c3 = qkv.shape
    d = wqkv.shape[0]
    block = length // SEQ_N
    c = c3 // 3
    heads = c // HD
    one = lambda shape: pl.BlockSpec((1,) + shape, lambda b: (b,) + (0,) * len(shape))
    fixed = lambda shape: pl.BlockSpec(shape, lambda b: (0,) * len(shape))
    outs = (struct((nb, length, c3), BF16), struct((8, c3), F32)) + (
        struct((nb, block, d), BF16),
    ) * SEQ_N
    return call(
        attend_back_kernel,
        outs,
        (qkv, lse, *grads, wqkv),
        name="attend_back",
        grid=(nb,),
        in_specs=[one((length, c3)), one((heads, length))]
        + [one((block, c))] * SEQ_N
        + [fixed(wqkv.shape)],
        out_specs=(one((length, c3)), fixed((8, c3))) + (one((block, d)),) * SEQ_N,
        scratch=[VMEM((length, c), BF16), VMEM((c, length), F32)],
        flops=2 * nb * length * (c3 * d + 5 * length * c),
        trans=nb * heads * length * length,
    )


def row_norm(hidden):
    average = jnp.mean(hidden, -1, keepdims=True)
    centered = hidden - average
    spread = jnp.mean(centered * centered, -1, keepdims=True)
    scale = lax.rsqrt(spread + EPSILON)
    return centered * scale, scale


def norm_back(grad, normed, scale, gain):
    inner = grad * gain
    first = jnp.mean(inner, -1, keepdims=True)
    second = jnp.mean(inner * normed, -1, keepdims=True)
    return scale * (inner - first - normed * second)


def out_kernel(ids, m0, m1, m2, m3, w0, w1, w2, w3, tokens, vec, attn_sum, normed, low, mix):
    s = ids[0]
    c = m0.shape[1]
    places = [pl.ds(pl.multiple_of((s ^ r) * c, c), c) for r in range(SEQ_N)]
    for place, m in zip(places, (m0, m1, m2, m3)):
        mix[:, place] = m[...]
    for place, w in zip(places, (w0, w1, w2, w3)):
        attn_sum[:, place] = dot(mix[...], w[...])
    hidden = tokens[...].astype(F32) + attn_sum[...] + vec[ROW_OB : ROW_OB + 1, :]
    attn_sum[...] = hidden
    unit, _ = row_norm(hidden)
    first = unit * vec[ROW_G1 : ROW_G1 + 1, :] + vec[ROW_S1 : ROW_S1 + 1, :]
    normed[...] = first
    low[...] = first.astype(BF16)


def out_project(ids, mixtures, wo, tokens, vec):
    rows, d = tokens.shape
    outs = (
        struct((rows, d), F32),
        struct((rows, d), F32),
        struct((rows, d), BF16),
        struct((rows, d), BF16),
    )
    args = (ids, *mixtures, *wo, tokens, vec)
    return call(
        out_kernel,
        outs,
        args,
        name="out_project",
        in_specs=[whole(pltpu.SMEM)] + [whole()] * (len(args) - 1),
        flops=2 * rows * d * d,
    )


def second_norm_kernel(normed, p0, p1, p2, cotangent, vec, layer_out, ffn_grad, low, sums):
    hidden = (
        normed[...]
        + (p0[...].astype(F32) + p1[...].astype(F32) + p2[...].astype(F32))
        + vec[ROW_DB : ROW_DB + 1, :]
    )
    unit, scale = row_norm(hidden)
    gain = vec[ROW_G2 : ROW_G2 + 1, :]
    layer_out[...] = (unit * gain + vec[ROW_S2 : ROW_S2 + 1, :]).astype(BF16)
    grad = cotangent[...].astype(F32)
    back = norm_back(grad, unit, scale, gain)
    ffn_grad[...] = back
    rounded = back.astype(BF16)
    low[...] = rounded
    sums[...] = jnp.zeros_like(sums)
    sums[0:1, :] = jnp.sum(grad * unit, 0, keepdims=True)
    sums[1:2, :] = jnp.sum(grad, 0, keepdims=True)
    sums[2:3, :] = jnp.sum(rounded.astype(F32), 0, keepdims=True)


def second_norm(normed, parts, cotangent, vec):
    rows, d = normed.shape
    outs = (
        struct((rows, d), BF16),
        struct((rows, d), F32),
        struct((rows, d), BF16),
        struct((8, d), F32),
    )
    return call(
        second_norm_kernel, outs, (normed, *parts, cotangent, vec), name="second_norm", flops=30 * rows * d
    )


def first_norm_kernel(ids, ffn_grad, p0, p1, p2, attn_sum, vec, mix, w0, w1, w2, w3,
                      attn_grad, sums, n0, n1, n2, n3, d0, d1, d2, d3, low, back):
    s = ids[0]
    c = w0.shape[1]
    grad = ffn_grad[...] + (p0[...].astype(F32) + p1[...].astype(F32) + p2[...].astype(F32))
    unit, scale = row_norm(attn_sum[...])
    gain = vec[ROW_G1 : ROW_G1 + 1, :]
    value = norm_back(grad, unit, scale, gain)
    attn_grad[...] = value
    rounded = value.astype(BF16)
    low[...] = rounded
    sums[...] = jnp.zeros_like(sums)
    sums[0:1, :] = jnp.sum(grad * unit, 0, keepdims=True)
    sums[1:2, :] = jnp.sum(grad, 0, keepdims=True)
    sums[2:3, :] = jnp.sum(rounded.astype(F32), 0, keepdims=True)
    places = [pl.ds(pl.multiple_of((s ^ r) * c, c), c) for r in range(SEQ_N)]
    total = dot_nt(low[:, places[0]], w0[...])
    for place, w in zip(places[1:], (w1, w2, w3)):
        total = total + dot_nt(low[:, place], w[...])
    back[...] = total
    for place, n in zip(places, (n0, n1, n2, n3)):
        n[...] = back[:, place].astype(BF16)
    for place, d in zip(places, (d0, d1, d2, d3)):
        d[...] = dot_tn(mix[...], low[:, place]).astype(BF16)


def first_norm(ids, ffn_grad, parts, attn_sum, vec, mix, wo):
    rows, d = ffn_grad.shape
    c = wo[0].shape[1]
    outs = (
        (struct((rows, d), F32), struct((8, d), F32))
        + (struct((rows, c), BF16),) * SEQ_N
        + (struct((d, c), BF16),) * SEQ_N
    )
    args = (ids, ffn_grad, *parts, attn_sum, vec, mix, *wo)
    return call(
        first_norm_kernel,
        outs,
        args,
        name="first_norm",
        in_specs=[whole(pltpu.SMEM)] + [whole()] * (len(args) - 1),
        scratch=[VMEM((rows, d), BF16), VMEM((rows, d), F32)],
        flops=4 * rows * d * d,
    )


TILE = 256
HALF = 512


def ffn_kernel(n, ids, f0, f1, f2, f3, weights, vec, p0, p1, p2, p3, gelu, slope, held, acc):
    fs = weights.shape[0]
    rows, d = f0.shape
    hidden = gelu.shape[1]
    for r, f in enumerate((f0, f1, f2, f3)):
        held[r * rows : (r + 1) * rows, :] = f[...]
    tiles = hidden // TILE
    per = fs // tiles
    inv = 1.0 / math.sqrt(2.0)
    norm = 1.0 / math.sqrt(2.0 * math.pi)

    def step(i, carry):
        part, t = i // tiles, i % tiles
        at = pl.ds(pl.multiple_of(part * HALF, HALF), HALF)
        cols = pl.ds(pl.multiple_of(t * TILE, TILE), TILE)
        up = weights[:, 0:n, cols].reshape(d, TILE)
        u = dot(held[at, :], up) + vec[pl.ds(ROW_UB + ids[0], 1), cols]
        phi = 0.5 * lax.erf(u * inv) + 0.5
        g = (u * phi).astype(BF16)
        gelu[at, cols] = g
        slope[at, cols] = phi + u * (norm * jnp.exp(-0.5 * u * u))
        down = weights[pl.ds(t * per, per), n:, :].reshape(TILE, d)
        y = dot(g, down)

        @pl.when(t == 0)
        def _():
            acc[at, :] = y

        @pl.when(t > 0)
        def _():
            acc[at, :] += y

        return carry

    lax.fori_loop(0, (SEQ_N * rows // HALF) * tiles, step, 0)
    for r, p in enumerate((p0, p1, p2, p3)):
        p[...] = acc[r * rows : (r + 1) * rows, :].astype(BF16)


def ffn(ids, blocks, weights, vec):
    rows, d = blocks[0].shape
    fs = weights.shape[0]
    n = d // fs
    hidden = fs * (weights.shape[1] - n)
    total = SEQ_N * rows
    outs = (struct((rows, d), BF16),) * SEQ_N + (
        struct((total, hidden), BF16),
        struct((total, hidden), F32),
    )
    args = (ids, *blocks, weights, vec)
    return call(
        functools.partial(ffn_kernel, n),
        outs,
        args,
        name="ffn",
        in_specs=[whole(pltpu.SMEM)] + [whole()] * (len(args) - 1),
        scratch=[VMEM((total, d), BF16), VMEM((total, d), F32)],
        flops=4 * total * d * hidden,
        trans=2 * total * hidden,
    )


def ffn_back_kernel(n, d0, d1, d2, d3, weights, slope, q0, q1, q2, q3, up_low, sums, held, acc):
    fs = weights.shape[0]
    rows, d = d0.shape
    hidden = up_low.shape[1]
    for r, x in enumerate((d0, d1, d2, d3)):
        held[r * rows : (r + 1) * rows, :] = x[...]
    tiles = hidden // TILE
    per = fs // tiles
    sums[...] = jnp.zeros_like(sums)

    def step(i, carry):
        part, t = i // tiles, i % tiles
        at = pl.ds(pl.multiple_of(part * HALF, HALF), HALF)
        cols = pl.ds(pl.multiple_of(t * TILE, TILE), TILE)
        down = weights[pl.ds(t * per, per), n:, :].reshape(TILE, d)
        u = (dot_nt(held[at, :], down) * slope[at, cols]).astype(BF16)
        up_low[at, cols] = u
        sums[0:1, cols] += jnp.sum(u.astype(F32), 0, keepdims=True)
        up = weights[:, 0:n, cols].reshape(d, TILE)
        y = dot_nt(u, up)

        @pl.when(t == 0)
        def _():
            acc[at, :] = y

        @pl.when(t > 0)
        def _():
            acc[at, :] += y

        return carry

    lax.fori_loop(0, (SEQ_N * rows // HALF) * tiles, step, 0)
    for r, q in enumerate((q0, q1, q2, q3)):
        q[...] = acc[r * rows : (r + 1) * rows, :].astype(BF16)


def ffn_back(blocks, weights, slope):
    rows, d = blocks[0].shape
    fs = weights.shape[0]
    total, hidden = slope.shape
    outs = (struct((rows, d), BF16),) * SEQ_N + (
        struct((total, hidden), BF16),
        struct((8, hidden), F32),
    )
    return call(
        functools.partial(ffn_back_kernel, d // fs),
        outs,
        (*blocks, weights, slope),
        name="ffn_back",
        scratch=[VMEM((total, d), BF16), VMEM((total, d), F32)],
        flops=4 * total * d * hidden,
    )


def ffn_grads_kernel(f0, f1, f2, f3, up_low, gelu, d0, d1, d2, d3, out, held):
    rows = f0.shape[0]
    per, both, d = out.shape
    n = both // 2

    @pl.when(pl.program_id(0) == 0)
    def _():
        for r, x in enumerate((d0, d1, d2, d3)):
            held[r * rows : (r + 1) * rows, :] = x[...]

    left = jnp.concatenate([f0[...], f1[...], f2[...], f3[...]], 0)
    out[:, 0:n, :] = dot_tn(left, up_low[...]).astype(BF16).reshape(per, n, d)
    out[:, n:, :] = dot_tn(gelu[...], held[...]).astype(BF16).reshape(per, n, d)


def ffn_grads(blocks, up_low, gelu, downs, fs):
    rows, d = blocks[0].shape
    total, hidden = gelu.shape
    steps = d // TILE
    n = d // fs
    col = lambda shape: pl.BlockSpec(shape, lambda i: (0, i))
    fixed = lambda shape: pl.BlockSpec(shape, lambda i: (0,) * len(shape))
    return call(
        ffn_grads_kernel,
        struct((fs, 2 * n, d), BF16),
        (*blocks, up_low, gelu, *downs),
        name="ffn_grads",
        grid=(steps,),
        in_specs=[col((rows, TILE))] * SEQ_N
        + [fixed((total, hidden)), col((total, TILE))]
        + [fixed((rows, d))] * SEQ_N,
        out_specs=pl.BlockSpec((fs // steps, 2 * n, d), lambda i: (i, 0, 0)),
        scratch=[VMEM((total, d), BF16)],
        flops=4 * total * d * hidden,
    )


def qkvo_grads_kernel(x0, x1, x2, x3, back, o0, o1, o2, out, held):
    nb, block, tile = x0.shape
    length = SEQ_N * block
    for b in range(nb):
        for r, x in enumerate((x0, x1, x2, x3)):
            held[b * length + r * block : b * length + (r + 1) * block, :] = x[b]
    c3 = back.shape[1]
    out[:, 0:c3] = dot_tn(held[...], back[...]).astype(BF16)
    total = o0[...].astype(F32) + o1[...].astype(F32) + o2[...].astype(F32)
    out[:, c3:] = total.astype(BF16)


def qkvo_grads(blocks, back, out_parts):
    nb, block, d = blocks[0].shape
    total, c3 = back.shape
    c = c3 // 3
    col = lambda i: (0, 0, i)
    return call(
        qkvo_grads_kernel,
        struct((d, c3 + c), BF16),
        (*blocks, back, *out_parts),
        name="qkvo_grads",
        grid=(d // TILE,),
        in_specs=[pl.BlockSpec((nb, block, TILE), col)] * SEQ_N
        + [pl.BlockSpec((total, c3), lambda i: (0, 0))]
        + [pl.BlockSpec((TILE, c), lambda i: (i, 0))] * 3,
        out_specs=pl.BlockSpec((TILE, c3 + c), lambda i: (i, 0)),
        scratch=[VMEM((total, TILE), BF16)],
        flops=2 * total * d * c3,
    )


def fill_vectors(s, vec, back_sums, first_sums, second_sums, up_sums):
    c = vec.shape[1] // SEQ_N
    vec[...] = jnp.zeros_like(vec)
    cols = pl.ds(pl.multiple_of(s * c, c), c)
    vec[ROW_QB : ROW_QB + 1, cols] = back_sums[0:1, 0:c]
    vec[ROW_VB : ROW_VB + 1, cols] = back_sums[0:1, 2 * c : 3 * c]
    vec[ROW_OB : ROW_OB + 1, :] = first_sums[2:3, :]
    vec[ROW_DB : ROW_DB + 1, :] = second_sums[2:3, :]
    vec[ROW_G1 : ROW_G1 + 1, :] = first_sums[0:1, :]
    vec[ROW_S1 : ROW_S1 + 1, :] = first_sums[1:2, :]
    vec[ROW_G2 : ROW_G2 + 1, :] = second_sums[0:1, :]
    vec[ROW_S2 : ROW_S2 + 1, :] = second_sums[1:2, :]
    vec[pl.ds(ROW_UB + s, 1), :] = up_sums[0:1, :]


def split_kernel(fs, ids, grads, back_sums, first_sums, second_sums, up_sums, *refs):
    outs, (vec, vec_low, sems) = refs[:fs], refs[fs:]
    s, f = ids[0], ids[1]
    n = outs[0].shape[0] - VEC
    copies = []
    for g in range(fs):
        rows = pl.ds(pl.multiple_of((f ^ g) * n, n), n)
        copies.append(
            pltpu.make_async_copy(grads.at[rows, :], outs[g].at[pl.ds(0, n), :], sems.at[g, 0])
        )
    for copy in copies:
        copy.start()
    fill_vectors(s, vec, back_sums, first_sums, second_sums, up_sums)
    vec_low[...] = jnp.zeros_like(vec_low)
    small = []
    for g in range(fs):
        cols = pl.ds(pl.multiple_of((f ^ g) * n, n), n)
        vec_low[g * VEC : (g + 1) * VEC, 0:n] = vec[:, cols].astype(BF16)
        small.append(
            pltpu.make_async_copy(
                vec_low.at[pl.ds(g * VEC, VEC), :], outs[g].at[pl.ds(n, VEC), :], sems.at[g, 1]
            )
        )
    for copy in small:
        copy.start()
    for copy in copies + small:
        copy.wait()


def vectors_kernel(ids, back_sums, first_sums, second_sums, up_sums, vec):
    fill_vectors(ids[0], vec, back_sums, first_sums, second_sums, up_sums)


def scatter_late(ids, grads, sums, fs):
    d = grads.shape[0]
    n = d // fs
    if fs == 8 and n % 128 == 0:
        pieces = call(
            functools.partial(split_kernel, fs),
            (struct((n + VEC, d), BF16),) * fs,
            (ids, grads, *sums),
            name="split",
            in_specs=[whole(pltpu.SMEM), whole(ANY)] + [whole()] * 4,
            out_specs=(whole(ANY),) * fs,
            scratch=[
                VMEM((VEC, d), F32),
                VMEM((fs * VEC, d), BF16),
                pltpu.SemaphoreType.DMA((fs, 2)),
            ],
        )
        add = lambda a, b: a.astype(F32) + b.astype(F32)
        total = None
        for g in (2, 4, 6, 0):
            here = add(pieces[g], fsdp_swap(pieces[g + 1], 1, fs))
            if g:
                here = fsdp_swap(here.astype(BF16), g, fs).astype(F32)
            total = here if total is None else total + here
        return total.astype(BF16)
    vec = call(
        vectors_kernel,
        struct((VEC, d), F32),
        (ids, *sums),
        name="vectors",
        in_specs=[whole(pltpu.SMEM)] + [whole()] * 4,
    )
    small = vec.reshape(VEC, fs, n).transpose(1, 0, 2).astype(BF16)
    small = jnp.pad(small, ((0, 0), (0, 0), (0, d - n)))
    packed = jnp.concatenate([grads.reshape(fs, n, d), small], 1)
    return lax.psum_scatter(packed.reshape(fs * (n + VEC), d), FSDP, scatter_dimension=0, tiled=True)


def finish_kernel(fs, ids, c0, c1, c2, c3, e0, e1, e2, e3, wq, wk, wv, wo, up, down, *vectors):
    s = ids[0]
    n = wq.shape[0]
    c = wq.shape[1] // SEQ_N
    w = up.shape[1] // fs // SEQ_N
    total = 0.0
    for r, (small, large) in enumerate(((c0, e0), (c1, e1), (c2, e2), (c3, e3))):
        at = s ^ r
        cols = pl.ds(pl.multiple_of(at * c, c), c)
        for i, out in enumerate((wq, wk, wv, wo)):
            out[:, cols] = small[0:n, i * c : (i + 1) * c].astype(F32)
        total = total + small[n:, 0:n].astype(F32)
        for j in range(fs):
            place = pl.ds(pl.multiple_of((j * SEQ_N + at) * w, w), w)
            up[:, place] = large[0:n, j * w : (j + 1) * w].astype(F32)
        down[pl.ds(pl.multiple_of(at * w, w), w), :] = large[n:, :].astype(F32)
    for row, out in enumerate(vectors[:ROW_UB]):
        out[...] = total[row : row + 1, :].reshape(n)
    for j in range(SEQ_N):
        vectors[ROW_UB][j * n : (j + 1) * n] = total[ROW_UB + j : ROW_UB + j + 1, :].reshape(n)


def finish(ids, s, small, large, fs):
    d = small[0].shape[1]
    n = d // fs
    c = d // SEQ_N
    w = large[0].shape[0] - n
    hidden = SEQ_N * fs * w
    if n % 128 == 0:
        outs = (
            (struct((n, d), F32),) * 4
            + (struct((n, hidden), F32), struct((SEQ_N * w, d), F32))
            + (struct((n,), F32),) * ROW_UB
            + (struct((SEQ_N * w,), F32),)
        )
        done = call(
            functools.partial(finish_kernel, fs),
            outs,
            (ids, *small, *large),
            name="finish",
            in_specs=[whole(pltpu.SMEM)] + [whole()] * 8,
        )
        return done[:4], done[4], done[5], done[6:]
    order = jnp.arange(SEQ_N) ^ s
    small = jnp.stack(small)[order].astype(F32)
    large = jnp.stack(large)[order].astype(F32)
    four = small[:, :n].reshape(SEQ_N, n, 4, c).transpose(2, 1, 0, 3).reshape(4, n, d)
    up = large[:, :n].reshape(SEQ_N, n, fs, w).transpose(1, 2, 0, 3).reshape(n, hidden)
    down = large[:, n:].reshape(SEQ_N * w, d)
    total = jnp.sum(small[:, n:, :n], 0)
    vectors = [total[row] for row in range(ROW_UB)]
    vectors.append(total[ROW_UB : ROW_UB + SEQ_N].reshape(SEQ_N * w))
    return [four[i] for i in range(4)], up, down, vectors


def body(fs, tokens_in, cotangent, query_weight, key_weight, value_weight, out_weight, up_weight,
         down_weight, query_bias, value_bias, out_bias, up_bias, down_bias, first_gain, first_shift,
         second_gain, second_shift):
    nb, block, d = tokens_in.shape
    rows = nb * block
    s = lax.axis_index(SEQ)
    f = lax.axis_index(FSDP)
    ids = jnp.stack([s, f]).astype(jnp.int32)
    flat = lambda a: a.reshape(rows, a.shape[-1])
    deep = lambda a: a.reshape(nb, block, a.shape[-1])

    vectors = {
        ROW_QB: query_bias, ROW_VB: value_bias, ROW_OB: out_bias, ROW_DB: down_bias,
        ROW_G1: first_gain, ROW_S1: first_shift, ROW_G2: second_gain, ROW_S2: second_shift,
        "up_bias": up_bias,
    }
    up_bias = vectors.pop("up_bias")
    named = {f"{k:02d}": v for k, v in vectors.items()}
    named["up_bias"] = up_bias
    early, late = pack_weights(
        ids, s, fs, query_weight, key_weight, value_weight, out_weight, up_weight, down_weight, named
    )
    weights = lax.all_gather(late, FSDP)
    tokens = gather_seq(tokens_in)
    wqkv, wo_own, vec = gather_early(ids, early, fs)
    wo = gather_seq(wo_own)

    qkv, lse, *mixtures = attend(ids, tokens, wqkv, vec)
    mixtures = exchange_seq([flat(m) for m in mixtures])
    attn_sum, normed, first_low, mix = out_project(ids, mixtures, wo, flat(tokens_in), vec)
    firsts = gather_seq(first_low)
    *parts, gelu, slope = ffn(ids, firsts, weights, vec)
    layer_out, ffn_grad, down_low, second_sums = second_norm(
        normed, reduce_seq(parts), flat(cotangent), vec
    )
    downs = gather_seq(down_low)
    *parts, up_low, up_sums = ffn_back(downs, weights, slope)
    packed = ffn_grads(firsts, up_low, gelu, downs, fs)
    large = lax.psum_scatter(
        packed.reshape(-1, d), FSDP, scatter_dimension=0, tiled=True
    )
    attn_grad, first_sums, *pieces = first_norm(
        ids, ffn_grad, reduce_seq(parts), attn_sum, vec, mix, wo
    )
    grads = exchange_seq(pieces[:SEQ_N])
    out_parts = reduce_seq(pieces[SEQ_N:])
    back, back_sums, *parts = attend_back(qkv, lse, [deep(g) for g in grads], wqkv)
    qkvo = qkvo_grads(tokens, back.reshape(-1, back.shape[-1]), out_parts)
    small = scatter_late(ids, qkvo, (back_sums, first_sums, second_sums, up_sums), fs)
    terms = reduce_seq([flat(p) for p in parts])
    input_grad = attn_grad + (
        terms[0].astype(F32) + terms[1].astype(F32) + terms[2].astype(F32)
    )
    four, up, down, vecs = finish(ids, s, gather_seq(small), gather_seq(large), fs)
    return (
        deep(layer_out), deep(input_grad), *four, up, down,
        vecs[ROW_QB], vecs[ROW_VB], vecs[ROW_OB], vecs[ROW_UB], vecs[ROW_DB],
        vecs[ROW_G1], vecs[ROW_S1], vecs[ROW_G2], vecs[ROW_S2],
    )


def solution(mesh):
    count, fs = mesh.shape["seq"], mesh.shape["fsdp"]
    assert count == SEQ_N and fs % 4 == 0
    inner = Mesh(mesh.devices.reshape(2, 2, fs // 2, 2), SEQ + FSDP)
    rows, matrix, vector = P(FSDP, SEQ, None), P(FSDP, None), P(FSDP)
    in_specs = (rows,) * 2 + (matrix,) * 6 + (vector,) * 9
    return jax.shard_map(
        functools.partial(body, fs), mesh=inner, in_specs=in_specs, out_specs=in_specs, check_vma=False
    )
```

```python
import functools
import math

import jax
import jax.numpy as jnp
from jax import lax
from jax.experimental import pallas as pl
from jax.experimental.pallas import tpu as pltpu
from jax.sharding import Mesh, PartitionSpec as P

HD = 64
EPSILON = 1e-05
F32 = jnp.float32
BF16 = jnp.bfloat16
SEQ = ("x", "c")
FSDP = ("z", "y")
SEQ_N = 4
VEC = 16
ROW_QB, ROW_VB, ROW_OB, ROW_DB, ROW_G1, ROW_S1, ROW_G2, ROW_S2, ROW_UB = range(9)
VMEM = pltpu.VMEM
ANY = pl.ANY


def dot(a, b):
    return lax.dot_general(a, b, (((1,), (0,)), ((), ())), preferred_element_type=F32)


def dot_nt(a, b):
    return lax.dot_general(a, b, (((1,), (1,)), ((), ())), preferred_element_type=F32)


def dot_tn(a, b):
    return lax.dot_general(a, b, (((0,), (0,)), ((), ())), preferred_element_type=F32)


def struct(shape, dtype):
    return jax.ShapeDtypeStruct(shape, dtype)


def nbytes(tree):
    return sum(math.prod(a.shape) * a.dtype.itemsize for a in jax.tree.leaves(tree))


def whole(space=VMEM):
    return pl.BlockSpec(memory_space=space)


def call(kernel, outs, args, *, name, grid=None, in_specs=None, out_specs=None, scratch=(), flops=0, trans=0):
    if in_specs is None:
        in_specs = [whole() for _ in args]
    if out_specs is None:
        out_specs = jax.tree.map(lambda _: whole(), outs)
    kwargs = {} if grid is None else {"grid": grid}
    return pl.pallas_call(
        kernel,
        out_shape=outs,
        in_specs=in_specs,
        out_specs=out_specs,
        scratch_shapes=list(scratch),
        compiler_params=pltpu.CompilerParams(vmem_limit_bytes=56 << 20),
        cost_estimate=pl.CostEstimate(
            flops=flops, bytes_accessed=nbytes(args) + nbytes(outs), transcendentals=trans
        ),
        name=name,
        **kwargs,
    )(*args)


def seq_swap(value, k):
    with jax.named_scope(f"seq{k}"):
        return lax.ppermute(value, SEQ, [(i, i ^ k) for i in range(SEQ_N)])


def gather_seq(value, *others):
    far = seq_swap(value, 2)
    near = seq_swap(value, 1)
    return [value, near, far, seq_swap(after(far, *others), 1)]


def reduce_seq(parts):
    near0 = seq_swap(parts[1], 1)
    near2 = seq_swap(parts[3], 1)
    onward = (parts[2].astype(F32) + near2.astype(F32)).astype(BF16)
    return [parts[0], near0, seq_swap(onward, 2)], onward


def exchange_seq(parts):
    return [parts[0]] + [seq_swap(parts[r], r) for r in (1, 2, 3)]


def swap_y(value):
    with jax.named_scope("y"):
        return lax.ppermute(value, "y", [(0, 1), (1, 0)])


def swap_z(value, k, count):
    with jax.named_scope(f"z{k}"):
        return lax.ppermute(value, "z", [(i, i ^ k) for i in range(count)])


def turn_z(value):
    with jax.named_scope("z"):
        return lax.all_to_all(value, "z", split_axis=0, concat_axis=0, tiled=True)


def after(value, *others):
    return lax.optimization_barrier((value, *others))[0] if others else value


def fits(n):
    return n % 128 == 0


def run_copies(copies):
    for copy in copies:
        copy.start()
    for copy in copies:
        copy.wait()


def early_pack_kernel(ids, wq, wk, wv, wo, *refs):
    *vectors, up_bias, out, sems = refs
    s = ids[0]
    n = wq.shape[0]
    c = wq.shape[1] // SEQ_N
    cols = pl.ds(pl.multiple_of(s * c, c), c)
    copies = [
        pltpu.make_async_copy(w.at[:, cols], out.at[pl.ds(0, n), pl.ds(i * c, c)], sems.at[i])
        for i, w in enumerate((wq, wk, wv, wo))
    ]
    for copy in copies:
        copy.start()
    rows = [v[...].astype(F32).reshape(1, n) for v in vectors]
    rows += [up_bias[j * n : (j + 1) * n].astype(F32).reshape(1, n) for j in range(SEQ_N)]
    rows.append(jnp.zeros((VEC - len(rows), n), F32))
    out[n:, 0:n] = jnp.concatenate(rows, 0).astype(BF16)
    out[n:, n:] = jnp.zeros((VEC, out.shape[1] - n), BF16)
    for copy in copies:
        copy.wait()


def late_pack_kernel(fs, ids, up, down, out, sems):
    s = ids[0]
    n = up.shape[0]
    w = up.shape[1] // fs // SEQ_N
    copies = []
    for j in range(fs):
        cols = pl.ds(pl.multiple_of((j * SEQ_N + s) * w, w), w)
        copies.append(
            pltpu.make_async_copy(
                up.at[:, cols], out.at[pl.ds(0, n), pl.ds(j * w, w)], sems.at[j]
            )
        )
    rows = pl.ds(pl.multiple_of(s * w, w), w)
    copies.append(pltpu.make_async_copy(down.at[rows, :], out.at[pl.ds(n, w), :], sems.at[fs]))
    run_copies(copies)


def pack_early(ids, s, wq, wk, wv, wo, vectors, up_bias):
    n, d = wq.shape
    c = d // SEQ_N
    if fits(n):
        return call(
            early_pack_kernel,
            struct((n + VEC, d), BF16),
            (ids, wq, wk, wv, wo, *vectors, up_bias),
            name="early_pack",
            in_specs=[whole(pltpu.SMEM)] + [whole(ANY)] * 4 + [whole()] * (len(vectors) + 1),
            scratch=[pltpu.SemaphoreType.DMA((4,))],
        )
    rows = jnp.concatenate(vectors + [up_bias]).reshape(-1, n)
    vec = jnp.pad(rows, ((0, VEC - rows.shape[0]), (0, d - n)))
    four = [lax.dynamic_slice(m, (0, s * c), (n, c)) for m in (wq, wk, wv, wo)]
    return jnp.concatenate([jnp.concatenate(four, 1), vec], 0)


def pack_late(ids, s, fs, up, down):
    n, d = up.shape[0], down.shape[1]
    w = up.shape[1] // fs // SEQ_N
    if fits(n):
        return call(
            functools.partial(late_pack_kernel, fs),
            struct((n + w, d), BF16),
            (ids, up, down),
            name="late_pack",
            in_specs=[whole(pltpu.SMEM)] + [whole(ANY)] * 2,
            scratch=[pltpu.SemaphoreType.DMA((fs + 1,))],
        )
    mine = lax.dynamic_index_in_dim(up.reshape(n, fs, SEQ_N, w), s, 2, keepdims=False)
    return jnp.concatenate([mine.reshape(n, fs * w), lax.dynamic_slice(down, (s * w, 0), (w, d))], 0)


def gather_early(value, fs, *others):
    zs = fs // 2
    if zs != 4:
        own = turn_z(jnp.broadcast_to(value, (zs,) + value.shape))
        return [own, swap_y(own)]
    own = [value] + [swap_z(value, k, zs) for k in (3, 2, 1)][::-1]
    first = swap_y(value)
    return own + [first] + [swap_y(after(own[k], *others)) for k in (1, 2, 3)]


def load_blocks(pieces, f, first, rows, target, sems):
    zs = target.shape[0] // 2
    y = f & 1
    rows = pl.ds(first, rows)
    cols = pl.ds(0, target.shape[2])
    if len(pieces) == 2:
        return [
            pltpu.make_async_copy(piece.at[j, rows, cols], target.at[2 * j + at], sems.at[i * zs + j])
            for i, (piece, at) in enumerate(zip(pieces, (y, 1 - y)))
            for j in range(zs)
        ]
    return [
        pltpu.make_async_copy(
            piece.at[rows, cols], target.at[f ^ (2 * (i % zs) + i // zs)], sems.at[i]
        )
        for i, piece in enumerate(pieces)
    ]


def attend_kernel(count, ids, x0, x1, x2, x3, *refs):
    pieces = refs[:count]
    qkv, lse, m0, m1, m2, m3, w_out, vec, held, mix, w, small, sems, small_sems = refs[count:]
    fs = w.shape[0]
    n = w.shape[1]
    c = w.shape[2] // 3
    d = fs * n
    heads = c // HD
    block = x0.shape[1]
    f = ids[1]
    out_copy = pltpu.make_async_copy(w, w_out, sems.at[fs])

    @pl.when(pl.program_id(0) == 0)
    def _():
        copies = load_blocks(pieces, f, 0, n, w, sems)
        copies += load_blocks(pieces, f, n, VEC, small, small_sems)
        run_copies(copies)
        for j in range(fs):
            vec[:, j * n : (j + 1) * n] = small[j, :, 0:n].astype(F32)
        out_copy.start()

    for r, x in enumerate((x0, x1, x2, x3)):
        held[r * block : (r + 1) * block, :] = x[0]
    cols = pl.ds(pl.multiple_of(ids[0] * c, c), c)
    for part in range(3):
        acc = dot(held[...], w[:, :, part * c : (part + 1) * c].reshape(d, c))
        if part != 1:
            row = ROW_QB if part == 0 else ROW_VB
            acc = acc + vec[row : row + 1, cols]
        qkv[0, :, part * c : (part + 1) * c] = acc.astype(BF16)
    scale = 1.0 / math.sqrt(HD)
    for h in range(heads):
        at = h * HD
        query = (qkv[0, :, at : at + HD].astype(F32) * scale).astype(BF16)
        key = qkv[0, :, c + at : c + at + HD]
        value = qkv[0, :, 2 * c + at : 2 * c + at + HD]
        scores = dot_nt(key, query)
        highest = jnp.max(scores, 0, keepdims=True)
        raised = jnp.exp(scores - highest)
        summed = jnp.sum(raised, 0, keepdims=True)
        lse[0, h : h + 1, :] = highest + jnp.log(summed)
        low = (raised * (1.0 / summed)).astype(BF16)
        mix[at : at + HD, :] = dot_tn(value, low)
    mixture = mix[...].T.astype(BF16)
    for r, m in enumerate((m0, m1, m2, m3)):
        m[0] = mixture[r * block : (r + 1) * block, :]

    @pl.when(pl.program_id(0) == pl.num_programs(0) - 1)
    def _():
        out_copy.wait()


def attend(ids, blocks, pieces, fs):
    nb, block, d = blocks[0].shape
    c = d // SEQ_N
    n = d // fs
    length = SEQ_N * block
    heads = c // HD
    one = lambda shape: pl.BlockSpec((1,) + shape, lambda b: (b,) + (0,) * len(shape))
    fixed = lambda shape: pl.BlockSpec(shape, lambda b: (0,) * len(shape))
    outs = (
        (struct((nb, length, 3 * c), BF16), struct((nb, heads, length), F32))
        + (struct((nb, block, c), BF16),) * SEQ_N
        + (struct((fs, n, 3 * c), BF16), struct((VEC, d), F32))
    )
    return call(
        functools.partial(attend_kernel, len(pieces)),
        outs,
        (ids, *blocks, *pieces),
        name="attend",
        grid=(nb,),
        in_specs=[whole(pltpu.SMEM)] + [one((block, d))] * SEQ_N + [whole(ANY)] * len(pieces),
        out_specs=(one((length, 3 * c)), one((heads, length)))
        + (one((block, c)),) * SEQ_N
        + (whole(ANY), fixed((VEC, d))),
        scratch=[
            VMEM((length, d), BF16),
            VMEM((c, length), F32),
            VMEM((fs, n, 3 * c), BF16),
            VMEM((fs, VEC, max(n, 128)), BF16),
            pltpu.SemaphoreType.DMA((fs + 1,)),
            pltpu.SemaphoreType.DMA((fs,)),
        ],
        flops=2 * nb * length * (3 * c * d + 2 * length * c),
        trans=nb * heads * length * length,
    )


def attend_back_kernel(qkv, lse, h0, h1, h2, h3, w, back, sums, r0, r1, r2, r3, held, turned):
    c = w.shape[1] // 3
    heads = c // HD
    block = h0.shape[1]
    for r, h in enumerate((h0, h1, h2, h3)):
        held[r * block : (r + 1) * block, :] = h[0]
    scale = 1.0 / math.sqrt(HD)
    for h in range(heads):
        at = h * HD
        query = (qkv[0, :, at : at + HD].astype(F32) * scale).astype(BF16)
        key = qkv[0, :, c + at : c + at + HD]
        value = qkv[0, :, 2 * c + at : 2 * c + at + HD]
        grad = held[:, at : at + HD]
        scores = dot_nt(key, query)
        attention = jnp.exp(scores - lse[0, h : h + 1, :])
        attention_grad = dot_nt(value, grad)
        inner = jnp.sum(attention * attention_grad, 0, keepdims=True)
        low = (attention * (attention_grad - inner)).astype(BF16)
        turned[at : at + HD, :] = dot_tn(key, low) * scale
        back[0, :, c + at : c + at + HD] = dot(low, query).astype(BF16)
        back[0, :, 2 * c + at : 2 * c + at + HD] = dot(attention.astype(BF16), grad).astype(BF16)
    back[0, :, 0:c] = turned[...].T.astype(BF16)
    whole_back = back[0]
    total = jnp.sum(whole_back.astype(F32), 0, keepdims=True)

    @pl.when(pl.program_id(0) == 0)
    def _():
        sums[...] = jnp.zeros_like(sums)

    sums[0:1, :] += total
    for r, out in enumerate((r0, r1, r2, r3)):
        out[0] = dot_nt(back[0, r * block : (r + 1) * block, :], w[...]).astype(BF16)


def attend_back(qkv, lse, grads, wqkv):
    nb, length, c3 = qkv.shape
    d = wqkv.shape[0]
    block = length // SEQ_N
    c = c3 // 3
    heads = c // HD
    one = lambda shape: pl.BlockSpec((1,) + shape, lambda b: (b,) + (0,) * len(shape))
    fixed = lambda shape: pl.BlockSpec(shape, lambda b: (0,) * len(shape))
    outs = (struct((nb, length, c3), BF16), struct((8, c3), F32)) + (
        struct((nb, block, d), BF16),
    ) * SEQ_N
    return call(
        attend_back_kernel,
        outs,
        (qkv, lse, *grads, wqkv),
        name="attend_back",
        grid=(nb,),
        in_specs=[one((length, c3)), one((heads, length))]
        + [one((block, c))] * SEQ_N
        + [fixed(wqkv.shape)],
        out_specs=(one((length, c3)), fixed((8, c3))) + (one((block, d)),) * SEQ_N,
        scratch=[VMEM((length, c), BF16), VMEM((c, length), F32)],
        flops=2 * nb * length * (c3 * d + 5 * length * c),
        trans=nb * heads * length * length,
    )


def row_norm(hidden):
    average = jnp.mean(hidden, -1, keepdims=True)
    centered = hidden - average
    spread = jnp.mean(centered * centered, -1, keepdims=True)
    scale = lax.rsqrt(spread + EPSILON)
    return centered * scale, scale


def norm_back(grad, normed, scale, gain):
    inner = grad * gain
    first = jnp.mean(inner, -1, keepdims=True)
    second = jnp.mean(inner * normed, -1, keepdims=True)
    return scale * (inner - first - normed * second)


def out_kernel(ids, m0, m1, m2, m3, w0, w1, w2, w3, tokens, vec,
               attn_sum, normed, low, mix, w, sems):
    s, f = ids[0], ids[1]
    c = m0.shape[1]
    fs, n, d = w.shape
    places = [pl.ds(pl.multiple_of((s ^ r) * c, c), c) for r in range(SEQ_N)]
    copies = []
    for r, (place, wr) in enumerate(zip(places, (w0, w1, w2, w3))):
        copies += load_blocks([wr.at[i] for i in range(wr.shape[0])], f, 0, n, w.at[:, :, place], sems.at[r])
    for copy in copies:
        copy.start()
    for place, m in zip(places, (m0, m1, m2, m3)):
        mix[:, place] = m[...]
    for copy in copies:
        copy.wait()
    for t in range(d // TILE):
        cols = slice(t * TILE, (t + 1) * TILE)
        product = dot(mix[...], w[:, :, cols].reshape(d, TILE))
        attn_sum[:, cols] = (
            tokens[:, cols].astype(F32) + product + vec[ROW_OB : ROW_OB + 1, cols]
        )
    unit, _ = row_norm(attn_sum[...])
    first = unit * vec[ROW_G1 : ROW_G1 + 1, :] + vec[ROW_S1 : ROW_S1 + 1, :]
    normed[...] = first
    low[...] = first.astype(BF16)


def out_project(ids, mixtures, wo, tokens, vec):
    rows, d = tokens.shape
    n = wo[0].shape[-2]
    fs = d // n
    outs = (
        struct((rows, d), F32),
        struct((rows, d), F32),
        struct((rows, d), BF16),
        struct((rows, d), BF16),
        struct((fs, n, d), BF16),
    )
    args = (ids, *mixtures, *wo, tokens, vec)
    return call(
        out_kernel,
        outs,
        args,
        name="out_project",
        in_specs=[whole(pltpu.SMEM)] + [whole()] * SEQ_N + [whole(ANY)] * SEQ_N + [whole()] * 2,
        scratch=[pltpu.SemaphoreType.DMA((SEQ_N, fs))],
        flops=2 * rows * d * d,
    )


def second_norm_kernel(normed, p0, p1, p2, cotangent, vec, layer_out, ffn_grad, low, sums):
    hidden = (
        normed[...]
        + (p0[...].astype(F32) + p1[...].astype(F32) + p2[...].astype(F32))
        + vec[ROW_DB : ROW_DB + 1, :]
    )
    unit, scale = row_norm(hidden)
    gain = vec[ROW_G2 : ROW_G2 + 1, :]
    layer_out[...] = (unit * gain + vec[ROW_S2 : ROW_S2 + 1, :]).astype(BF16)
    grad = cotangent[...].astype(F32)
    back = norm_back(grad, unit, scale, gain)
    ffn_grad[...] = back
    rounded = back.astype(BF16)
    low[...] = rounded
    sums[...] = jnp.zeros_like(sums)
    sums[0:1, :] = jnp.sum(grad * unit, 0, keepdims=True)
    sums[1:2, :] = jnp.sum(grad, 0, keepdims=True)
    sums[2:3, :] = jnp.sum(rounded.astype(F32), 0, keepdims=True)


def second_norm(normed, parts, cotangent, vec):
    rows, d = normed.shape
    outs = (
        struct((rows, d), BF16),
        struct((rows, d), F32),
        struct((rows, d), BF16),
        struct((8, d), F32),
    )
    return call(
        second_norm_kernel, outs, (normed, *parts, cotangent, vec), name="second_norm", flops=30 * rows * d
    )


def first_norm_kernel(ids, ffn_grad, p0, p1, p2, attn_sum, vec, mix, w,
                      attn_grad, sums, n0, n1, n2, n3, low_out, low, back):
    s = ids[0]
    c = n0.shape[1]
    d = ffn_grad.shape[1]
    grad = ffn_grad[...] + (p0[...].astype(F32) + p1[...].astype(F32) + p2[...].astype(F32))
    unit, scale = row_norm(attn_sum[...])
    gain = vec[ROW_G1 : ROW_G1 + 1, :]
    value = norm_back(grad, unit, scale, gain)
    attn_grad[...] = value
    rounded = value.astype(BF16)
    low[...] = rounded
    low_out[...] = rounded
    sums[...] = jnp.zeros_like(sums)
    sums[0:1, :] = jnp.sum(grad * unit, 0, keepdims=True)
    sums[1:2, :] = jnp.sum(grad, 0, keepdims=True)
    sums[2:3, :] = jnp.sum(rounded.astype(F32), 0, keepdims=True)
    back[...] = dot_nt(low[...], w[...].reshape(d, d)).astype(BF16)
    for r, n in enumerate((n0, n1, n2, n3)):
        n[...] = back[:, pl.ds(pl.multiple_of((s ^ r) * c, c), c)]


def first_norm(ids, ffn_grad, parts, attn_sum, vec, mix, wo):
    rows, d = ffn_grad.shape
    c = d // SEQ_N
    outs = (
        (struct((rows, d), F32), struct((8, d), F32))
        + (struct((rows, c), BF16),) * SEQ_N
        + (struct((rows, d), BF16),)
    )
    args = (ids, ffn_grad, *parts, attn_sum, vec, mix, wo)
    return call(
        first_norm_kernel,
        outs,
        args,
        name="first_norm",
        in_specs=[whole(pltpu.SMEM)] + [whole()] * (len(args) - 1),
        scratch=[VMEM((rows, d), BF16), VMEM((rows, d), BF16)],
        flops=2 * rows * d * d,
    )


def out_grads_kernel(ids, mix, low, d0, d1, d2, d3):
    s = ids[0]
    c = d0.shape[1]
    for r, out in enumerate((d0, d1, d2, d3)):
        place = pl.ds(pl.multiple_of((s ^ r) * c, c), c)
        out[...] = dot_tn(mix[...], low[:, place]).astype(BF16)


def out_grads(ids, mix, low):
    rows, d = mix.shape
    c = d // SEQ_N
    return call(
        out_grads_kernel,
        (struct((d, c), BF16),) * SEQ_N,
        (ids, mix, low),
        name="out_grads",
        in_specs=[whole(pltpu.SMEM)] + [whole()] * 2,
        flops=2 * rows * d * d,
    )


TILE = 256


def gelu_and_slope(u):
    phi = 0.5 * lax.erf(u * (1.0 / math.sqrt(2.0))) + 0.5
    bell = u * (jnp.exp(-0.5 * u * u) * (1.0 / math.sqrt(2.0 * math.pi)))
    return u * phi, phi + bell


def ffn_kernel(ids, f0, f1, f2, f3, vec, packed, p0, p1, p2, p3, gelu, slope,
               held, up, down, sems):
    n = up.shape[1]
    up_copies = [pltpu.make_async_copy(packed.at[:, pl.ds(0, n), :], up, sems.at[0])]
    down_copies = [pltpu.make_async_copy(packed.at[:, pl.ds(n, down.shape[1]), :], down, sems.at[1])]
    for copy in up_copies + down_copies:
        copy.start()
    rows, d = f0.shape
    hidden = gelu.shape[1]
    half = 2 * rows
    for i, f in enumerate((f1, f3, f0, f2)):
        held[i * rows : (i + 1) * rows, :] = f[...]
    bias = vec[pl.ds(ROW_UB + ids[0], 1), :]
    outs = (p1, p3, p0, p2)
    for copy in up_copies:
        copy.wait()
    for part in range(2):
        at = slice(part * half, (part + 1) * half)
        for t in range(hidden // TILE):
            cols = slice(t * TILE, (t + 1) * TILE)
            u = dot(held[at, :], up[:, :, cols].reshape(d, TILE)) + bias[:, cols]
            g, b = gelu_and_slope(u)
            gelu[at, cols] = g.astype(BF16)
            slope[at, cols] = b.astype(BF16)
        if part == 0:
            for copy in down_copies:
                copy.wait()
        for t in range(d // TILE):
            cols = slice(t * TILE, (t + 1) * TILE)
            y = dot(gelu[at, :], down[:, :, cols].reshape(hidden, TILE)).astype(BF16)
            outs[2 * part][:, cols] = y[0:rows]
            outs[2 * part + 1][:, cols] = y[rows:]


def weight_scratch(fs, d, hidden):
    return [
        VMEM((fs, d // fs, hidden), BF16),
        VMEM((fs, hidden // fs, d), BF16),
        pltpu.SemaphoreType.DMA((2,)),
    ]


def ffn(ids, blocks, packed, vec, hidden, fs):
    rows, d = blocks[0].shape
    total = SEQ_N * rows
    outs = (struct((rows, d), BF16),) * SEQ_N + (struct((total, hidden), BF16),) * 2
    return call(
        ffn_kernel,
        outs,
        (ids, *blocks, vec, packed),
        name="ffn",
        in_specs=[whole(pltpu.SMEM)] + [whole()] * (SEQ_N + 1) + [whole(ANY)],
        scratch=[VMEM((total, d), BF16)] + weight_scratch(fs, d, hidden),
        flops=4 * total * d * hidden,
        trans=2 * total * hidden,
    )


def ffn_back_kernel(ids, d0, d1, d2, d3, slope, packed, q0, q1, q2, q3, up_low, sums,
                    held, up, down, sems):
    n = up.shape[1]
    up_copies = [pltpu.make_async_copy(packed.at[:, pl.ds(0, n), :], up, sems.at[0])]
    down_copies = [pltpu.make_async_copy(packed.at[:, pl.ds(n, down.shape[1]), :], down, sems.at[1])]
    for copy in down_copies + up_copies:
        copy.start()
    rows, d = d0.shape
    hidden = up_low.shape[1]
    half = 2 * rows
    per = TILE // up.shape[1]
    for i, x in enumerate((d1, d3, d0, d2)):
        held[i * rows : (i + 1) * rows, :] = x[...]
    sums[...] = jnp.zeros_like(sums)
    outs = (q1, q3, q0, q2)
    for copy in down_copies:
        copy.wait()
    for part in range(2):
        at = slice(part * half, (part + 1) * half)
        for t in range(hidden // TILE):
            cols = slice(t * TILE, (t + 1) * TILE)
            rhs = down[t * per : (t + 1) * per].reshape(TILE, d)
            u = (dot_nt(held[at, :], rhs) * slope[at, cols].astype(F32)).astype(BF16)
            up_low[at, cols] = u
            sums[0:1, cols] += jnp.sum(u.astype(F32), 0, keepdims=True)
        if part == 0:
            for copy in up_copies:
                copy.wait()
        for t in range(d // TILE):
            cols = slice(t * TILE, (t + 1) * TILE)
            rhs = up[t * per : (t + 1) * per].reshape(TILE, hidden)
            y = dot_nt(up_low[at, :], rhs).astype(BF16)
            outs[2 * part][:, cols] = y[0:rows]
            outs[2 * part + 1][:, cols] = y[rows:]


def ffn_back(ids, blocks, packed, slope, fs):
    rows, d = blocks[0].shape
    total, hidden = slope.shape
    outs = (struct((rows, d), BF16),) * SEQ_N + (
        struct((total, hidden), BF16),
        struct((8, hidden), F32),
    )
    return call(
        ffn_back_kernel,
        outs,
        (ids, *blocks, slope, packed),
        name="ffn_back",
        in_specs=[whole(pltpu.SMEM)] + [whole()] * (SEQ_N + 1) + [whole(ANY)],
        scratch=[VMEM((total, d), BF16)] + weight_scratch(fs, d, hidden),
        flops=4 * total * d * hidden,
    )


def put_rows(f, tile, value, keep, send, turn):
    n = keep.shape[1]
    per = TILE // (2 * n)
    y = f & 1
    turn[...] = value
    for j in range(per):
        z = tile * per + j
        own = pl.multiple_of((2 * j + y) * n, n)
        other = pl.multiple_of((2 * j + 1 - y) * n, n)
        keep[z, 0:n, :] = turn[pl.ds(own, n), :]
        send[z, 0:n, :] = turn[pl.ds(other, n), :]


def outer_kernel(lefts, ids, *refs):
    left, right = refs[:lefts], refs[lefts:5]
    keep, send, held, turn = refs[5:]
    many = left if lefts > 1 else right
    rows = many[0].shape[0]
    for i, x in enumerate(many):
        held[i * rows : (i + 1) * rows, :] = x[...]
    a, b = (held, right[0]) if lefts > 1 else (left[0], held)
    for t in range(a.shape[1] // TILE):
        value = dot_tn(a[:, t * TILE : (t + 1) * TILE], b[...]).astype(BF16)
        put_rows(ids[1], t, value, keep, send, turn)


def outer(ids, lefts, rights, fs, name):
    rows = lefts[0].shape[0] if len(lefts) > 1 else rights[0].shape[0]
    d, e = lefts[0].shape[1], rights[0].shape[1]
    total = SEQ_N * rows
    return call(
        functools.partial(outer_kernel, len(lefts)),
        (struct((fs // 2, d // fs, e), BF16),) * 2,
        (ids, *lefts, *rights),
        name=name,
        in_specs=[whole(pltpu.SMEM)] + [whole()] * 5,
        scratch=[VMEM((total, d if len(lefts) > 1 else e), BF16), VMEM((TILE, e), BF16)],
        flops=2 * total * d * e,
    )


def add(a, b):
    return (a.astype(F32) + b.astype(F32)).astype(BF16)


def scatter_fsdp(keep, came, *others):
    if isinstance(keep, (list, tuple)):
        total = None
        for k in (1, 2, 3, 0):
            here = keep[k].astype(F32) + came[k].astype(F32)
            if k:
                here = swap_z(here.astype(BF16), k, len(keep)).astype(F32)
            total = here if total is None else total + here
        return total.astype(BF16)
    came = turn_z(after(add(keep, came), *others))
    return jnp.sum(came.astype(F32), 0).astype(BF16)


def fill_vectors(s, vec, back_sums, first_sums, second_sums, up_sums):
    c = vec.shape[1] // SEQ_N
    vec[...] = jnp.zeros_like(vec)
    cols = pl.ds(pl.multiple_of(s * c, c), c)
    vec[ROW_QB : ROW_QB + 1, cols] = back_sums[0:1, 0:c]
    vec[ROW_VB : ROW_VB + 1, cols] = back_sums[0:1, 2 * c : 3 * c]
    vec[ROW_OB : ROW_OB + 1, :] = first_sums[2:3, :]
    vec[ROW_DB : ROW_DB + 1, :] = second_sums[2:3, :]
    vec[ROW_G1 : ROW_G1 + 1, :] = first_sums[0:1, :]
    vec[ROW_S1 : ROW_S1 + 1, :] = first_sums[1:2, :]
    vec[ROW_G2 : ROW_G2 + 1, :] = second_sums[0:1, :]
    vec[ROW_S2 : ROW_S2 + 1, :] = second_sums[1:2, :]
    vec[pl.ds(ROW_UB + s, 1), :] = up_sums[0:1, :]


def qkvo_grads_kernel(ids, x0, x1, x2, x3, back, o0, o1, o2, s0, s1, s2, s3, *refs):
    outs, (held, vec, turn) = refs[:-3], refs[-3:]
    s, f = ids[0], ids[1]
    nb, block, d = x0.shape
    length = SEQ_N * block
    e = back.shape[1]
    n = outs[0].shape[-2] - VEC
    zs = d // (2 * n)
    per = TILE // (2 * n)
    y = f & 1
    for b in range(nb):
        for r, x in enumerate((x0, x1, x2, x3)):
            held[b * length + r * block : b * length + (r + 1) * block, :] = x[b]
    fill_vectors(s, vec, s0, s1, s2, s3)
    if len(outs) > 2:
        for k in (1, 2, 3, 0):
            z = (f >> 1) ^ k
            rows = pl.ds(pl.multiple_of(z * TILE, TILE), TILE)
            turn[:, 0:e] = dot_tn(held[:, rows], back[...]).astype(BF16)
            turn[:, e:] = (
                o0[rows, :].astype(F32) + o1[rows, :].astype(F32) + o2[rows, :].astype(F32)
            ).astype(BF16)
            for out, side in ((outs[k], y), (outs[zs + k], 1 - y)):
                out[0:n, :] = turn[pl.ds(pl.multiple_of(side * n, n), n), :]
                out[n:, :] = jnp.zeros((VEC, out.shape[1]), BF16)
                cols = pl.ds(pl.multiple_of((2 * z + side) * n, n), n)
                out[n:, 0:n] = vec[:, cols].astype(BF16)
        return
    keep, send = outs
    for t in range(d // TILE):
        rows = slice(t * TILE, (t + 1) * TILE)
        turn[:, 0:e] = dot_tn(held[:, rows], back[...]).astype(BF16)
        turn[:, e:] = (
            o0[rows, :].astype(F32) + o1[rows, :].astype(F32) + o2[rows, :].astype(F32)
        ).astype(BF16)
        for j in range(per):
            z = t * per + j
            for out, side in ((keep, y), (send, 1 - y)):
                out[z, 0:n, :] = turn[pl.ds(pl.multiple_of((2 * j + side) * n, n), n), :]
    low = vec[...].astype(BF16)
    for z in range(zs):
        first, second = (low[:, (2 * z + i) * n : (2 * z + i + 1) * n] for i in range(2))
        for out, pick in ((keep, y == 0), (send, y != 0)):
            out[z, n:, :] = jnp.zeros((VEC, out.shape[2]), BF16)
            out[z, n:, 0:n] = jnp.where(pick, first, second)


def qkvo_grads(ids, blocks, back, out_parts, sums, fs):
    nb, block, d = blocks[0].shape
    total, e = back.shape
    n = d // fs
    wide = e + out_parts[0].shape[1]
    if fs == 8 and fits(n):
        outs = (struct((n + VEC, wide), BF16),) * 8
    else:
        outs = (struct((fs // 2, n + VEC, wide), BF16),) * 2
    return call(
        qkvo_grads_kernel,
        outs,
        (ids, *blocks, back, *out_parts, *sums),
        name="qkvo_grads",
        in_specs=[whole(pltpu.SMEM)] + [whole()] * 12,
        scratch=[VMEM((total, d), BF16), VMEM((VEC, d), F32), VMEM((TILE, wide), BF16)],
        flops=2 * total * d * e,
    )


def finish_ffn_kernel(fs, ids, *refs):
    ups, downs, (up, down) = refs[:4], refs[4:8], refs[8:]
    s = ids[0]
    w = up.shape[1] // fs // SEQ_N
    for r in range(SEQ_N):
        at = s ^ r
        for j in range(fs):
            place = pl.ds(pl.multiple_of((j * SEQ_N + at) * w, w), w)
            up[:, place] = ups[r][:, j * w : (j + 1) * w].astype(F32)
        down[pl.ds(pl.multiple_of(at * w, w), w), :] = downs[r][...].astype(F32)


def finish_qkvo_kernel(ids, c0, c1, c2, c3, wq, wk, wv, wo, *vectors):
    s = ids[0]
    n = wq.shape[0]
    c = wq.shape[1] // SEQ_N
    total = 0.0
    for r, small in enumerate((c0, c1, c2, c3)):
        cols = pl.ds(pl.multiple_of((s ^ r) * c, c), c)
        for i, out in enumerate((wq, wk, wv, wo)):
            out[:, cols] = small[0:n, i * c : (i + 1) * c].astype(F32)
        total = total + small[n:, 0:n].astype(F32)
    for row, out in enumerate(vectors[:ROW_UB]):
        out[...] = total[row : row + 1, :].reshape(n)
    for j in range(SEQ_N):
        vectors[ROW_UB][j * n : (j + 1) * n] = total[ROW_UB + j : ROW_UB + j + 1, :].reshape(n)


def finish_ffn(ids, s, ups, downs, fs):
    n = ups[0].shape[0]
    w, d = downs[0].shape
    hidden = SEQ_N * fs * w
    if fits(n):
        return call(
            functools.partial(finish_ffn_kernel, fs),
            (struct((n, hidden), F32), struct((SEQ_N * w, d), F32)),
            (ids, *ups, *downs),
            name="finish_ffn",
            in_specs=[whole(pltpu.SMEM)] + [whole()] * 8,
        )
    order = jnp.arange(SEQ_N) ^ s
    up, down = (jnp.stack(v)[order].astype(F32) for v in (ups, downs))
    return (
        up.reshape(SEQ_N, n, fs, w).transpose(1, 2, 0, 3).reshape(n, hidden),
        down.reshape(SEQ_N * w, d),
    )


def finish_qkvo(ids, s, small):
    n = small[0].shape[0] - VEC
    d = small[0].shape[1]
    c = d // SEQ_N
    if fits(n):
        outs = (struct((n, d), F32),) * 4 + (struct((n,), F32),) * ROW_UB + (struct((SEQ_N * n,), F32),)
        done = call(
            finish_qkvo_kernel,
            outs,
            (ids, *small),
            name="finish_qkvo",
            in_specs=[whole(pltpu.SMEM)] + [whole()] * 4,
        )
        return done[:4], done[4:]
    small = jnp.stack(small)[jnp.arange(SEQ_N) ^ s].astype(F32)
    four = small[:, :n].reshape(SEQ_N, n, 4, c).transpose(2, 1, 0, 3).reshape(4, n, d)
    total = jnp.sum(small[:, n:, :n], 0)
    vectors = [total[row] for row in range(ROW_UB)]
    vectors.append(total[ROW_UB : ROW_UB + SEQ_N].reshape(SEQ_N * n))
    return [four[i] for i in range(4)], vectors


def body(fs, tokens_in, cotangent, query_weight, key_weight, value_weight, out_weight, up_weight,
         down_weight, query_bias, value_bias, out_bias, up_bias, down_bias, first_gain, first_shift,
         second_gain, second_shift):
    nb, block, d = tokens_in.shape
    rows = nb * block
    s = lax.axis_index(SEQ)
    f = lax.axis_index(FSDP)
    ids = jnp.stack([s, f]).astype(jnp.int32)
    flat = lambda a: a.reshape(rows, a.shape[-1])
    deep = lambda a: a.reshape(nb, block, a.shape[-1])

    scope = jax.named_scope
    early = pack_early(
        ids, s, query_weight, key_weight, value_weight, out_weight,
        [query_bias, value_bias, out_bias, down_bias, first_gain, first_shift, second_gain, second_shift],
        up_bias,
    )
    packed = pack_late(ids, s, fs, up_weight, down_weight)
    hidden = up_weight.shape[1] // SEQ_N
    with scope("tok"):
        tokens = gather_seq(tokens_in)
    with scope("wqkv"):
        wqkv = gather_early(early, fs, tokens[2])
    with scope("ffnw"):
        packed = lax.all_gather(after(packed, *wqkv[:5], tokens[2]), FSDP)
    with scope("wo"):
        n = d // fs
        wo = jnp.stack([p[..., :n, 3 * (d // SEQ_N) :] for p in wqkv])
        wo = [wo, seq_swap(wo, 1), seq_swap(wo, 2)]
    qkv, lse, *mixtures, wqkv, vec = attend(ids, tokens, wqkv, fs)
    with scope("wo"):
        wo.append(seq_swap(after(wo[2], vec), 1))
    with scope("mix"):
        mixtures = exchange_seq([flat(m) for m in mixtures])
    attn_sum, normed, first_low, mix, wo = out_project(ids, mixtures, wo, flat(tokens_in), vec)
    with scope("first"):
        firsts = gather_seq(first_low)
    *parts, gelu, slope = ffn(ids, firsts, packed, vec, hidden, fs)
    with scope("ffn"):
        parts, _ = reduce_seq(parts)
    layer_out, ffn_grad, down_low, second_sums = second_norm(normed, parts, flat(cotangent), vec)
    with scope("low"):
        lows = gather_seq(down_low)
    *parts, up_low, up_sums = ffn_back(ids, lows, packed, slope, fs)
    with scope("ffnback"):
        parts, onward = reduce_seq(parts)
        gelu = after(gelu, onward)
    turned = lambda blocks: (blocks[1], blocks[3], blocks[0], blocks[2])
    keep_down, send_down = outer(ids, (gelu,), turned(lows), fs, "down_grads")
    with scope("gdown"):
        came_down = swap_y(send_down)
    keep_up, send_up = outer(ids, turned(firsts), (up_low,), fs, "up_grads")
    parts[0] = after(parts[0], keep_down, keep_up)
    attn_grad, first_sums, *pieces, out_low = first_norm(ids, ffn_grad, parts, attn_sum, vec, mix, wo)
    with scope("mixback"):
        grads = exchange_seq(pieces)
    out_parts = out_grads(ids, mix, out_low)
    came_down = after(came_down, out_parts[0])
    with scope("gup"):
        came_up = swap_y(after(send_up, came_down))
    with scope("gdown"):
        down_grad = scatter_fsdp(keep_down, came_down)
    with scope("outs"):
        out_parts, onward = reduce_seq(out_parts)
    grads[0] = after(grads[0], onward)
    back, back_sums, *parts = attend_back(qkv, lse, [deep(g) for g in grads], wqkv.reshape(d, -1))
    came_up = after(came_up, back)
    with scope("gup"):
        up_grad = scatter_fsdp(keep_up, came_up)
    with scope("fdown"):
        down_full = gather_seq(down_grad)
    back = after(back, came_up, down_grad)
    pieces = qkvo_grads(
        ids, tokens, back.reshape(-1, back.shape[-1]), out_parts,
        (back_sums, first_sums, second_sums, up_sums), fs,
    )
    with scope("fup"):
        up_full = gather_seq(up_grad)
    up, down = finish_ffn(ids, s, up_full, down_full, fs)
    with scope("gqkvo"):
        half = len(pieces) // 2
        keep, send = pieces[:half], pieces[half:]
        if half == 1:
            small = scatter_fsdp(keep[0], swap_y(send[0]), up_grad)
        else:
            came = {k: swap_y(send[k]) for k in (1, 2, 3, 0)}
            small = scatter_fsdp(keep, came)
        small = gather_seq(after(small, up))
    with scope("input"):
        terms, _ = reduce_seq([flat(p) for p in parts])
    input_grad = attn_grad + (
        terms[0].astype(F32) + terms[1].astype(F32) + terms[2].astype(F32)
    )
    four, vecs = finish_qkvo(ids, s, small)
    return (
        deep(layer_out), deep(input_grad), *four, up, down,
        vecs[ROW_QB], vecs[ROW_VB], vecs[ROW_OB], vecs[ROW_UB], vecs[ROW_DB],
        vecs[ROW_G1], vecs[ROW_S1], vecs[ROW_G2], vecs[ROW_S2],
    )


def solution(mesh):
    count, fs = mesh.shape["seq"], mesh.shape["fsdp"]
    assert count == SEQ_N and fs % 4 == 0
    inner = Mesh(mesh.devices.reshape(2, 2, fs // 2, 2), SEQ + FSDP)
    rows, matrix, vector = P(FSDP, SEQ, None), P(FSDP, None), P(FSDP)
    in_specs = (rows,) * 2 + (matrix,) * 6 + (vector,) * 9
    return jax.shard_map(
        functools.partial(body, fs), mesh=inner, in_specs=in_specs, out_specs=in_specs, check_vma=False
    )
```

```python
import functools
import math

import jax
import jax.numpy as jnp
from jax import lax
from jax.experimental import pallas as pl
from jax.experimental.pallas import tpu as pltpu
from jax.sharding import Mesh, PartitionSpec as P

HD = 64
EPSILON = 1e-05
F32 = jnp.float32
BF16 = jnp.bfloat16
SEQ = ("x", "c")
FSDP = ("z", "y")
SEQ_N = 4
VEC = 16
ROW_QB, ROW_VB, ROW_OB, ROW_DB, ROW_G1, ROW_S1, ROW_G2, ROW_S2, ROW_UB = range(9)
VMEM = pltpu.VMEM
ANY = pl.ANY
HBM = pltpu.HBM
LIMITS = {"early_pack": 56, "late_pack": 56}


def dot(a, b):
    return lax.dot_general(a, b, (((1,), (0,)), ((), ())), preferred_element_type=F32)


def dot_nt(a, b):
    return lax.dot_general(a, b, (((1,), (1,)), ((), ())), preferred_element_type=F32)


def dot_tn(a, b):
    return lax.dot_general(a, b, (((0,), (0,)), ((), ())), preferred_element_type=F32)


def struct(shape, dtype):
    return jax.ShapeDtypeStruct(shape, dtype)


def nbytes(tree):
    return sum(math.prod(a.shape) * a.dtype.itemsize for a in jax.tree.leaves(tree))


def whole(space=VMEM):
    return pl.BlockSpec(memory_space=space)


def call(kernel, outs, args, *, name, grid=None, in_specs=None, out_specs=None, scratch=(), flops=0, trans=0, light=1):
    if in_specs is None:
        in_specs = [whole() for _ in args]
    if out_specs is None:
        out_specs = jax.tree.map(lambda _: whole(), outs)
    kwargs = {} if grid is None else {"grid": grid}
    return pl.pallas_call(
        kernel,
        out_shape=outs,
        in_specs=in_specs,
        out_specs=out_specs,
        scratch_shapes=list(scratch),
        compiler_params=pltpu.CompilerParams(vmem_limit_bytes=LIMITS.get(name, 20) << 20),
        cost_estimate=pl.CostEstimate(
            flops=flops // light,
            bytes_accessed=(nbytes(args) + nbytes(outs)) // light,
            transcendentals=trans,
        ),
        name=name,
        **kwargs,
    )(*args)


def seq_swap(value, k):
    with jax.named_scope(f"seq{k}"):
        return lax.ppermute(value, SEQ, [(i, i ^ k) for i in range(SEQ_N)])


def gather_seq(value, *others):
    far = seq_swap(value, 2)
    near = seq_swap(value, 1)
    return [value, near, far, seq_swap(after(far, *others), 1)]


def reduce_seq(parts, *others):
    near2 = seq_swap(parts[3], 1)
    onward = (parts[2].astype(F32) + near2.astype(F32)).astype(BF16)
    near0 = seq_swap(after(parts[1], onward), 1)
    return [parts[0], near0, seq_swap(after(onward, *others), 2)], onward


def exchange_seq(parts):
    return [parts[0]] + [seq_swap(parts[r], r) for r in (1, 2, 3)]


def swap_y(value):
    with jax.named_scope("y"):
        return lax.ppermute(value, "y", [(0, 1), (1, 0)])


def swap_z(value, k, count):
    with jax.named_scope(f"z{k}"):
        return lax.ppermute(value, "z", [(i, i ^ k) for i in range(count)])


def turn_z(value):
    with jax.named_scope("z"):
        return lax.all_to_all(value, "z", split_axis=0, concat_axis=0, tiled=True)


def after(value, *others):
    return lax.optimization_barrier((value, *others))[0] if others else value


def fits(n):
    return n % 128 == 0


def row_copies(blocks, target, sems):
    rows = blocks[0].shape[0]
    return [
        pltpu.make_async_copy(x, target.at[pl.ds(i * rows, rows), :], sems.at[i])
        for i, x in enumerate(blocks)
        if x is not None
    ]


def hbm(value):
    return pltpu.with_memory_space_constraint(value, HBM)


def run_copies(copies):
    for copy in copies:
        copy.start()
    for copy in copies:
        copy.wait()


def early_pack_kernel(ids, wq, wk, wv, wo, *refs):
    *vectors, up_bias, out, sems = refs
    s = ids[0]
    n = wq.shape[0]
    c = wq.shape[1] // SEQ_N
    cols = pl.ds(pl.multiple_of(s * c, c), c)
    copies = [
        pltpu.make_async_copy(w.at[:, cols], out.at[pl.ds(0, n), pl.ds(i * c, c)], sems.at[i])
        for i, w in enumerate((wq, wk, wv, wo))
    ]
    for copy in copies:
        copy.start()
    rows = [v[...].astype(F32).reshape(1, n) for v in vectors]
    rows += [up_bias[j * n : (j + 1) * n].astype(F32).reshape(1, n) for j in range(SEQ_N)]
    rows.append(jnp.zeros((VEC - len(rows), n), F32))
    out[n:, 0:n] = jnp.concatenate(rows, 0).astype(BF16)
    out[n:, n:] = jnp.zeros((VEC, out.shape[1] - n), BF16)
    for copy in copies:
        copy.wait()


def late_pack_kernel(fs, ids, up, down, out, sems):
    s = ids[0]
    n = up.shape[0]
    w = up.shape[1] // fs // SEQ_N
    copies = []
    for j in range(fs):
        cols = pl.ds(pl.multiple_of((j * SEQ_N + s) * w, w), w)
        copies.append(
            pltpu.make_async_copy(
                up.at[:, cols], out.at[pl.ds(0, n), pl.ds(j * w, w)], sems.at[j]
            )
        )
    rows = pl.ds(pl.multiple_of(s * w, w), w)
    copies.append(pltpu.make_async_copy(down.at[rows, :], out.at[pl.ds(n, w), :], sems.at[fs]))
    run_copies(copies)


def pack_early(ids, s, wq, wk, wv, wo, vectors, up_bias):
    n, d = wq.shape
    c = d // SEQ_N
    if fits(n):
        return call(
            early_pack_kernel,
            struct((n + VEC, d), BF16),
            (ids, wq, wk, wv, wo, *vectors, up_bias),
            name="early_pack",
            in_specs=[whole(pltpu.SMEM)] + [whole(HBM)] * 4 + [whole()] * (len(vectors) + 1),
            scratch=[pltpu.SemaphoreType.DMA((4,))],
        )
    rows = jnp.concatenate(vectors + [up_bias]).reshape(-1, n)
    vec = jnp.pad(rows, ((0, VEC - rows.shape[0]), (0, d - n)))
    four = [lax.dynamic_slice(m, (0, s * c), (n, c)) for m in (wq, wk, wv, wo)]
    return jnp.concatenate([jnp.concatenate(four, 1), vec], 0)


def pack_late(ids, s, fs, up, down):
    n, d = up.shape[0], down.shape[1]
    w = up.shape[1] // fs // SEQ_N
    if fits(n):
        return call(
            functools.partial(late_pack_kernel, fs),
            struct((n + w, d), BF16),
            (ids, up, down),
            name="late_pack",
            in_specs=[whole(pltpu.SMEM)] + [whole(HBM)] * 2,
            scratch=[pltpu.SemaphoreType.DMA((fs + 1,))],
        )
    mine = lax.dynamic_index_in_dim(up.reshape(n, fs, SEQ_N, w), s, 2, keepdims=False)
    return jnp.concatenate([mine.reshape(n, fs * w), lax.dynamic_slice(down, (s * w, 0), (w, d))], 0)


def gather_early(value, fs):
    zs = fs // 2
    if zs != 4:
        own = turn_z(jnp.broadcast_to(value, (zs,) + value.shape))
        return [own, swap_y(own)]
    own = [value] + [swap_z(value, k, zs) for k in (3, 2, 1)][::-1]
    return own + [swap_y(own[k]) for k in range(zs)]


def load_blocks(pieces, f, first, rows, target, sems):
    zs = target.shape[0] // 2
    y = f & 1
    rows = pl.ds(first, rows)
    cols = pl.ds(0, target.shape[2])
    if len(pieces) == 2:
        return [
            pltpu.make_async_copy(piece.at[j, rows, cols], target.at[2 * j + at], sems.at[i * zs + j])
            for i, (piece, at) in enumerate(zip(pieces, (y, 1 - y)))
            for j in range(zs)
        ]
    return [
        pltpu.make_async_copy(
            piece.at[rows, cols], target.at[f ^ (2 * (i % zs) + i // zs)], sems.at[i]
        )
        for i, piece in enumerate(pieces)
    ]


def attend_kernel(count, ids, x0, x1, x2, x3, *refs):
    pieces = refs[:count]
    qkv, lse, m0, m1, m2, m3, w_out, vec, held, mix, w, small, sems, small_sems, x_sems = refs[count:]
    fs = w.shape[0]
    n = w.shape[1]
    c = w.shape[2] // 3
    d = fs * n
    heads = c // HD
    nb, block, _ = x0.shape
    f = ids[1]
    b = pl.program_id(0)
    out_copy = pltpu.make_async_copy(w, w_out, sems.at[fs])

    @pl.when(pl.program_id(0) == 0)
    def _():
        for i in range(nb):
            for copy in row_copies([x.at[i] for x in (x0, x1, x2, x3)], held.at[i], x_sems.at[i]):
                copy.start()
        copies = load_blocks(pieces, f, 0, n, w, sems)
        copies += load_blocks(pieces, f, n, VEC, small, small_sems)
        run_copies(copies)
        for j in range(fs):
            vec[:, j * n : (j + 1) * n] = small[j, :, 0:n].astype(F32)
        out_copy.start()

    for copy in row_copies([x.at[b] for x in (x0, x1, x2, x3)], held.at[b], x_sems.at[b]):
        copy.wait()
    cols = pl.ds(pl.multiple_of(ids[0] * c, c), c)
    for part in range(3):
        acc = dot(held[b], w[:, :, part * c : (part + 1) * c].reshape(d, c))
        if part != 1:
            row = ROW_QB if part == 0 else ROW_VB
            acc = acc + vec[row : row + 1, cols]
        qkv[0, :, part * c : (part + 1) * c] = acc.astype(BF16)
    scale = 1.0 / math.sqrt(HD)
    for h in range(heads):
        at = h * HD
        query = (qkv[0, :, at : at + HD].astype(F32) * scale).astype(BF16)
        key = qkv[0, :, c + at : c + at + HD]
        value = qkv[0, :, 2 * c + at : 2 * c + at + HD]
        scores = dot_nt(key, query)
        highest = jnp.max(scores, 0, keepdims=True)
        raised = jnp.exp(scores - highest)
        summed = jnp.sum(raised, 0, keepdims=True)
        lse[0, h : h + 1, :] = highest + jnp.log(summed)
        low = (raised * (1.0 / summed)).astype(BF16)
        mix[at : at + HD, :] = dot_tn(value, low)
    mixture = mix[...].T.astype(BF16)
    for r, m in enumerate((m0, m1, m2, m3)):
        m[0] = mixture[r * block : (r + 1) * block, :]

    @pl.when(pl.program_id(0) == pl.num_programs(0) - 1)
    def _():
        out_copy.wait()


def attend(ids, blocks, pieces, fs):
    nb, block, d = blocks[0].shape
    c = d // SEQ_N
    n = d // fs
    length = SEQ_N * block
    heads = c // HD
    one = lambda shape: pl.BlockSpec((1,) + shape, lambda b: (b,) + (0,) * len(shape))
    fixed = lambda shape: pl.BlockSpec(shape, lambda b: (0,) * len(shape))
    outs = (
        (struct((nb, length, 3 * c), BF16), struct((nb, heads, length), F32))
        + (struct((nb, block, c), BF16),) * SEQ_N
        + (struct((fs, n, 3 * c), BF16), struct((VEC, d), F32))
    )
    return call(
        functools.partial(attend_kernel, len(pieces)),
        outs,
        (ids, *blocks, *pieces),
        name="attend",
        grid=(nb,),
        in_specs=[whole(pltpu.SMEM)] + [whole(HBM)] * (SEQ_N + len(pieces)),
        out_specs=(one((length, 3 * c)), one((heads, length)))
        + (one((block, c)),) * SEQ_N
        + (whole(ANY), fixed((VEC, d))),
        scratch=[
            VMEM((nb, length, d), BF16),
            VMEM((c, length), F32),
            VMEM((fs, n, 3 * c), BF16),
            VMEM((fs, VEC, max(n, 128)), BF16),
            pltpu.SemaphoreType.DMA((fs + 1,)),
            pltpu.SemaphoreType.DMA((fs,)),
            pltpu.SemaphoreType.DMA((nb, SEQ_N)),
        ],
        flops=2 * nb * length * (3 * c * d + 2 * length * c),
        trans=nb * heads * length * length,
    )


def attend_back_kernel(qkv, lse, h0, h1, h2, h3, w, back, sums, r0, r1, r2, r3, held, turned):
    c = w.shape[1] // 3
    heads = c // HD
    block = h0.shape[1]
    for r, h in enumerate((h0, h1, h2, h3)):
        held[r * block : (r + 1) * block, :] = h[0]
    scale = 1.0 / math.sqrt(HD)
    for h in range(heads):
        at = h * HD
        query = (qkv[0, :, at : at + HD].astype(F32) * scale).astype(BF16)
        key = qkv[0, :, c + at : c + at + HD]
        value = qkv[0, :, 2 * c + at : 2 * c + at + HD]
        grad = held[:, at : at + HD]
        scores = dot_nt(key, query)
        attention = jnp.exp(scores - lse[0, h : h + 1, :])
        attention_grad = dot_nt(value, grad)
        inner = jnp.sum(attention * attention_grad, 0, keepdims=True)
        low = (attention * (attention_grad - inner)).astype(BF16)
        turned[at : at + HD, :] = dot_tn(key, low) * scale
        back[0, :, c + at : c + at + HD] = dot(low, query).astype(BF16)
        back[0, :, 2 * c + at : 2 * c + at + HD] = dot(attention.astype(BF16), grad).astype(BF16)
    back[0, :, 0:c] = turned[...].T.astype(BF16)
    whole_back = back[0]
    total = jnp.sum(whole_back.astype(F32), 0, keepdims=True)

    @pl.when(pl.program_id(0) == 0)
    def _():
        sums[...] = jnp.zeros_like(sums)

    sums[0:1, :] += total
    for r, out in enumerate((r0, r1, r2, r3)):
        out[0] = dot_nt(back[0, r * block : (r + 1) * block, :], w[...]).astype(BF16)


def attend_back(qkv, lse, grads, wqkv):
    nb, length, c3 = qkv.shape
    d = wqkv.shape[0]
    block = length // SEQ_N
    c = c3 // 3
    heads = c // HD
    one = lambda shape: pl.BlockSpec((1,) + shape, lambda b: (b,) + (0,) * len(shape))
    fixed = lambda shape: pl.BlockSpec(shape, lambda b: (0,) * len(shape))
    outs = (struct((nb, length, c3), BF16), struct((8, c3), F32)) + (
        struct((nb, block, d), BF16),
    ) * SEQ_N
    return call(
        attend_back_kernel,
        outs,
        (qkv, lse, *grads, wqkv),
        name="attend_back",
        grid=(nb,),
        in_specs=[one((length, c3)), one((heads, length))]
        + [one((block, c))] * SEQ_N
        + [fixed(wqkv.shape)],
        out_specs=(one((length, c3)), fixed((8, c3))) + (one((block, d)),) * SEQ_N,
        scratch=[VMEM((length, c), BF16), VMEM((c, length), F32)],
        flops=2 * nb * length * (c3 * d + 5 * length * c),
        trans=nb * heads * length * length,
    )


def row_norm(hidden):
    average = jnp.mean(hidden, -1, keepdims=True)
    centered = hidden - average
    spread = jnp.mean(centered * centered, -1, keepdims=True)
    scale = lax.rsqrt(spread + EPSILON)
    return centered * scale, scale


def norm_back(grad, normed, scale, gain):
    inner = grad * gain
    first = jnp.mean(inner, -1, keepdims=True)
    second = jnp.mean(inner * normed, -1, keepdims=True)
    return scale * (inner - first - normed * second)


def out_kernel(ids, m0, m1, m2, m3, w0, w1, w2, w3, tokens, vec,
               attn_sum, normed, low, mix, w, sems):
    s, f = ids[0], ids[1]
    c = m0.shape[1]
    fs, n, d = w.shape
    places = [pl.ds(pl.multiple_of((s ^ r) * c, c), c) for r in range(SEQ_N)]
    copies = []
    for r, (place, wr) in enumerate(zip(places, (w0, w1, w2, w3))):
        copies += load_blocks([wr.at[i] for i in range(wr.shape[0])], f, 0, n, w.at[:, :, place], sems.at[r])
    for copy in copies:
        copy.start()
    for place, m in zip(places, (m0, m1, m2, m3)):
        mix[:, place] = m[...]
    for copy in copies:
        copy.wait()
    for t in range(d // TILE):
        cols = slice(t * TILE, (t + 1) * TILE)
        product = dot(mix[...], w[:, :, cols].reshape(d, TILE))
        attn_sum[:, cols] = (
            tokens[:, cols].astype(F32) + product + vec[ROW_OB : ROW_OB + 1, cols]
        )
    unit, _ = row_norm(attn_sum[...])
    first = unit * vec[ROW_G1 : ROW_G1 + 1, :] + vec[ROW_S1 : ROW_S1 + 1, :]
    normed[...] = first
    low[...] = first.astype(BF16)


def out_project(ids, mixtures, wo, tokens, vec):
    rows, d = tokens.shape
    n = wo[0].shape[-2]
    fs = d // n
    outs = (
        struct((rows, d), F32),
        struct((rows, d), F32),
        struct((rows, d), BF16),
        struct((rows, d), BF16),
        struct((fs, n, d), BF16),
    )
    args = (ids, *mixtures, *wo, tokens, vec)
    return call(
        out_kernel,
        outs,
        args,
        name="out_project",
        in_specs=[whole(pltpu.SMEM)] + [whole()] * SEQ_N + [whole(HBM)] * SEQ_N + [whole()] * 2,
        scratch=[pltpu.SemaphoreType.DMA((SEQ_N, fs))],
        flops=2 * rows * d * d,
    )


def second_norm_kernel(normed, p0, p1, p2, cotangent, vec, layer_out, ffn_grad, low, sums):
    hidden = (
        normed[...]
        + (p0[...].astype(F32) + p1[...].astype(F32) + p2[...].astype(F32))
        + vec[ROW_DB : ROW_DB + 1, :]
    )
    unit, scale = row_norm(hidden)
    gain = vec[ROW_G2 : ROW_G2 + 1, :]
    layer_out[...] = (unit * gain + vec[ROW_S2 : ROW_S2 + 1, :]).astype(BF16)
    grad = cotangent[...].astype(F32)
    back = norm_back(grad, unit, scale, gain)
    ffn_grad[...] = back
    rounded = back.astype(BF16)
    low[...] = rounded
    sums[...] = jnp.zeros_like(sums)
    sums[0:1, :] = jnp.sum(grad * unit, 0, keepdims=True)
    sums[1:2, :] = jnp.sum(grad, 0, keepdims=True)
    sums[2:3, :] = jnp.sum(rounded.astype(F32), 0, keepdims=True)


def second_norm(normed, parts, cotangent, vec):
    rows, d = normed.shape
    outs = (
        struct((rows, d), BF16),
        struct((rows, d), F32),
        struct((rows, d), BF16),
        struct((8, d), F32),
    )
    return call(
        second_norm_kernel, outs, (normed, *parts, cotangent, vec), name="second_norm", flops=30 * rows * d
    )


def first_norm_kernel(ids, ffn_grad, p0, p1, p2, attn_sum, vec, w,
                      attn_grad, sums, n0, n1, n2, n3, low_out, low, back):
    s = ids[0]
    c = n0.shape[1]
    d = ffn_grad.shape[1]
    grad = ffn_grad[...] + (p0[...].astype(F32) + p1[...].astype(F32) + p2[...].astype(F32))
    unit, scale = row_norm(attn_sum[...])
    gain = vec[ROW_G1 : ROW_G1 + 1, :]
    value = norm_back(grad, unit, scale, gain)
    attn_grad[...] = value
    rounded = value.astype(BF16)
    low[...] = rounded
    low_out[...] = rounded
    sums[...] = jnp.zeros_like(sums)
    sums[0:1, :] = jnp.sum(grad * unit, 0, keepdims=True)
    sums[1:2, :] = jnp.sum(grad, 0, keepdims=True)
    sums[2:3, :] = jnp.sum(rounded.astype(F32), 0, keepdims=True)
    back[...] = dot_nt(low[...], w[...].reshape(d, d)).astype(BF16)
    for r, n in enumerate((n0, n1, n2, n3)):
        n[...] = back[:, pl.ds(pl.multiple_of((s ^ r) * c, c), c)]


def first_norm(ids, ffn_grad, parts, attn_sum, vec, wo):
    rows, d = ffn_grad.shape
    c = d // SEQ_N
    outs = (
        (struct((rows, d), F32), struct((8, d), F32))
        + (struct((rows, c), BF16),) * SEQ_N
        + (struct((rows, d), BF16),)
    )
    args = (ids, ffn_grad, *parts, attn_sum, vec, wo)
    return call(
        first_norm_kernel,
        outs,
        args,
        name="first_norm",
        in_specs=[whole(pltpu.SMEM)] + [whole()] * (len(args) - 1),
        scratch=[VMEM((rows, d), BF16), VMEM((rows, d), BF16)],
        flops=2 * rows * d * d,
    )


def out_grads_kernel(ids, mix, low, d0, d1, d2, d3):
    s = ids[0]
    c = d0.shape[1]
    for r, out in enumerate((d0, d1, d2, d3)):
        place = pl.ds(pl.multiple_of((s ^ r) * c, c), c)
        out[...] = dot_tn(mix[...], low[:, place]).astype(BF16)


def out_grads(ids, mix, low):
    rows, d = mix.shape
    c = d // SEQ_N
    return call(
        out_grads_kernel,
        (struct((d, c), BF16),) * SEQ_N,
        (ids, mix, low),
        name="out_grads",
        in_specs=[whole(pltpu.SMEM)] + [whole()] * 2,
        flops=2 * rows * d * d,
    )


TILE = 256


def gelu_and_slope(u):
    phi = 0.5 * lax.erf(u * (1.0 / math.sqrt(2.0))) + 0.5
    bell = u * (jnp.exp(-0.5 * u * u) * (1.0 / math.sqrt(2.0 * math.pi)))
    return u * phi, phi + bell


def ffn_kernel(ids, f0, f1, f2, f3, vec, packed, p0, p1, p2, p3, gelu, slope,
               held, made, up, down, sems, row_sems):
    rows, d = f0.shape
    held[2 * rows : 3 * rows, :] = f0[...]
    blocks = row_copies((f1, f3, None, f2), held, row_sems)
    n = up.shape[1]
    up_copies = [pltpu.make_async_copy(packed.at[:, pl.ds(0, n), :], up, sems.at[0])]
    down_copies = [pltpu.make_async_copy(packed.at[:, pl.ds(n, down.shape[1]), :], down, sems.at[1])]
    for copy in blocks + up_copies + down_copies:
        copy.start()
    hidden = gelu.shape[1]
    half = 2 * rows
    bias = vec[pl.ds(ROW_UB + ids[0], 1), :]
    for copy in blocks + up_copies + down_copies:
        copy.wait()

    def step(part, carry):
        at = pl.ds(pl.multiple_of(part * half, half), half)
        for t in range(hidden // TILE):
            cols = slice(t * TILE, (t + 1) * TILE)
            u = dot(held[at, :], up[:, :, cols].reshape(d, TILE)) + bias[:, cols]
            g, b = gelu_and_slope(u)
            gelu[at, cols] = g.astype(BF16)
            slope[at, cols] = b.astype(BF16)
        for t in range(d // TILE):
            cols = slice(t * TILE, (t + 1) * TILE)
            made[at, cols] = dot(gelu[at, :], down[:, :, cols].reshape(hidden, TILE)).astype(BF16)
        return carry

    lax.fori_loop(0, 2, step, 0)
    for i, out in enumerate((p1, p3, p0, p2)):
        out[...] = made[i * rows : (i + 1) * rows, :]


def weight_scratch(fs, d, hidden):
    return [
        VMEM((fs, d // fs, hidden), BF16),
        VMEM((fs, hidden // fs, d), BF16),
        pltpu.SemaphoreType.DMA((2,)),
        pltpu.SemaphoreType.DMA((SEQ_N,)),
    ]


def ffn(ids, blocks, packed, vec, hidden, fs):
    rows, d = blocks[0].shape
    total = SEQ_N * rows
    outs = (struct((rows, d), BF16),) * SEQ_N + (struct((total, hidden), BF16),) * 2
    return call(
        ffn_kernel,
        outs,
        (ids, blocks[0], *(hbm(b) for b in blocks[1:]), vec, hbm(packed)),
        name="ffn",
        in_specs=[whole(pltpu.SMEM), whole()] + [whole(HBM)] * 3 + [whole(), whole(HBM)],
        scratch=[VMEM((total, d), BF16)] * 2 + weight_scratch(fs, d, hidden),
        flops=4 * total * d * hidden,
        trans=2 * total * hidden,
    )


def ffn_back_kernel(ids, d0, d1, d2, d3, slope, packed, q0, q1, q2, q3, up_low, sums,
                    held, made, up, down, sems, row_sems):
    rows, d = d0.shape
    held[2 * rows : 3 * rows, :] = d0[...]
    blocks = row_copies((d1, d3, None, d2), held, row_sems)
    n = up.shape[1]
    up_copies = [pltpu.make_async_copy(packed.at[:, pl.ds(0, n), :], up, sems.at[0])]
    down_copies = [pltpu.make_async_copy(packed.at[:, pl.ds(n, down.shape[1]), :], down, sems.at[1])]
    for copy in blocks + down_copies + up_copies:
        copy.start()
    hidden = up_low.shape[1]
    half = 2 * rows
    per = TILE // up.shape[1]
    sums[...] = jnp.zeros_like(sums)
    for copy in blocks + down_copies + up_copies:
        copy.wait()

    def step(part, carry):
        at = pl.ds(pl.multiple_of(part * half, half), half)
        for t in range(hidden // TILE):
            cols = slice(t * TILE, (t + 1) * TILE)
            rhs = down[t * per : (t + 1) * per].reshape(TILE, d)
            u = (dot_nt(held[at, :], rhs) * slope[at, cols].astype(F32)).astype(BF16)
            up_low[at, cols] = u
            sums[0:1, cols] += jnp.sum(u.astype(F32), 0, keepdims=True)
        for t in range(d // TILE):
            cols = slice(t * TILE, (t + 1) * TILE)
            rhs = up[t * per : (t + 1) * per].reshape(TILE, hidden)
            made[at, cols] = dot_nt(up_low[at, :], rhs).astype(BF16)
        return carry

    lax.fori_loop(0, 2, step, 0)
    for i, out in enumerate((q1, q3, q0, q2)):
        out[...] = made[i * rows : (i + 1) * rows, :]


def ffn_back(ids, blocks, packed, slope, fs):
    rows, d = blocks[0].shape
    total, hidden = slope.shape
    outs = (struct((rows, d), BF16),) * SEQ_N + (
        struct((total, hidden), BF16),
        struct((8, hidden), F32),
    )
    return call(
        ffn_back_kernel,
        outs,
        (ids, *blocks, slope, packed),
        name="ffn_back",
        in_specs=[whole(pltpu.SMEM), whole()] + [whole(HBM)] * 3 + [whole(), whole(HBM)],
        scratch=[VMEM((total, d), BF16)] * 2 + weight_scratch(fs, d, hidden),
        flops=4 * total * d * hidden,
    )


def down_grads_kernel(gelu, d0, d1, d2, d3, out, right, made, sems, out_sems):
    rows, e = d0.shape
    copies = row_copies((d1, d3, None, d2), right, sems)
    for copy in copies:
        copy.start()
    right[2 * rows : 3 * rows, :] = d0[...]
    for copy in copies:
        copy.wait()
    results = []
    for t in range(gelu.shape[1] // TILE):
        at = slice(t * TILE, (t + 1) * TILE)
        made[at, :] = dot_tn(gelu[:, at], right[...]).astype(BF16)
        at = pl.ds(t * TILE, TILE)
        copy = pltpu.make_async_copy(made.at[at, :], out.at[at, :], out_sems.at[t])
        copy.start()
        results.append(copy)
    for copy in results:
        copy.wait()


def down_grads(gelu, lows):
    rows, d = lows[0].shape
    total, hidden = gelu.shape
    return call(
        down_grads_kernel,
        struct((hidden, d), BF16),
        (gelu, *lows),
        name="down_grads",
        light=32,
        in_specs=[whole()] * 2 + [whole(HBM)] * 3,
        out_specs=whole(HBM),
        scratch=[
            VMEM((total, d), BF16),
            VMEM((hidden, d), BF16),
            pltpu.SemaphoreType.DMA((SEQ_N,)),
            pltpu.SemaphoreType.DMA((hidden // TILE,)),
        ],
        flops=2 * total * d * hidden,
    )


def up_grads_kernel(ids, f0, f1, f2, f3, up_low, keep, send, left, turn, sems):
    copies = row_copies((f1, f3, f0, f2), left, sems)
    for copy in copies:
        copy.start()
    n = keep.shape[1]
    per = TILE // (2 * n)
    y = ids[1] & 1
    for copy in copies:
        copy.wait()
    for t in range(left.shape[1] // TILE):
        turn[...] = dot_tn(left[:, t * TILE : (t + 1) * TILE], up_low[...]).astype(BF16)
        for j in range(per):
            for out, side in ((keep, y), (send, 1 - y)):
                out[t * per + j] = turn[pl.ds(pl.multiple_of((2 * j + side) * n, n), n), :]


def up_grads(ids, firsts, up_low, fs):
    rows, d = firsts[0].shape
    total, hidden = up_low.shape
    return call(
        up_grads_kernel,
        (struct((fs // 2, d // fs, hidden), BF16),) * 2,
        (ids, *(hbm(f) for f in firsts), up_low),
        name="up_grads",
        light=32,
        in_specs=[whole(pltpu.SMEM)] + [whole(HBM)] * SEQ_N + [whole()],
        scratch=[VMEM((total, d), BF16), VMEM((TILE, hidden), BF16), pltpu.SemaphoreType.DMA((SEQ_N,))],
        flops=2 * total * d * hidden,
    )


def add(a, b):
    return (a.astype(F32) + b.astype(F32)).astype(BF16)


def sum_z(terms):
    return jnp.sum(turn_z(terms).astype(F32), 0).astype(BF16)


def scatter_fsdp(keep, came, *others):
    if isinstance(keep, (list, tuple)):
        total = None
        for k in (1, 2, 3, 0):
            here = keep[k].astype(F32) + came[k].astype(F32)
            if k:
                here = swap_z(here.astype(BF16), k, len(keep)).astype(F32)
            total = here if total is None else total + here
        return total.astype(BF16)
    return sum_z(after(add(keep, came), *others))


def fill_vectors(s, vec, back_sums, first_sums, second_sums, up_sums):
    c = vec.shape[1] // SEQ_N
    vec[...] = jnp.zeros_like(vec)
    cols = pl.ds(pl.multiple_of(s * c, c), c)
    vec[ROW_QB : ROW_QB + 1, cols] = back_sums[0:1, 0:c]
    vec[ROW_VB : ROW_VB + 1, cols] = back_sums[0:1, 2 * c : 3 * c]
    vec[ROW_OB : ROW_OB + 1, :] = first_sums[2:3, :]
    vec[ROW_DB : ROW_DB + 1, :] = second_sums[2:3, :]
    vec[ROW_G1 : ROW_G1 + 1, :] = first_sums[0:1, :]
    vec[ROW_S1 : ROW_S1 + 1, :] = first_sums[1:2, :]
    vec[ROW_G2 : ROW_G2 + 1, :] = second_sums[0:1, :]
    vec[ROW_S2 : ROW_S2 + 1, :] = second_sums[1:2, :]
    vec[pl.ds(ROW_UB + s, 1), :] = up_sums[0:1, :]


def qkvo_grads_kernel(ids, x0, x1, x2, x3, back, o0, o1, o2, s0, s1, s2, s3, *refs):
    outs, (held, vec, turn, sems) = refs[:-4], refs[-4:]
    s, f = ids[0], ids[1]
    nb, block, d = x0.shape
    e = back.shape[1]
    n = outs[0].shape[-2] - VEC
    zs = d // (2 * n)
    per = TILE // (2 * n)
    y = f & 1
    copies = row_copies([x.at[b] for b in range(nb) for x in (x0, x1, x2, x3)], held, sems)
    for copy in copies:
        copy.start()
    fill_vectors(s, vec, s0, s1, s2, s3)
    for copy in copies:
        copy.wait()
    if len(outs) > 2:
        for k in (1, 2, 3, 0):
            z = (f >> 1) ^ k
            rows = pl.ds(pl.multiple_of(z * TILE, TILE), TILE)
            turn[:, 0:e] = dot_tn(held[:, rows], back[...]).astype(BF16)
            turn[:, e:] = (
                o0[rows, :].astype(F32) + o1[rows, :].astype(F32) + o2[rows, :].astype(F32)
            ).astype(BF16)
            for out, side in ((outs[k], y), (outs[zs + k], 1 - y)):
                out[0:n, :] = turn[pl.ds(pl.multiple_of(side * n, n), n), :]
                out[n:, :] = jnp.zeros((VEC, out.shape[1]), BF16)
                cols = pl.ds(pl.multiple_of((2 * z + side) * n, n), n)
                out[n:, 0:n] = vec[:, cols].astype(BF16)
        return
    keep, send = outs
    for t in range(d // TILE):
        rows = slice(t * TILE, (t + 1) * TILE)
        turn[:, 0:e] = dot_tn(held[:, rows], back[...]).astype(BF16)
        turn[:, e:] = (
            o0[rows, :].astype(F32) + o1[rows, :].astype(F32) + o2[rows, :].astype(F32)
        ).astype(BF16)
        for j in range(per):
            z = t * per + j
            for out, side in ((keep, y), (send, 1 - y)):
                out[z, 0:n, :] = turn[pl.ds(pl.multiple_of((2 * j + side) * n, n), n), :]
    low = vec[...].astype(BF16)
    for z in range(zs):
        first, second = (low[:, (2 * z + i) * n : (2 * z + i + 1) * n] for i in range(2))
        for out, pick in ((keep, y == 0), (send, y != 0)):
            out[z, n:, :] = jnp.zeros((VEC, out.shape[2]), BF16)
            out[z, n:, 0:n] = jnp.where(pick, first, second)


def qkvo_grads(ids, blocks, back, out_parts, sums, fs):
    nb, block, d = blocks[0].shape
    total, e = back.shape
    n = d // fs
    wide = e + out_parts[0].shape[1]
    if fs == 8 and fits(n):
        outs = (struct((n + VEC, wide), BF16),) * 8
    else:
        outs = (struct((fs // 2, n + VEC, wide), BF16),) * 2
    return call(
        qkvo_grads_kernel,
        outs,
        (ids, *(hbm(b) for b in blocks), back, *out_parts, *sums),
        name="qkvo_grads",
        in_specs=[whole(pltpu.SMEM)] + [whole(HBM)] * SEQ_N + [whole()] * 8,
        scratch=[
            VMEM((total, d), BF16),
            VMEM((VEC, d), F32),
            VMEM((TILE, wide), BF16),
            pltpu.SemaphoreType.DMA((nb * SEQ_N,)),
        ],
        flops=2 * total * d * e,
    )


def finish_ffn_kernel(fs, ids, *refs):
    ups, downs, (up, down) = refs[:4], refs[4:8], refs[8:]
    s = ids[0]
    w = up.shape[1] // fs // SEQ_N
    for r in range(SEQ_N):
        at = s ^ r
        for j in range(fs):
            place = pl.ds(pl.multiple_of((j * SEQ_N + at) * w, w), w)
            up[:, place] = ups[r][:, j * w : (j + 1) * w].astype(F32)
        down[pl.ds(pl.multiple_of(at * w, w), w), :] = downs[r][...].astype(F32)


def finish_qkvo_kernel(ids, c0, c1, c2, c3, wq, wk, wv, wo, *vectors):
    s = ids[0]
    n = wq.shape[0]
    c = wq.shape[1] // SEQ_N
    total = 0.0
    for r, small in enumerate((c0, c1, c2, c3)):
        cols = pl.ds(pl.multiple_of((s ^ r) * c, c), c)
        for i, out in enumerate((wq, wk, wv, wo)):
            out[:, cols] = small[0:n, i * c : (i + 1) * c].astype(F32)
        total = total + small[n:, 0:n].astype(F32)
    for row, out in enumerate(vectors[:ROW_UB]):
        out[...] = total[row : row + 1, :].reshape(n)
    for j in range(SEQ_N):
        vectors[ROW_UB][j * n : (j + 1) * n] = total[ROW_UB + j : ROW_UB + j + 1, :].reshape(n)


def finish_ffn(ids, s, ups, downs, fs):
    n = ups[0].shape[0]
    w, d = downs[0].shape
    hidden = SEQ_N * fs * w
    if fits(n):
        return call(
            functools.partial(finish_ffn_kernel, fs),
            (struct((n, hidden), F32), struct((SEQ_N * w, d), F32)),
            (ids, *ups, *downs),
            name="finish_ffn",
            in_specs=[whole(pltpu.SMEM)] + [whole()] * 8,
        )
    order = jnp.arange(SEQ_N) ^ s
    up, down = (jnp.stack(v)[order].astype(F32) for v in (ups, downs))
    return (
        up.reshape(SEQ_N, n, fs, w).transpose(1, 2, 0, 3).reshape(n, hidden),
        down.reshape(SEQ_N * w, d),
    )


def finish_qkvo(ids, s, small):
    n = small[0].shape[0] - VEC
    d = small[0].shape[1]
    c = d // SEQ_N
    if fits(n):
        outs = (struct((n, d), F32),) * 4 + (struct((n,), F32),) * ROW_UB + (struct((SEQ_N * n,), F32),)
        done = call(
            finish_qkvo_kernel,
            outs,
            (ids, *small),
            name="finish_qkvo",
            in_specs=[whole(pltpu.SMEM)] + [whole()] * 4,
        )
        return done[:4], done[4:]
    small = jnp.stack(small)[jnp.arange(SEQ_N) ^ s].astype(F32)
    four = small[:, :n].reshape(SEQ_N, n, 4, c).transpose(2, 1, 0, 3).reshape(4, n, d)
    total = jnp.sum(small[:, n:, :n], 0)
    vectors = [total[row] for row in range(ROW_UB)]
    vectors.append(total[ROW_UB : ROW_UB + SEQ_N].reshape(SEQ_N * n))
    return [four[i] for i in range(4)], vectors


def body(fs, tokens_in, cotangent, query_weight, key_weight, value_weight, out_weight, up_weight,
         down_weight, query_bias, value_bias, out_bias, up_bias, down_bias, first_gain, first_shift,
         second_gain, second_shift):
    nb, block, d = tokens_in.shape
    rows = nb * block
    s = lax.axis_index(SEQ)
    f = lax.axis_index(FSDP)
    ids = jnp.stack([s, f]).astype(jnp.int32)
    flat = lambda a: a.reshape(rows, a.shape[-1])
    deep = lambda a: a.reshape(nb, block, a.shape[-1])

    scope = jax.named_scope
    early = pack_early(
        ids, s, query_weight, key_weight, value_weight, out_weight,
        [query_bias, value_bias, out_bias, down_bias, first_gain, first_shift, second_gain, second_shift],
        up_bias,
    )
    packed = pack_late(ids, s, fs, up_weight, down_weight)
    hidden = up_weight.shape[1] // SEQ_N
    with scope("tok"):
        tokens = gather_seq(tokens_in)
    with scope("wqkv"):
        wqkv = gather_early(early, fs)
    with scope("ffnw"):
        packed = lax.all_gather(after(packed, wqkv[0], *wqkv[3:5]), FSDP)
    with scope("wo"):
        n = d // fs
        wo = jnp.stack([p[..., :n, 3 * (d // SEQ_N) :] for p in wqkv])
        wo = [wo, seq_swap(wo, 1), seq_swap(wo, 2)]
    qkv, lse, *mixtures, wqkv, vec = attend(ids, tokens, wqkv, fs)
    with scope("wo"):
        wo.append(seq_swap(after(wo[2], vec), 1))
    with scope("mix"):
        mixtures = exchange_seq([flat(m) for m in mixtures])
    attn_sum, normed, first_low, mix, wo = out_project(ids, mixtures, wo, flat(tokens_in), vec)
    with scope("first"):
        firsts = gather_seq(first_low)
    *parts, gelu, slope = ffn(ids, firsts, packed, vec, hidden, fs)
    with scope("ffn"):
        parts, _ = reduce_seq(parts)
    layer_out, ffn_grad, down_low, second_sums = second_norm(normed, parts, flat(cotangent), vec)
    with scope("low"):
        lows = gather_seq(down_low)
    down_full = down_grads(gelu, lows)
    with scope("gdown"):
        down_grad = lax.psum_scatter(down_full, FSDP, scatter_dimension=0, tiled=True)
    slope = after(slope, down_full)
    *parts, up_low, up_sums = ffn_back(ids, lows, packed, slope, fs)
    with scope("ffnback"):
        parts, onward = reduce_seq(parts)
    attn_grad, first_sums, *pieces, out_low = first_norm(ids, ffn_grad, parts, attn_sum, vec, wo)
    with scope("mixback"):
        grads = exchange_seq(pieces)
    keep_up, send_up = up_grads(ids, firsts, after(up_low, grads[1]), fs)
    with scope("gup"):
        came_up = swap_y(send_up)
    out_parts = out_grads(ids, mix, out_low)
    with scope("outs"):
        out_parts, onward = reduce_seq(out_parts, *grads[2:])
    grads[0] = after(grads[0], onward, keep_up)
    back, back_sums, *parts = attend_back(qkv, lse, [deep(g) for g in grads], wqkv.reshape(d, -1))
    with scope("gup"):
        up_terms = add(keep_up, after(came_up, back))
        up_grad = sum_z(up_terms)
    back = after(back, up_terms)
    pieces = qkvo_grads(
        ids, tokens, back.reshape(-1, back.shape[-1]), out_parts,
        (back_sums, first_sums, second_sums, up_sums), fs,
    )
    with scope("gqkvo"):
        half = len(pieces) // 2
        keep, send = pieces[:half], pieces[half:]
        if half == 1:
            small = scatter_fsdp(keep[0], swap_y(send[0]))
        else:
            came = {k: swap_y(send[k]) for k in (1, 2, 3, 0)}
            small = scatter_fsdp(keep, came)
    with scope("input"):
        terms, _ = reduce_seq([flat(p) for p in parts])
    input_grad = attn_grad + (
        terms[0].astype(F32) + terms[1].astype(F32) + terms[2].astype(F32)
    )
    with scope("fdown"):
        downs = gather_seq(after(down_grad, terms[2]))
    with scope("fup"):
        ups = gather_seq(after(up_grad, downs[2]))
    up, down = finish_ffn(ids, s, ups, downs, fs)
    with scope("small"):
        small = gather_seq(small, up)
    four, vecs = finish_qkvo(ids, s, small)
    return (
        deep(layer_out), deep(input_grad), *four, up, down,
        vecs[ROW_QB], vecs[ROW_VB], vecs[ROW_OB], vecs[ROW_UB], vecs[ROW_DB],
        vecs[ROW_G1], vecs[ROW_S1], vecs[ROW_G2], vecs[ROW_S2],
    )


def solution(mesh):
    count, fs = mesh.shape["seq"], mesh.shape["fsdp"]
    assert count == SEQ_N and fs % 4 == 0
    inner = Mesh(mesh.devices.reshape(2, 2, fs // 2, 2), SEQ + FSDP)
    rows, matrix, vector = P(FSDP, SEQ, None), P(FSDP, None), P(FSDP)
    in_specs = (rows,) * 2 + (matrix,) * 6 + (vector,) * 9
    return jax.shard_map(
        functools.partial(body, fs), mesh=inner, in_specs=in_specs, out_specs=in_specs, check_vma=False
    )
```

```python
import functools
import math

import jax
import jax.numpy as jnp
from jax import lax
from jax.experimental import pallas as pl
from jax.experimental.pallas import tpu as pltpu
from jax.sharding import Mesh, PartitionSpec as P

HD = 64
EPSILON = 1e-05
F32 = jnp.float32
BF16 = jnp.bfloat16
SEQ = ("x", "c")
FSDP = ("z", "y")
SEQ_N = 4
VEC = 16
ROW_QB, ROW_VB, ROW_OB, ROW_DB, ROW_G1, ROW_S1, ROW_G2, ROW_S2, ROW_UB = range(9)
VMEM = pltpu.VMEM
ANY = pl.ANY
HBM = pltpu.HBM
LIMITS = {"early_pack": 56, "late_pack": 56}


def dot(a, b):
    return lax.dot_general(a, b, (((1,), (0,)), ((), ())), preferred_element_type=F32)


def dot_nt(a, b):
    return lax.dot_general(a, b, (((1,), (1,)), ((), ())), preferred_element_type=F32)


def dot_tn(a, b):
    return lax.dot_general(a, b, (((0,), (0,)), ((), ())), preferred_element_type=F32)


def struct(shape, dtype):
    return jax.ShapeDtypeStruct(shape, dtype)


def nbytes(tree):
    return sum(math.prod(a.shape) * a.dtype.itemsize for a in jax.tree.leaves(tree))


def whole(space=VMEM):
    return pl.BlockSpec(memory_space=space)


def call(kernel, outs, args, *, name, grid=None, in_specs=None, out_specs=None, scratch=(), flops=0, trans=0, light=1):
    if in_specs is None:
        in_specs = [whole() for _ in args]
    if out_specs is None:
        out_specs = jax.tree.map(lambda _: whole(), outs)
    kwargs = {} if grid is None else {"grid": grid}
    return pl.pallas_call(
        kernel,
        out_shape=outs,
        in_specs=in_specs,
        out_specs=out_specs,
        scratch_shapes=list(scratch),
        compiler_params=pltpu.CompilerParams(vmem_limit_bytes=LIMITS.get(name, 20) << 20),
        cost_estimate=pl.CostEstimate(
            flops=flops // light,
            bytes_accessed=(nbytes(args) + nbytes(outs)) // light,
            transcendentals=trans,
        ),
        name=name,
        **kwargs,
    )(*args)


def seq_swap(value, k):
    with jax.named_scope(f"seq{k}"):
        return lax.ppermute(value, SEQ, [(i, i ^ k) for i in range(SEQ_N)])


def gather_seq(value, *others):
    far = seq_swap(value, 2)
    near = seq_swap(value, 1)
    return [value, near, far, seq_swap(after(far, *others), 1)]


def reduce_seq(parts, *others):
    near2 = seq_swap(parts[3], 1)
    onward = (parts[2].astype(F32) + near2.astype(F32)).astype(BF16)
    near0 = seq_swap(after(parts[1], onward), 1)
    return [parts[0], near0, seq_swap(after(onward, *others), 2)], onward


def exchange_seq(parts):
    return [parts[0]] + [seq_swap(parts[r], r) for r in (1, 2, 3)]


def swap_y(value):
    with jax.named_scope("y"):
        return lax.ppermute(value, "y", [(0, 1), (1, 0)])


def swap_z(value, k, count):
    with jax.named_scope(f"z{k}"):
        return lax.ppermute(value, "z", [(i, i ^ k) for i in range(count)])


def turn_z(value):
    with jax.named_scope("z"):
        return lax.all_to_all(value, "z", split_axis=0, concat_axis=0, tiled=True)


def after(value, *others):
    return lax.optimization_barrier((value, *others))[0] if others else value


def fits(n):
    return n % 128 == 0


def row_copies(blocks, target, sems):
    rows = blocks[0].shape[0]
    return [
        pltpu.make_async_copy(x, target.at[pl.ds(i * rows, rows), :], sems.at[i])
        for i, x in enumerate(blocks)
        if x is not None
    ]


def hbm(value):
    return pltpu.with_memory_space_constraint(value, HBM)


def run_copies(copies):
    for copy in copies:
        copy.start()
    for copy in copies:
        copy.wait()


def early_pack_kernel(ids, wq, wk, wv, wo, *refs):
    *vectors, up_bias, out, sems = refs
    s = ids[0]
    n = wq.shape[0]
    c = wq.shape[1] // SEQ_N
    cols = pl.ds(pl.multiple_of(s * c, c), c)
    copies = [
        pltpu.make_async_copy(w.at[:, cols], out.at[pl.ds(0, n), pl.ds(i * c, c)], sems.at[i])
        for i, w in enumerate((wq, wk, wv, wo))
    ]
    for copy in copies:
        copy.start()
    rows = [v[...].astype(F32).reshape(1, n) for v in vectors]
    rows += [up_bias[j * n : (j + 1) * n].astype(F32).reshape(1, n) for j in range(SEQ_N)]
    rows.append(jnp.zeros((VEC - len(rows), n), F32))
    out[n:, 0:n] = jnp.concatenate(rows, 0).astype(BF16)
    out[n:, n:] = jnp.zeros((VEC, out.shape[1] - n), BF16)
    for copy in copies:
        copy.wait()


def late_pack_kernel(fs, ids, up, down, out, sems):
    s = ids[0]
    n = up.shape[0]
    w = up.shape[1] // fs // SEQ_N
    copies = []
    for j in range(fs):
        cols = pl.ds(pl.multiple_of((j * SEQ_N + s) * w, w), w)
        copies.append(
            pltpu.make_async_copy(
                up.at[:, cols], out.at[pl.ds(0, n), pl.ds(j * w, w)], sems.at[j]
            )
        )
    rows = pl.ds(pl.multiple_of(s * w, w), w)
    copies.append(pltpu.make_async_copy(down.at[rows, :], out.at[pl.ds(n, w), :], sems.at[fs]))
    run_copies(copies)


def pack_early(ids, s, wq, wk, wv, wo, vectors, up_bias):
    n, d = wq.shape
    c = d // SEQ_N
    if fits(n):
        return call(
            early_pack_kernel,
            struct((n + VEC, d), BF16),
            (ids, wq, wk, wv, wo, *vectors, up_bias),
            name="early_pack",
            in_specs=[whole(pltpu.SMEM)] + [whole(HBM)] * 4 + [whole()] * (len(vectors) + 1),
            scratch=[pltpu.SemaphoreType.DMA((4,))],
        )
    rows = jnp.concatenate(vectors + [up_bias]).reshape(-1, n)
    vec = jnp.pad(rows, ((0, VEC - rows.shape[0]), (0, d - n)))
    four = [lax.dynamic_slice(m, (0, s * c), (n, c)) for m in (wq, wk, wv, wo)]
    return jnp.concatenate([jnp.concatenate(four, 1), vec], 0)


def pack_late(ids, s, fs, up, down):
    n, d = up.shape[0], down.shape[1]
    w = up.shape[1] // fs // SEQ_N
    if fits(n):
        return call(
            functools.partial(late_pack_kernel, fs),
            struct((n + w, d), BF16),
            (ids, up, down),
            name="late_pack",
            in_specs=[whole(pltpu.SMEM)] + [whole(HBM)] * 2,
            scratch=[pltpu.SemaphoreType.DMA((fs + 1,))],
        )
    mine = lax.dynamic_index_in_dim(up.reshape(n, fs, SEQ_N, w), s, 2, keepdims=False)
    return jnp.concatenate([mine.reshape(n, fs * w), lax.dynamic_slice(down, (s * w, 0), (w, d))], 0)


def gather_early(value, fs):
    zs = fs // 2
    if zs != 4:
        own = turn_z(jnp.broadcast_to(value, (zs,) + value.shape))
        return [own, swap_y(own)]
    own = [value] + [swap_z(value, k, zs) for k in (3, 2, 1)][::-1]
    return own + [swap_y(own[k]) for k in range(zs)]


def load_blocks(pieces, f, first, rows, target, sems):
    zs = target.shape[0] // 2
    y = f & 1
    rows = pl.ds(first, rows)
    cols = pl.ds(0, target.shape[2])
    if len(pieces) == 2:
        return [
            pltpu.make_async_copy(piece.at[j, rows, cols], target.at[2 * j + at], sems.at[i * zs + j])
            for i, (piece, at) in enumerate(zip(pieces, (y, 1 - y)))
            for j in range(zs)
        ]
    return [
        pltpu.make_async_copy(
            piece.at[rows, cols], target.at[f ^ (2 * (i % zs) + i // zs)], sems.at[i]
        )
        for i, piece in enumerate(pieces)
    ]


def attend_kernel(count, ids, x0, x1, x2, x3, *refs):
    pieces = refs[:count]
    qkv, lse, m0, m1, m2, m3, w_out, vec, held, mix, w, small, sems, small_sems, x_sems = refs[count:]
    fs = w.shape[0]
    n = w.shape[1]
    c = w.shape[2] // 3
    d = fs * n
    heads = c // HD
    nb, block, _ = x0.shape
    f = ids[1]
    b = pl.program_id(0)
    out_copy = pltpu.make_async_copy(w, w_out, sems.at[fs])

    @pl.when(pl.program_id(0) == 0)
    def _():
        for i in range(nb):
            for copy in row_copies([x.at[i] for x in (x0, x1, x2, x3)], held.at[i], x_sems.at[i]):
                copy.start()
        copies = load_blocks(pieces, f, 0, n, w, sems)
        copies += load_blocks(pieces, f, n, VEC, small, small_sems)
        run_copies(copies)
        for j in range(fs):
            vec[:, j * n : (j + 1) * n] = small[j, :, 0:n].astype(F32)
        out_copy.start()

    for copy in row_copies([x.at[b] for x in (x0, x1, x2, x3)], held.at[b], x_sems.at[b]):
        copy.wait()
    cols = pl.ds(pl.multiple_of(ids[0] * c, c), c)
    for part in range(3):
        acc = dot(held[b], w[:, :, part * c : (part + 1) * c].reshape(d, c))
        if part != 1:
            row = ROW_QB if part == 0 else ROW_VB
            acc = acc + vec[row : row + 1, cols]
        qkv[0, :, part * c : (part + 1) * c] = acc.astype(BF16)
    scale = 1.0 / math.sqrt(HD)
    for h in range(heads):
        at = h * HD
        query = (qkv[0, :, at : at + HD].astype(F32) * scale).astype(BF16)
        key = qkv[0, :, c + at : c + at + HD]
        value = qkv[0, :, 2 * c + at : 2 * c + at + HD]
        scores = dot_nt(key, query)
        highest = jnp.max(scores, 0, keepdims=True)
        raised = jnp.exp(scores - highest)
        summed = jnp.sum(raised, 0, keepdims=True)
        lse[0, h : h + 1, :] = highest + jnp.log(summed)
        low = (raised * (1.0 / summed)).astype(BF16)
        mix[at : at + HD, :] = dot_tn(value, low)
    mixture = mix[...].T.astype(BF16)
    for r, m in enumerate((m0, m1, m2, m3)):
        m[0] = mixture[r * block : (r + 1) * block, :]

    @pl.when(pl.program_id(0) == pl.num_programs(0) - 1)
    def _():
        out_copy.wait()


def attend(ids, blocks, pieces, fs):
    nb, block, d = blocks[0].shape
    c = d // SEQ_N
    n = d // fs
    length = SEQ_N * block
    heads = c // HD
    one = lambda shape: pl.BlockSpec((1,) + shape, lambda b: (b,) + (0,) * len(shape))
    fixed = lambda shape: pl.BlockSpec(shape, lambda b: (0,) * len(shape))
    outs = (
        (struct((nb, length, 3 * c), BF16), struct((nb, heads, length), F32))
        + (struct((nb, block, c), BF16),) * SEQ_N
        + (struct((fs, n, 3 * c), BF16), struct((VEC, d), F32))
    )
    return call(
        functools.partial(attend_kernel, len(pieces)),
        outs,
        (ids, *blocks, *pieces),
        name="attend",
        grid=(nb,),
        in_specs=[whole(pltpu.SMEM)] + [whole(HBM)] * (SEQ_N + len(pieces)),
        out_specs=(one((length, 3 * c)), one((heads, length)))
        + (one((block, c)),) * SEQ_N
        + (whole(ANY), fixed((VEC, d))),
        scratch=[
            VMEM((nb, length, d), BF16),
            VMEM((c, length), F32),
            VMEM((fs, n, 3 * c), BF16),
            VMEM((fs, VEC, max(n, 128)), BF16),
            pltpu.SemaphoreType.DMA((fs + 1,)),
            pltpu.SemaphoreType.DMA((fs,)),
            pltpu.SemaphoreType.DMA((nb, SEQ_N)),
        ],
        flops=2 * nb * length * (3 * c * d + 2 * length * c),
        trans=nb * heads * length * length,
    )


def attend_back_kernel(qkv, lse, h0, h1, h2, h3, w, back, sums, r0, r1, r2, r3, held, turned):
    c = w.shape[1] // 3
    heads = c // HD
    block = h0.shape[1]
    for r, h in enumerate((h0, h1, h2, h3)):
        held[r * block : (r + 1) * block, :] = h[0]
    scale = 1.0 / math.sqrt(HD)
    for h in range(heads):
        at = h * HD
        query = (qkv[0, :, at : at + HD].astype(F32) * scale).astype(BF16)
        key = qkv[0, :, c + at : c + at + HD]
        value = qkv[0, :, 2 * c + at : 2 * c + at + HD]
        grad = held[:, at : at + HD]
        scores = dot_nt(key, query)
        attention = jnp.exp(scores - lse[0, h : h + 1, :])
        attention_grad = dot_nt(value, grad)
        inner = jnp.sum(attention * attention_grad, 0, keepdims=True)
        low = (attention * (attention_grad - inner)).astype(BF16)
        turned[at : at + HD, :] = dot_tn(key, low) * scale
        back[0, :, c + at : c + at + HD] = dot(low, query).astype(BF16)
        back[0, :, 2 * c + at : 2 * c + at + HD] = dot(attention.astype(BF16), grad).astype(BF16)
    back[0, :, 0:c] = turned[...].T.astype(BF16)
    whole_back = back[0]
    total = jnp.sum(whole_back.astype(F32), 0, keepdims=True)

    @pl.when(pl.program_id(0) == 0)
    def _():
        sums[...] = jnp.zeros_like(sums)

    sums[0:1, :] += total
    for r, out in enumerate((r0, r1, r2, r3)):
        out[0] = dot_nt(back[0, r * block : (r + 1) * block, :], w[...]).astype(BF16)


def attend_back(qkv, lse, grads, wqkv):
    nb, length, c3 = qkv.shape
    d = wqkv.shape[0]
    block = length // SEQ_N
    c = c3 // 3
    heads = c // HD
    one = lambda shape: pl.BlockSpec((1,) + shape, lambda b: (b,) + (0,) * len(shape))
    fixed = lambda shape: pl.BlockSpec(shape, lambda b: (0,) * len(shape))
    outs = (struct((nb, length, c3), BF16), struct((8, c3), F32)) + (
        struct((nb, block, d), BF16),
    ) * SEQ_N
    return call(
        attend_back_kernel,
        outs,
        (qkv, lse, *grads, wqkv),
        name="attend_back",
        grid=(nb,),
        in_specs=[one((length, c3)), one((heads, length))]
        + [one((block, c))] * SEQ_N
        + [fixed(wqkv.shape)],
        out_specs=(one((length, c3)), fixed((8, c3))) + (one((block, d)),) * SEQ_N,
        scratch=[VMEM((length, c), BF16), VMEM((c, length), F32)],
        flops=2 * nb * length * (c3 * d + 5 * length * c),
        trans=nb * heads * length * length,
    )


def row_norm(hidden):
    average = jnp.mean(hidden, -1, keepdims=True)
    centered = hidden - average
    spread = jnp.mean(centered * centered, -1, keepdims=True)
    scale = lax.rsqrt(spread + EPSILON)
    return centered * scale, scale


def norm_back(grad, normed, scale, gain):
    inner = grad * gain
    first = jnp.mean(inner, -1, keepdims=True)
    second = jnp.mean(inner * normed, -1, keepdims=True)
    return scale * (inner - first - normed * second)


def out_kernel(ids, m0, m1, m2, m3, w0, w1, w2, w3, tokens, vec,
               attn_sum, normed, low, mix, w, sems):
    s, f = ids[0], ids[1]
    c = m0.shape[1]
    fs, n, d = w.shape
    places = [pl.ds(pl.multiple_of((s ^ r) * c, c), c) for r in range(SEQ_N)]
    copies = []
    for r, (place, wr) in enumerate(zip(places, (w0, w1, w2, w3))):
        copies += load_blocks([wr.at[i] for i in range(wr.shape[0])], f, 0, n, w.at[:, :, place], sems.at[r])
    for copy in copies:
        copy.start()
    for place, m in zip(places, (m0, m1, m2, m3)):
        mix[:, place] = m[...]
    for copy in copies:
        copy.wait()
    for t in range(d // TILE):
        cols = slice(t * TILE, (t + 1) * TILE)
        product = dot(mix[...], w[:, :, cols].reshape(d, TILE))
        attn_sum[:, cols] = (
            tokens[:, cols].astype(F32) + product + vec[ROW_OB : ROW_OB + 1, cols]
        )
    unit, _ = row_norm(attn_sum[...])
    first = unit * vec[ROW_G1 : ROW_G1 + 1, :] + vec[ROW_S1 : ROW_S1 + 1, :]
    normed[...] = first
    low[...] = first.astype(BF16)


def out_project(ids, mixtures, wo, tokens, vec):
    rows, d = tokens.shape
    n = wo[0].shape[-2]
    fs = d // n
    outs = (
        struct((rows, d), F32),
        struct((rows, d), F32),
        struct((rows, d), BF16),
        struct((rows, d), BF16),
        struct((fs, n, d), BF16),
    )
    args = (ids, *mixtures, *wo, tokens, vec)
    return call(
        out_kernel,
        outs,
        args,
        name="out_project",
        in_specs=[whole(pltpu.SMEM)] + [whole()] * SEQ_N + [whole(HBM)] * SEQ_N + [whole()] * 2,
        scratch=[pltpu.SemaphoreType.DMA((SEQ_N, fs))],
        flops=2 * rows * d * d,
    )


def second_norm_kernel(normed, p0, p1, p2, cotangent, vec, layer_out, ffn_grad, low, sums):
    hidden = (
        normed[...]
        + (p0[...].astype(F32) + p1[...].astype(F32) + p2[...].astype(F32))
        + vec[ROW_DB : ROW_DB + 1, :]
    )
    unit, scale = row_norm(hidden)
    gain = vec[ROW_G2 : ROW_G2 + 1, :]
    layer_out[...] = (unit * gain + vec[ROW_S2 : ROW_S2 + 1, :]).astype(BF16)
    grad = cotangent[...].astype(F32)
    back = norm_back(grad, unit, scale, gain)
    ffn_grad[...] = back
    rounded = back.astype(BF16)
    low[...] = rounded
    sums[...] = jnp.zeros_like(sums)
    sums[0:1, :] = jnp.sum(grad * unit, 0, keepdims=True)
    sums[1:2, :] = jnp.sum(grad, 0, keepdims=True)
    sums[2:3, :] = jnp.sum(rounded.astype(F32), 0, keepdims=True)


def second_norm(normed, parts, cotangent, vec):
    rows, d = normed.shape
    outs = (
        struct((rows, d), BF16),
        struct((rows, d), F32),
        struct((rows, d), BF16),
        struct((8, d), F32),
    )
    return call(
        second_norm_kernel, outs, (normed, *parts, cotangent, vec), name="second_norm", flops=30 * rows * d
    )


def first_norm_kernel(ids, ffn_grad, p0, p1, p2, attn_sum, vec, w,
                      attn_grad, sums, n0, n1, n2, n3, low_out, low, back):
    s = ids[0]
    c = n0.shape[1]
    d = ffn_grad.shape[1]
    grad = ffn_grad[...] + (p0[...].astype(F32) + p1[...].astype(F32) + p2[...].astype(F32))
    unit, scale = row_norm(attn_sum[...])
    gain = vec[ROW_G1 : ROW_G1 + 1, :]
    value = norm_back(grad, unit, scale, gain)
    attn_grad[...] = value
    rounded = value.astype(BF16)
    low[...] = rounded
    low_out[...] = rounded
    sums[...] = jnp.zeros_like(sums)
    sums[0:1, :] = jnp.sum(grad * unit, 0, keepdims=True)
    sums[1:2, :] = jnp.sum(grad, 0, keepdims=True)
    sums[2:3, :] = jnp.sum(rounded.astype(F32), 0, keepdims=True)
    back[...] = dot_nt(low[...], w[...].reshape(d, d)).astype(BF16)
    for r, n in enumerate((n0, n1, n2, n3)):
        n[...] = back[:, pl.ds(pl.multiple_of((s ^ r) * c, c), c)]


def first_norm(ids, ffn_grad, parts, attn_sum, vec, wo):
    rows, d = ffn_grad.shape
    c = d // SEQ_N
    outs = (
        (struct((rows, d), F32), struct((8, d), F32))
        + (struct((rows, c), BF16),) * SEQ_N
        + (struct((rows, d), BF16),)
    )
    args = (ids, ffn_grad, *parts, attn_sum, vec, wo)
    return call(
        first_norm_kernel,
        outs,
        args,
        name="first_norm",
        in_specs=[whole(pltpu.SMEM)] + [whole()] * (len(args) - 1),
        scratch=[VMEM((rows, d), BF16), VMEM((rows, d), BF16)],
        flops=2 * rows * d * d,
    )


def out_grads_kernel(ids, mix, low, d0, d1, d2, d3):
    s = ids[0]
    c = d0.shape[1]
    for r, out in enumerate((d0, d1, d2, d3)):
        place = pl.ds(pl.multiple_of((s ^ r) * c, c), c)
        out[...] = dot_tn(mix[...], low[:, place]).astype(BF16)


def out_grads(ids, mix, low):
    rows, d = mix.shape
    c = d // SEQ_N
    return call(
        out_grads_kernel,
        (struct((d, c), BF16),) * SEQ_N,
        (ids, mix, low),
        name="out_grads",
        in_specs=[whole(pltpu.SMEM)] + [whole()] * 2,
        flops=2 * rows * d * d,
    )


TILE = 256


def gelu_and_slope(u):
    phi = 0.5 * lax.erf(u * (1.0 / math.sqrt(2.0))) + 0.5
    bell = u * (jnp.exp(-0.5 * u * u) * (1.0 / math.sqrt(2.0 * math.pi)))
    return u * phi, phi + bell


def ffn_kernel(ids, f0, f1, f2, f3, vec, packed, p0, p1, p2, p3, gelu, slope,
               held, made, up, down, sems, row_sems):
    rows, d = f0.shape
    held[2 * rows : 3 * rows, :] = f0[...]
    blocks = row_copies((f1, f3, None, f2), held, row_sems)
    n = up.shape[1]
    up_copies = [pltpu.make_async_copy(packed.at[:, pl.ds(0, n), :], up, sems.at[0])]
    down_copies = [pltpu.make_async_copy(packed.at[:, pl.ds(n, down.shape[1]), :], down, sems.at[1])]
    for copy in blocks + up_copies + down_copies:
        copy.start()
    hidden = gelu.shape[1]
    half = 2 * rows
    bias = vec[pl.ds(ROW_UB + ids[0], 1), :]
    for copy in blocks + up_copies + down_copies:
        copy.wait()

    def step(part, carry):
        at = pl.ds(pl.multiple_of(part * half, half), half)
        for t in range(hidden // TILE):
            cols = slice(t * TILE, (t + 1) * TILE)
            u = dot(held[at, :], up[:, :, cols].reshape(d, TILE)) + bias[:, cols]
            g, b = gelu_and_slope(u)
            gelu[at, cols] = g.astype(BF16)
            slope[at, cols] = b.astype(BF16)
        for t in range(d // TILE):
            cols = slice(t * TILE, (t + 1) * TILE)
            made[at, cols] = dot(gelu[at, :], down[:, :, cols].reshape(hidden, TILE)).astype(BF16)
        return carry

    lax.fori_loop(0, 2, step, 0)
    for i, out in enumerate((p1, p3, p0, p2)):
        out[...] = made[i * rows : (i + 1) * rows, :]


def weight_scratch(fs, d, hidden):
    return [
        VMEM((fs, d // fs, hidden), BF16),
        VMEM((fs, hidden // fs, d), BF16),
        pltpu.SemaphoreType.DMA((2,)),
        pltpu.SemaphoreType.DMA((SEQ_N,)),
    ]


def ffn(ids, blocks, packed, vec, hidden, fs):
    rows, d = blocks[0].shape
    total = SEQ_N * rows
    outs = (struct((rows, d), BF16),) * SEQ_N + (struct((total, hidden), BF16),) * 2
    return call(
        ffn_kernel,
        outs,
        (ids, blocks[0], *(hbm(b) for b in blocks[1:]), vec, hbm(packed)),
        name="ffn",
        in_specs=[whole(pltpu.SMEM), whole()] + [whole(HBM)] * 3 + [whole(), whole(HBM)],
        scratch=[VMEM((total, d), BF16)] * 2 + weight_scratch(fs, d, hidden),
        flops=4 * total * d * hidden,
        trans=2 * total * hidden,
    )


def ffn_back_kernel(ids, d0, d1, d2, d3, slope, packed, q0, q1, q2, q3, up_low, sums,
                    held, made, up, down, sems, row_sems):
    rows, d = d0.shape
    held[2 * rows : 3 * rows, :] = d0[...]
    blocks = row_copies((d1, d3, None, d2), held, row_sems)
    n = up.shape[1]
    up_copies = [pltpu.make_async_copy(packed.at[:, pl.ds(0, n), :], up, sems.at[0])]
    down_copies = [pltpu.make_async_copy(packed.at[:, pl.ds(n, down.shape[1]), :], down, sems.at[1])]
    for copy in blocks + down_copies + up_copies:
        copy.start()
    hidden = up_low.shape[1]
    half = 2 * rows
    per = TILE // up.shape[1]
    sums[...] = jnp.zeros_like(sums)
    for copy in blocks + down_copies + up_copies:
        copy.wait()

    def step(part, carry):
        at = pl.ds(pl.multiple_of(part * half, half), half)
        for t in range(hidden // TILE):
            cols = slice(t * TILE, (t + 1) * TILE)
            rhs = down[t * per : (t + 1) * per].reshape(TILE, d)
            u = (dot_nt(held[at, :], rhs) * slope[at, cols].astype(F32)).astype(BF16)
            up_low[at, cols] = u
            sums[0:1, cols] += jnp.sum(u.astype(F32), 0, keepdims=True)
        for t in range(d // TILE):
            cols = slice(t * TILE, (t + 1) * TILE)
            rhs = up[t * per : (t + 1) * per].reshape(TILE, hidden)
            made[at, cols] = dot_nt(up_low[at, :], rhs).astype(BF16)
        return carry

    lax.fori_loop(0, 2, step, 0)
    for i, out in enumerate((q1, q3, q0, q2)):
        out[...] = made[i * rows : (i + 1) * rows, :]


def ffn_back(ids, blocks, packed, slope, fs):
    rows, d = blocks[0].shape
    total, hidden = slope.shape
    outs = (struct((rows, d), BF16),) * SEQ_N + (
        struct((total, hidden), BF16),
        struct((8, hidden), F32),
    )
    return call(
        ffn_back_kernel,
        outs,
        (ids, *blocks, slope, packed),
        name="ffn_back",
        in_specs=[whole(pltpu.SMEM), whole()] + [whole(HBM)] * 3 + [whole(), whole(HBM)],
        scratch=[VMEM((total, d), BF16)] * 2 + weight_scratch(fs, d, hidden),
        flops=4 * total * d * hidden,
    )


def down_grads_kernel(gelu, d0, d1, d2, d3, out, right, made, sems, out_sems):
    rows, e = d0.shape
    copies = row_copies((d1, d3, None, d2), right, sems)
    for copy in copies:
        copy.start()
    right[2 * rows : 3 * rows, :] = d0[...]
    for copy in copies:
        copy.wait()
    results = []
    for t in range(gelu.shape[1] // TILE):
        at = slice(t * TILE, (t + 1) * TILE)
        made[at, :] = dot_tn(gelu[:, at], right[...]).astype(BF16)
        at = pl.ds(t * TILE, TILE)
        copy = pltpu.make_async_copy(made.at[at, :], out.at[at, :], out_sems.at[t])
        copy.start()
        results.append(copy)
    for copy in results:
        copy.wait()


def down_grads(gelu, lows):
    rows, d = lows[0].shape
    total, hidden = gelu.shape
    return call(
        down_grads_kernel,
        struct((hidden, d), BF16),
        (gelu, *lows),
        name="down_grads",
        light=32,
        in_specs=[whole()] * 2 + [whole(HBM)] * 3,
        out_specs=whole(HBM),
        scratch=[
            VMEM((total, d), BF16),
            VMEM((hidden, d), BF16),
            pltpu.SemaphoreType.DMA((SEQ_N,)),
            pltpu.SemaphoreType.DMA((hidden // TILE,)),
        ],
        flops=2 * total * d * hidden,
    )


def up_grads_kernel(ids, f0, f1, f2, f3, up_low, keep, send, left, turn, sems):
    copies = row_copies((f1, f3, f0, f2), left, sems)
    for copy in copies:
        copy.start()
    n = keep.shape[1]
    per = TILE // (2 * n)
    y = ids[1] & 1
    for copy in copies:
        copy.wait()
    for t in range(left.shape[1] // TILE):
        turn[...] = dot_tn(left[:, t * TILE : (t + 1) * TILE], up_low[...]).astype(BF16)
        for j in range(per):
            for out, side in ((keep, y), (send, 1 - y)):
                out[t * per + j] = turn[pl.ds(pl.multiple_of((2 * j + side) * n, n), n), :]


def up_grads(ids, firsts, up_low, fs):
    rows, d = firsts[0].shape
    total, hidden = up_low.shape
    return call(
        up_grads_kernel,
        (struct((fs // 2, d // fs, hidden), BF16),) * 2,
        (ids, *(hbm(f) for f in firsts), up_low),
        name="up_grads",
        light=32,
        in_specs=[whole(pltpu.SMEM)] + [whole(HBM)] * SEQ_N + [whole()],
        scratch=[VMEM((total, d), BF16), VMEM((TILE, hidden), BF16), pltpu.SemaphoreType.DMA((SEQ_N,))],
        flops=2 * total * d * hidden,
    )


def add(a, b):
    return (a.astype(F32) + b.astype(F32)).astype(BF16)


def sum_z(terms):
    return jnp.sum(turn_z(terms).astype(F32), 0).astype(BF16)


def scatter_fsdp(keep, came, *others):
    if isinstance(keep, (list, tuple)):
        total = None
        for k in (1, 2, 3, 0):
            here = keep[k].astype(F32) + came[k].astype(F32)
            if k:
                here = swap_z(here.astype(BF16), k, len(keep)).astype(F32)
            total = here if total is None else total + here
        return total.astype(BF16)
    return sum_z(after(add(keep, came), *others))


def fill_vectors(s, vec, back_sums, first_sums, second_sums, up_sums):
    c = vec.shape[1] // SEQ_N
    vec[...] = jnp.zeros_like(vec)
    cols = pl.ds(pl.multiple_of(s * c, c), c)
    vec[ROW_QB : ROW_QB + 1, cols] = back_sums[0:1, 0:c]
    vec[ROW_VB : ROW_VB + 1, cols] = back_sums[0:1, 2 * c : 3 * c]
    vec[ROW_OB : ROW_OB + 1, :] = first_sums[2:3, :]
    vec[ROW_DB : ROW_DB + 1, :] = second_sums[2:3, :]
    vec[ROW_G1 : ROW_G1 + 1, :] = first_sums[0:1, :]
    vec[ROW_S1 : ROW_S1 + 1, :] = first_sums[1:2, :]
    vec[ROW_G2 : ROW_G2 + 1, :] = second_sums[0:1, :]
    vec[ROW_S2 : ROW_S2 + 1, :] = second_sums[1:2, :]
    vec[pl.ds(ROW_UB + s, 1), :] = up_sums[0:1, :]


def qkvo_grads_kernel(ids, x0, x1, x2, x3, back, o0, o1, o2, s0, s1, s2, s3, *refs):
    outs, (held, vec, turn, sems) = refs[:-4], refs[-4:]
    s, f = ids[0], ids[1]
    nb, block, d = x0.shape
    e = back.shape[1]
    n = outs[0].shape[-2] - VEC
    zs = d // (2 * n)
    per = TILE // (2 * n)
    y = f & 1
    copies = row_copies([x.at[b] for b in range(nb) for x in (x0, x1, x2, x3)], held, sems)
    for copy in copies:
        copy.start()
    fill_vectors(s, vec, s0, s1, s2, s3)
    for copy in copies:
        copy.wait()
    if len(outs) > 2:
        for k in (1, 2, 3, 0):
            z = (f >> 1) ^ k
            rows = pl.ds(pl.multiple_of(z * TILE, TILE), TILE)
            turn[:, 0:e] = dot_tn(held[:, rows], back[...]).astype(BF16)
            turn[:, e:] = (
                o0[rows, :].astype(F32) + o1[rows, :].astype(F32) + o2[rows, :].astype(F32)
            ).astype(BF16)
            for out, side in ((outs[k], y), (outs[zs + k], 1 - y)):
                out[0:n, :] = turn[pl.ds(pl.multiple_of(side * n, n), n), :]
                out[n:, :] = jnp.zeros((VEC, out.shape[1]), BF16)
                cols = pl.ds(pl.multiple_of((2 * z + side) * n, n), n)
                out[n:, 0:n] = vec[:, cols].astype(BF16)
        return
    keep, send = outs
    for t in range(d // TILE):
        rows = slice(t * TILE, (t + 1) * TILE)
        turn[:, 0:e] = dot_tn(held[:, rows], back[...]).astype(BF16)
        turn[:, e:] = (
            o0[rows, :].astype(F32) + o1[rows, :].astype(F32) + o2[rows, :].astype(F32)
        ).astype(BF16)
        for j in range(per):
            z = t * per + j
            for out, side in ((keep, y), (send, 1 - y)):
                out[z, 0:n, :] = turn[pl.ds(pl.multiple_of((2 * j + side) * n, n), n), :]
    low = vec[...].astype(BF16)
    for z in range(zs):
        first, second = (low[:, (2 * z + i) * n : (2 * z + i + 1) * n] for i in range(2))
        for out, pick in ((keep, y == 0), (send, y != 0)):
            out[z, n:, :] = jnp.zeros((VEC, out.shape[2]), BF16)
            out[z, n:, 0:n] = jnp.where(pick, first, second)


def qkvo_grads(ids, blocks, back, out_parts, sums, fs):
    nb, block, d = blocks[0].shape
    total, e = back.shape
    n = d // fs
    wide = e + out_parts[0].shape[1]
    if fs == 8 and fits(n):
        outs = (struct((n + VEC, wide), BF16),) * 8
    else:
        outs = (struct((fs // 2, n + VEC, wide), BF16),) * 2
    return call(
        qkvo_grads_kernel,
        outs,
        (ids, *(hbm(b) for b in blocks), back, *out_parts, *sums),
        name="qkvo_grads",
        in_specs=[whole(pltpu.SMEM)] + [whole(HBM)] * SEQ_N + [whole()] * 8,
        scratch=[
            VMEM((total, d), BF16),
            VMEM((VEC, d), F32),
            VMEM((TILE, wide), BF16),
            pltpu.SemaphoreType.DMA((nb * SEQ_N,)),
        ],
        flops=2 * total * d * e,
    )


def finish_ffn_kernel(fs, ids, *refs):
    ups, downs, (up, down) = refs[:4], refs[4:8], refs[8:]
    s = ids[0]
    w = up.shape[1] // fs // SEQ_N
    for r in range(SEQ_N):
        at = s ^ r
        for j in range(fs):
            place = pl.ds(pl.multiple_of((j * SEQ_N + at) * w, w), w)
            up[:, place] = ups[r][:, j * w : (j + 1) * w].astype(F32)
        down[pl.ds(pl.multiple_of(at * w, w), w), :] = downs[r][...].astype(F32)


def finish_qkvo_kernel(ids, c0, c1, c2, c3, wq, wk, wv, wo, *vectors):
    s = ids[0]
    n = wq.shape[0]
    c = wq.shape[1] // SEQ_N
    total = 0.0
    for r, small in enumerate((c0, c1, c2, c3)):
        cols = pl.ds(pl.multiple_of((s ^ r) * c, c), c)
        for i, out in enumerate((wq, wk, wv, wo)):
            out[:, cols] = small[0:n, i * c : (i + 1) * c].astype(F32)
        total = total + small[n:, 0:n].astype(F32)
    for row, out in enumerate(vectors[:ROW_UB]):
        out[...] = total[row : row + 1, :].reshape(n)
    for j in range(SEQ_N):
        vectors[ROW_UB][j * n : (j + 1) * n] = total[ROW_UB + j : ROW_UB + j + 1, :].reshape(n)


def finish_ffn(ids, s, ups, downs, fs):
    n = ups[0].shape[0]
    w, d = downs[0].shape
    hidden = SEQ_N * fs * w
    if fits(n):
        return call(
            functools.partial(finish_ffn_kernel, fs),
            (struct((n, hidden), F32), struct((SEQ_N * w, d), F32)),
            (ids, *ups, *downs),
            name="finish_ffn",
            in_specs=[whole(pltpu.SMEM)] + [whole()] * 8,
        )
    order = jnp.arange(SEQ_N) ^ s
    up, down = (jnp.stack(v)[order].astype(F32) for v in (ups, downs))
    return (
        up.reshape(SEQ_N, n, fs, w).transpose(1, 2, 0, 3).reshape(n, hidden),
        down.reshape(SEQ_N * w, d),
    )


def finish_qkvo(ids, s, small):
    n = small[0].shape[0] - VEC
    d = small[0].shape[1]
    c = d // SEQ_N
    if fits(n):
        outs = (struct((n, d), F32),) * 4 + (struct((n,), F32),) * ROW_UB + (struct((SEQ_N * n,), F32),)
        done = call(
            finish_qkvo_kernel,
            outs,
            (ids, *small),
            name="finish_qkvo",
            in_specs=[whole(pltpu.SMEM)] + [whole()] * 4,
        )
        return done[:4], done[4:]
    small = jnp.stack(small)[jnp.arange(SEQ_N) ^ s].astype(F32)
    four = small[:, :n].reshape(SEQ_N, n, 4, c).transpose(2, 1, 0, 3).reshape(4, n, d)
    total = jnp.sum(small[:, n:, :n], 0)
    vectors = [total[row] for row in range(ROW_UB)]
    vectors.append(total[ROW_UB : ROW_UB + SEQ_N].reshape(SEQ_N * n))
    return [four[i] for i in range(4)], vectors


def body(fs, tokens_in, cotangent, query_weight, key_weight, value_weight, out_weight, up_weight,
         down_weight, query_bias, value_bias, out_bias, up_bias, down_bias, first_gain, first_shift,
         second_gain, second_shift):
    nb, block, d = tokens_in.shape
    rows = nb * block
    s = lax.axis_index(SEQ)
    f = lax.axis_index(FSDP)
    ids = jnp.stack([s, f]).astype(jnp.int32)
    flat = lambda a: a.reshape(rows, a.shape[-1])
    deep = lambda a: a.reshape(nb, block, a.shape[-1])

    scope = jax.named_scope
    early = pack_early(
        ids, s, query_weight, key_weight, value_weight, out_weight,
        [query_bias, value_bias, out_bias, down_bias, first_gain, first_shift, second_gain, second_shift],
        up_bias,
    )
    packed = pack_late(ids, s, fs, up_weight, down_weight)
    hidden = up_weight.shape[1] // SEQ_N
    with scope("tok"):
        tokens = gather_seq(tokens_in)
    with scope("wqkv"):
        wqkv = gather_early(early, fs)
    with scope("ffnw"):
        packed = lax.all_gather(after(packed, wqkv[0], *wqkv[3:5]), FSDP)
    with scope("wo"):
        n = d // fs
        wo = jnp.stack([p[..., :n, 3 * (d // SEQ_N) :] for p in wqkv])
        wo = [wo, seq_swap(wo, 1), seq_swap(wo, 2)]
    qkv, lse, *mixtures, wqkv, vec = attend(ids, tokens, wqkv, fs)
    with scope("wo"):
        wo.append(seq_swap(after(wo[2], vec), 1))
    with scope("mix"):
        mixtures = exchange_seq([flat(m) for m in mixtures])
    attn_sum, normed, first_low, mix, wo = out_project(ids, mixtures, wo, flat(tokens_in), vec)
    with scope("first"):
        firsts = gather_seq(first_low)
    *parts, gelu, slope = ffn(ids, firsts, packed, vec, hidden, fs)
    with scope("ffn"):
        parts, _ = reduce_seq(parts)
    layer_out, ffn_grad, down_low, second_sums = second_norm(normed, parts, flat(cotangent), vec)
    with scope("low"):
        lows = gather_seq(down_low)
    down_full = down_grads(gelu, lows)
    with scope("gdown"):
        down_grad = lax.psum_scatter(down_full, FSDP, scatter_dimension=0, tiled=True)
    slope = after(slope, down_full)
    *parts, up_low, up_sums = ffn_back(ids, lows, packed, slope, fs)
    with scope("ffnback"):
        parts, onward = reduce_seq(parts)
    keep_up, send_up = up_grads(ids, firsts, after(up_low, parts[1]), fs)
    with scope("gup"):
        came_up = swap_y(send_up)
    parts[0] = after(parts[0], keep_up)
    attn_grad, first_sums, *pieces, out_low = first_norm(ids, ffn_grad, parts, attn_sum, vec, wo)
    with scope("mixback"):
        grads = exchange_seq(pieces)
    out_parts = out_grads(ids, mix, out_low)
    with scope("outs"):
        out_parts, onward = reduce_seq(out_parts, *grads[2:])
    grads[0] = after(grads[0], onward, keep_up)
    back, back_sums, *parts = attend_back(qkv, lse, [deep(g) for g in grads], wqkv.reshape(d, -1))
    with scope("gup"):
        up_terms = add(keep_up, after(came_up, back))
        up_grad = sum_z(up_terms)
    back = after(back, up_terms, down_grad)
    pieces = qkvo_grads(
        ids, tokens, back.reshape(-1, back.shape[-1]), out_parts,
        (back_sums, first_sums, second_sums, up_sums), fs,
    )
    with scope("gqkvo"):
        half = len(pieces) // 2
        keep, send = pieces[:half], pieces[half:]
        if half == 1:
            small = scatter_fsdp(keep[0], swap_y(send[0]))
        else:
            came = {k: swap_y(send[k]) for k in (1, 2, 3, 0)}
            small = scatter_fsdp(keep, came)
    with scope("input"):
        terms, _ = reduce_seq([flat(p) for p in parts])
    input_grad = attn_grad + (
        terms[0].astype(F32) + terms[1].astype(F32) + terms[2].astype(F32)
    )
    with scope("fdown"):
        downs = gather_seq(after(down_grad, terms[2]))
    with scope("fup"):
        ups = gather_seq(after(up_grad, downs[2]))
    up, down = finish_ffn(ids, s, ups, downs, fs)
    with scope("small"):
        small = gather_seq(small, up)
    four, vecs = finish_qkvo(ids, s, small)
    return (
        deep(layer_out), deep(input_grad), *four, up, down,
        vecs[ROW_QB], vecs[ROW_VB], vecs[ROW_OB], vecs[ROW_UB], vecs[ROW_DB],
        vecs[ROW_G1], vecs[ROW_S1], vecs[ROW_G2], vecs[ROW_S2],
    )


def solution(mesh):
    count, fs = mesh.shape["seq"], mesh.shape["fsdp"]
    assert count == SEQ_N and fs % 4 == 0
    inner = Mesh(mesh.devices.reshape(2, 2, fs // 2, 2), SEQ + FSDP)
    rows, matrix, vector = P(FSDP, SEQ, None), P(FSDP, None), P(FSDP)
    in_specs = (rows,) * 2 + (matrix,) * 6 + (vector,) * 9
    return jax.shard_map(
        functools.partial(body, fs), mesh=inner, in_specs=in_specs, out_specs=in_specs, check_vma=False
    )
```

```python
import functools
import math

import jax
import jax.numpy as jnp
from jax import lax
from jax.experimental import pallas as pl
from jax.experimental.pallas import tpu as pltpu
from jax.sharding import Mesh, PartitionSpec as P

HD = 64
EPSILON = 1e-05
F32 = jnp.float32
BF16 = jnp.bfloat16
SEQ = ("x", "c")
FSDP = ("z", "y")
SEQ_N = 4
VEC = 16
ROW_QB, ROW_VB, ROW_OB, ROW_DB, ROW_G1, ROW_S1, ROW_G2, ROW_S2, ROW_UB = range(9)
VMEM = pltpu.VMEM
ANY = pl.ANY
HBM = pltpu.HBM
LIMITS = {"early_pack": 56, "late_pack": 56}


def dot(a, b):
    return lax.dot_general(a, b, (((1,), (0,)), ((), ())), preferred_element_type=F32)


def dot_nt(a, b):
    return lax.dot_general(a, b, (((1,), (1,)), ((), ())), preferred_element_type=F32)


def dot_tn(a, b):
    return lax.dot_general(a, b, (((0,), (0,)), ((), ())), preferred_element_type=F32)


def struct(shape, dtype):
    return jax.ShapeDtypeStruct(shape, dtype)


def nbytes(tree):
    return sum(math.prod(a.shape) * a.dtype.itemsize for a in jax.tree.leaves(tree))


def whole(space=VMEM):
    return pl.BlockSpec(memory_space=space)


def call(kernel, outs, args, *, name, grid=None, in_specs=None, out_specs=None, scratch=(), flops=0, trans=0, light=1):
    if in_specs is None:
        in_specs = [whole() for _ in args]
    if out_specs is None:
        out_specs = jax.tree.map(lambda _: whole(), outs)
    kwargs = {} if grid is None else {"grid": grid}
    return pl.pallas_call(
        kernel,
        out_shape=outs,
        in_specs=in_specs,
        out_specs=out_specs,
        scratch_shapes=list(scratch),
        compiler_params=pltpu.CompilerParams(vmem_limit_bytes=LIMITS.get(name, 20) << 20),
        cost_estimate=pl.CostEstimate(
            flops=flops // light,
            bytes_accessed=(nbytes(args) + nbytes(outs)) // light,
            transcendentals=trans,
        ),
        name=name,
        **kwargs,
    )(*args)


def seq_swap(value, k):
    with jax.named_scope(f"seq{k}"):
        return lax.ppermute(value, SEQ, [(i, i ^ k) for i in range(SEQ_N)])


def gather_seq(value, *others):
    far = seq_swap(value, 2)
    near = seq_swap(value, 1)
    return [value, near, far, seq_swap(after(far, *others), 1)]


def reduce_seq(parts, *others):
    near2 = seq_swap(parts[3], 1)
    onward = (parts[2].astype(F32) + near2.astype(F32)).astype(BF16)
    near0 = seq_swap(after(parts[1], onward), 1)
    return [parts[0], near0, seq_swap(after(onward, *others), 2)], onward


def exchange_seq(parts):
    return [parts[0]] + [seq_swap(parts[r], r) for r in (1, 2, 3)]


def swap_y(value):
    with jax.named_scope("y"):
        return lax.ppermute(value, "y", [(0, 1), (1, 0)])


def swap_z(value, k, count):
    with jax.named_scope(f"z{k}"):
        return lax.ppermute(value, "z", [(i, i ^ k) for i in range(count)])


def turn_z(value):
    with jax.named_scope("z"):
        return lax.all_to_all(value, "z", split_axis=0, concat_axis=0, tiled=True)


def after(value, *others):
    return lax.optimization_barrier((value, *others))[0] if others else value


def fits(n):
    return n % 128 == 0


def row_copies(blocks, target, sems):
    rows = blocks[0].shape[0]
    return [
        pltpu.make_async_copy(x, target.at[pl.ds(i * rows, rows), :], sems.at[i])
        for i, x in enumerate(blocks)
        if x is not None
    ]


def hbm(value):
    return pltpu.with_memory_space_constraint(value, HBM)


def run_copies(copies):
    for copy in copies:
        copy.start()
    for copy in copies:
        copy.wait()


def early_pack_kernel(ids, wq, wk, wv, wo, *refs):
    *vectors, up_bias, out, sems = refs
    s = ids[0]
    n = wq.shape[0]
    c = wq.shape[1] // SEQ_N
    cols = pl.ds(pl.multiple_of(s * c, c), c)
    copies = [
        pltpu.make_async_copy(w.at[:, cols], out.at[pl.ds(0, n), pl.ds(i * c, c)], sems.at[i])
        for i, w in enumerate((wq, wk, wv, wo))
    ]
    for copy in copies:
        copy.start()
    rows = [v[...].astype(F32).reshape(1, n) for v in vectors]
    rows += [up_bias[j * n : (j + 1) * n].astype(F32).reshape(1, n) for j in range(SEQ_N)]
    rows.append(jnp.zeros((VEC - len(rows), n), F32))
    out[n:, 0:n] = jnp.concatenate(rows, 0).astype(BF16)
    out[n:, n:] = jnp.zeros((VEC, out.shape[1] - n), BF16)
    for copy in copies:
        copy.wait()


def late_pack_kernel(fs, ids, up, down, out, sems):
    s = ids[0]
    n = up.shape[0]
    w = up.shape[1] // fs // SEQ_N
    copies = []
    for j in range(fs):
        cols = pl.ds(pl.multiple_of((j * SEQ_N + s) * w, w), w)
        copies.append(
            pltpu.make_async_copy(
                up.at[:, cols], out.at[pl.ds(0, n), pl.ds(j * w, w)], sems.at[j]
            )
        )
    rows = pl.ds(pl.multiple_of(s * w, w), w)
    copies.append(pltpu.make_async_copy(down.at[rows, :], out.at[pl.ds(n, w), :], sems.at[fs]))
    run_copies(copies)


def pack_early(ids, s, wq, wk, wv, wo, vectors, up_bias):
    n, d = wq.shape
    c = d // SEQ_N
    if fits(n):
        return call(
            early_pack_kernel,
            struct((n + VEC, d), BF16),
            (ids, wq, wk, wv, wo, *vectors, up_bias),
            name="early_pack",
            in_specs=[whole(pltpu.SMEM)] + [whole(HBM)] * 4 + [whole()] * (len(vectors) + 1),
            scratch=[pltpu.SemaphoreType.DMA((4,))],
        )
    rows = jnp.concatenate(vectors + [up_bias]).reshape(-1, n)
    vec = jnp.pad(rows, ((0, VEC - rows.shape[0]), (0, d - n)))
    four = [lax.dynamic_slice(m, (0, s * c), (n, c)) for m in (wq, wk, wv, wo)]
    return jnp.concatenate([jnp.concatenate(four, 1), vec], 0)


def pack_late(ids, s, fs, up, down):
    n, d = up.shape[0], down.shape[1]
    w = up.shape[1] // fs // SEQ_N
    if fits(n):
        return call(
            functools.partial(late_pack_kernel, fs),
            struct((n + w, d), BF16),
            (ids, up, down),
            name="late_pack",
            in_specs=[whole(pltpu.SMEM)] + [whole(HBM)] * 2,
            scratch=[pltpu.SemaphoreType.DMA((fs + 1,))],
        )
    mine = lax.dynamic_index_in_dim(up.reshape(n, fs, SEQ_N, w), s, 2, keepdims=False)
    return jnp.concatenate([mine.reshape(n, fs * w), lax.dynamic_slice(down, (s * w, 0), (w, d))], 0)


def gather_early(value, fs):
    zs = fs // 2
    if zs != 4:
        own = turn_z(jnp.broadcast_to(value, (zs,) + value.shape))
        return [own, swap_y(own)]
    own = [value] + [swap_z(value, k, zs) for k in (3, 2, 1)][::-1]
    return own + [swap_y(own[k]) for k in range(zs)]


def load_blocks(pieces, f, first, rows, target, sems):
    zs = target.shape[0] // 2
    y = f & 1
    rows = pl.ds(first, rows)
    cols = pl.ds(0, target.shape[2])
    if len(pieces) == 2:
        return [
            pltpu.make_async_copy(piece.at[j, rows, cols], target.at[2 * j + at], sems.at[i * zs + j])
            for i, (piece, at) in enumerate(zip(pieces, (y, 1 - y)))
            for j in range(zs)
        ]
    return [
        pltpu.make_async_copy(
            piece.at[rows, cols], target.at[f ^ (2 * (i % zs) + i // zs)], sems.at[i]
        )
        for i, piece in enumerate(pieces)
    ]


def attend_kernel(count, ids, x0, x1, x2, x3, *refs):
    pieces = refs[:count]
    qkv, lse, m0, m1, m2, m3, w_out, vec, held, mix, w, small, sems, small_sems, x_sems = refs[count:]
    fs = w.shape[0]
    n = w.shape[1]
    c = w.shape[2] // 3
    d = fs * n
    heads = c // HD
    nb, block, _ = x0.shape
    f = ids[1]
    b = pl.program_id(0)
    out_copy = pltpu.make_async_copy(w, w_out, sems.at[fs])

    @pl.when(pl.program_id(0) == 0)
    def _():
        for i in range(nb):
            for copy in row_copies([x.at[i] for x in (x0, x1, x2, x3)], held.at[i], x_sems.at[i]):
                copy.start()
        copies = load_blocks(pieces, f, 0, n, w, sems)
        copies += load_blocks(pieces, f, n, VEC, small, small_sems)
        run_copies(copies)
        for j in range(fs):
            vec[:, j * n : (j + 1) * n] = small[j, :, 0:n].astype(F32)
        out_copy.start()

    for copy in row_copies([x.at[b] for x in (x0, x1, x2, x3)], held.at[b], x_sems.at[b]):
        copy.wait()
    cols = pl.ds(pl.multiple_of(ids[0] * c, c), c)
    for part in range(3):
        acc = dot(held[b], w[:, :, part * c : (part + 1) * c].reshape(d, c))
        if part != 1:
            row = ROW_QB if part == 0 else ROW_VB
            acc = acc + vec[row : row + 1, cols]
        qkv[0, :, part * c : (part + 1) * c] = acc.astype(BF16)
    scale = 1.0 / math.sqrt(HD)
    for h in range(heads):
        at = h * HD
        query = (qkv[0, :, at : at + HD].astype(F32) * scale).astype(BF16)
        key = qkv[0, :, c + at : c + at + HD]
        value = qkv[0, :, 2 * c + at : 2 * c + at + HD]
        scores = dot_nt(key, query)
        highest = jnp.max(scores, 0, keepdims=True)
        raised = jnp.exp(scores - highest)
        summed = jnp.sum(raised, 0, keepdims=True)
        lse[0, h : h + 1, :] = highest + jnp.log(summed)
        low = (raised * (1.0 / summed)).astype(BF16)
        mix[at : at + HD, :] = dot_tn(value, low)
    mixture = mix[...].T.astype(BF16)
    for r, m in enumerate((m0, m1, m2, m3)):
        m[0] = mixture[r * block : (r + 1) * block, :]

    @pl.when(pl.program_id(0) == pl.num_programs(0) - 1)
    def _():
        out_copy.wait()


def attend(ids, blocks, pieces, fs):
    nb, block, d = blocks[0].shape
    c = d // SEQ_N
    n = d // fs
    length = SEQ_N * block
    heads = c // HD
    one = lambda shape: pl.BlockSpec((1,) + shape, lambda b: (b,) + (0,) * len(shape))
    fixed = lambda shape: pl.BlockSpec(shape, lambda b: (0,) * len(shape))
    outs = (
        (struct((nb, length, 3 * c), BF16), struct((nb, heads, length), F32))
        + (struct((nb, block, c), BF16),) * SEQ_N
        + (struct((fs, n, 3 * c), BF16), struct((VEC, d), F32))
    )
    return call(
        functools.partial(attend_kernel, len(pieces)),
        outs,
        (ids, *blocks, *pieces),
        name="attend",
        grid=(nb,),
        in_specs=[whole(pltpu.SMEM)] + [whole(HBM)] * (SEQ_N + len(pieces)),
        out_specs=(one((length, 3 * c)), one((heads, length)))
        + (one((block, c)),) * SEQ_N
        + (whole(ANY), fixed((VEC, d))),
        scratch=[
            VMEM((nb, length, d), BF16),
            VMEM((c, length), F32),
            VMEM((fs, n, 3 * c), BF16),
            VMEM((fs, VEC, max(n, 128)), BF16),
            pltpu.SemaphoreType.DMA((fs + 1,)),
            pltpu.SemaphoreType.DMA((fs,)),
            pltpu.SemaphoreType.DMA((nb, SEQ_N)),
        ],
        flops=2 * nb * length * (3 * c * d + 2 * length * c),
        trans=nb * heads * length * length,
    )


def attend_back_kernel(qkv, lse, h0, h1, h2, h3, w, back, sums, r0, r1, r2, r3, held, turned):
    c = w.shape[1] // 3
    heads = c // HD
    block = h0.shape[1]
    for r, h in enumerate((h0, h1, h2, h3)):
        held[r * block : (r + 1) * block, :] = h[0]
    scale = 1.0 / math.sqrt(HD)
    for h in range(heads):
        at = h * HD
        query = (qkv[0, :, at : at + HD].astype(F32) * scale).astype(BF16)
        key = qkv[0, :, c + at : c + at + HD]
        value = qkv[0, :, 2 * c + at : 2 * c + at + HD]
        grad = held[:, at : at + HD]
        scores = dot_nt(key, query)
        attention = jnp.exp(scores - lse[0, h : h + 1, :])
        attention_grad = dot_nt(value, grad)
        inner = jnp.sum(attention * attention_grad, 0, keepdims=True)
        low = (attention * (attention_grad - inner)).astype(BF16)
        turned[at : at + HD, :] = dot_tn(key, low) * scale
        back[0, :, c + at : c + at + HD] = dot(low, query).astype(BF16)
        back[0, :, 2 * c + at : 2 * c + at + HD] = dot(attention.astype(BF16), grad).astype(BF16)
    back[0, :, 0:c] = turned[...].T.astype(BF16)
    whole_back = back[0]
    total = jnp.sum(whole_back.astype(F32), 0, keepdims=True)

    @pl.when(pl.program_id(0) == 0)
    def _():
        sums[...] = jnp.zeros_like(sums)

    sums[0:1, :] += total
    for r, out in enumerate((r0, r1, r2, r3)):
        out[0] = dot_nt(back[0, r * block : (r + 1) * block, :], w[...]).astype(BF16)


def attend_back(qkv, lse, grads, wqkv):
    nb, length, c3 = qkv.shape
    d = wqkv.shape[0]
    block = length // SEQ_N
    c = c3 // 3
    heads = c // HD
    one = lambda shape: pl.BlockSpec((1,) + shape, lambda b: (b,) + (0,) * len(shape))
    fixed = lambda shape: pl.BlockSpec(shape, lambda b: (0,) * len(shape))
    outs = (struct((nb, length, c3), BF16), struct((8, c3), F32)) + (
        struct((nb, block, d), BF16),
    ) * SEQ_N
    return call(
        attend_back_kernel,
        outs,
        (qkv, lse, *grads, wqkv),
        name="attend_back",
        light=32,
        grid=(nb,),
        in_specs=[one((length, c3)), one((heads, length))]
        + [one((block, c))] * SEQ_N
        + [fixed(wqkv.shape)],
        out_specs=(one((length, c3)), fixed((8, c3))) + (one((block, d)),) * SEQ_N,
        scratch=[VMEM((length, c), BF16), VMEM((c, length), F32)],
        flops=2 * nb * length * (c3 * d + 5 * length * c),
        trans=nb * heads * length * length,
    )


def row_norm(hidden):
    average = jnp.mean(hidden, -1, keepdims=True)
    centered = hidden - average
    spread = jnp.mean(centered * centered, -1, keepdims=True)
    scale = lax.rsqrt(spread + EPSILON)
    return centered * scale, scale


def norm_back(grad, normed, scale, gain):
    inner = grad * gain
    first = jnp.mean(inner, -1, keepdims=True)
    second = jnp.mean(inner * normed, -1, keepdims=True)
    return scale * (inner - first - normed * second)


def out_kernel(ids, m0, m1, m2, m3, w0, w1, w2, w3, tokens, vec,
               attn_sum, normed, low, mix, w, sems):
    s, f = ids[0], ids[1]
    c = m0.shape[1]
    fs, n, d = w.shape
    places = [pl.ds(pl.multiple_of((s ^ r) * c, c), c) for r in range(SEQ_N)]
    copies = []
    for r, (place, wr) in enumerate(zip(places, (w0, w1, w2, w3))):
        copies += load_blocks([wr.at[i] for i in range(wr.shape[0])], f, 0, n, w.at[:, :, place], sems.at[r])
    for copy in copies:
        copy.start()
    for place, m in zip(places, (m0, m1, m2, m3)):
        mix[:, place] = m[...]
    for copy in copies:
        copy.wait()
    for t in range(d // TILE):
        cols = slice(t * TILE, (t + 1) * TILE)
        product = dot(mix[...], w[:, :, cols].reshape(d, TILE))
        attn_sum[:, cols] = (
            tokens[:, cols].astype(F32) + product + vec[ROW_OB : ROW_OB + 1, cols]
        )
    unit, _ = row_norm(attn_sum[...])
    first = unit * vec[ROW_G1 : ROW_G1 + 1, :] + vec[ROW_S1 : ROW_S1 + 1, :]
    normed[...] = first
    low[...] = first.astype(BF16)


def out_project(ids, mixtures, wo, tokens, vec):
    rows, d = tokens.shape
    n = wo[0].shape[-2]
    fs = d // n
    outs = (
        struct((rows, d), F32),
        struct((rows, d), F32),
        struct((rows, d), BF16),
        struct((rows, d), BF16),
        struct((fs, n, d), BF16),
    )
    args = (ids, *mixtures, *wo, tokens, vec)
    return call(
        out_kernel,
        outs,
        args,
        name="out_project",
        in_specs=[whole(pltpu.SMEM)] + [whole()] * SEQ_N + [whole(HBM)] * SEQ_N + [whole()] * 2,
        scratch=[pltpu.SemaphoreType.DMA((SEQ_N, fs))],
        flops=2 * rows * d * d,
    )


def second_norm_kernel(normed, p0, p1, p2, cotangent, vec, layer_out, ffn_grad, low, sums):
    hidden = (
        normed[...]
        + (p0[...].astype(F32) + p1[...].astype(F32) + p2[...].astype(F32))
        + vec[ROW_DB : ROW_DB + 1, :]
    )
    unit, scale = row_norm(hidden)
    gain = vec[ROW_G2 : ROW_G2 + 1, :]
    layer_out[...] = (unit * gain + vec[ROW_S2 : ROW_S2 + 1, :]).astype(BF16)
    grad = cotangent[...].astype(F32)
    back = norm_back(grad, unit, scale, gain)
    ffn_grad[...] = back
    rounded = back.astype(BF16)
    low[...] = rounded
    sums[...] = jnp.zeros_like(sums)
    sums[0:1, :] = jnp.sum(grad * unit, 0, keepdims=True)
    sums[1:2, :] = jnp.sum(grad, 0, keepdims=True)
    sums[2:3, :] = jnp.sum(rounded.astype(F32), 0, keepdims=True)


def second_norm(normed, parts, cotangent, vec):
    rows, d = normed.shape
    outs = (
        struct((rows, d), BF16),
        struct((rows, d), F32),
        struct((rows, d), BF16),
        struct((8, d), F32),
    )
    return call(
        second_norm_kernel, outs, (normed, *parts, cotangent, vec), name="second_norm", flops=30 * rows * d
    )


def first_norm_kernel(ids, ffn_grad, p0, p1, p2, attn_sum, vec, w,
                      attn_grad, sums, n0, n1, n2, n3, low_out, low, back):
    s = ids[0]
    c = n0.shape[1]
    d = ffn_grad.shape[1]
    grad = ffn_grad[...] + (p0[...].astype(F32) + p1[...].astype(F32) + p2[...].astype(F32))
    unit, scale = row_norm(attn_sum[...])
    gain = vec[ROW_G1 : ROW_G1 + 1, :]
    value = norm_back(grad, unit, scale, gain)
    attn_grad[...] = value
    rounded = value.astype(BF16)
    low[...] = rounded
    low_out[...] = rounded
    sums[...] = jnp.zeros_like(sums)
    sums[0:1, :] = jnp.sum(grad * unit, 0, keepdims=True)
    sums[1:2, :] = jnp.sum(grad, 0, keepdims=True)
    sums[2:3, :] = jnp.sum(rounded.astype(F32), 0, keepdims=True)
    back[...] = dot_nt(low[...], w[...].reshape(d, d)).astype(BF16)
    for r, n in enumerate((n0, n1, n2, n3)):
        n[...] = back[:, pl.ds(pl.multiple_of((s ^ r) * c, c), c)]


def first_norm(ids, ffn_grad, parts, attn_sum, vec, wo):
    rows, d = ffn_grad.shape
    c = d // SEQ_N
    outs = (
        (struct((rows, d), F32), struct((8, d), F32))
        + (struct((rows, c), BF16),) * SEQ_N
        + (struct((rows, d), BF16),)
    )
    args = (ids, ffn_grad, *parts, attn_sum, vec, wo)
    return call(
        first_norm_kernel,
        outs,
        args,
        name="first_norm",
        light=32,
        in_specs=[whole(pltpu.SMEM)] + [whole()] * (len(args) - 1),
        scratch=[VMEM((rows, d), BF16), VMEM((rows, d), BF16)],
        flops=2 * rows * d * d,
    )


def out_grads_kernel(ids, mix, low, d0, d1, d2, d3):
    s = ids[0]
    c = d0.shape[1]
    for r, out in enumerate((d0, d1, d2, d3)):
        place = pl.ds(pl.multiple_of((s ^ r) * c, c), c)
        out[...] = dot_tn(mix[...], low[:, place]).astype(BF16)


def out_grads(ids, mix, low):
    rows, d = mix.shape
    c = d // SEQ_N
    return call(
        out_grads_kernel,
        (struct((d, c), BF16),) * SEQ_N,
        (ids, mix, low),
        name="out_grads",
        light=32,
        in_specs=[whole(pltpu.SMEM)] + [whole()] * 2,
        flops=2 * rows * d * d,
    )


TILE = 256


def gelu_and_slope(u):
    phi = 0.5 * lax.erf(u * (1.0 / math.sqrt(2.0))) + 0.5
    bell = u * (jnp.exp(-0.5 * u * u) * (1.0 / math.sqrt(2.0 * math.pi)))
    return u * phi, phi + bell


def ffn_kernel(ids, f0, f1, f2, f3, vec, packed, p0, p1, p2, p3, gelu, slope,
               held, made, up, down, sems, row_sems):
    rows, d = f0.shape
    held[2 * rows : 3 * rows, :] = f0[...]
    blocks = row_copies((f1, f3, None, f2), held, row_sems)
    n = up.shape[1]
    up_copies = [pltpu.make_async_copy(packed.at[:, pl.ds(0, n), :], up, sems.at[0])]
    down_copies = [pltpu.make_async_copy(packed.at[:, pl.ds(n, down.shape[1]), :], down, sems.at[1])]
    for copy in blocks + up_copies + down_copies:
        copy.start()
    hidden = gelu.shape[1]
    half = 2 * rows
    bias = vec[pl.ds(ROW_UB + ids[0], 1), :]
    for copy in blocks + up_copies + down_copies:
        copy.wait()

    def step(part, carry):
        at = pl.ds(pl.multiple_of(part * half, half), half)
        for t in range(hidden // TILE):
            cols = slice(t * TILE, (t + 1) * TILE)
            u = dot(held[at, :], up[:, :, cols].reshape(d, TILE)) + bias[:, cols]
            g, b = gelu_and_slope(u)
            gelu[at, cols] = g.astype(BF16)
            slope[at, cols] = b.astype(BF16)
        for t in range(d // TILE):
            cols = slice(t * TILE, (t + 1) * TILE)
            made[at, cols] = dot(gelu[at, :], down[:, :, cols].reshape(hidden, TILE)).astype(BF16)
        return carry

    lax.fori_loop(0, 2, step, 0)
    for i, out in enumerate((p1, p3, p0, p2)):
        out[...] = made[i * rows : (i + 1) * rows, :]


def weight_scratch(fs, d, hidden):
    return [
        VMEM((fs, d // fs, hidden), BF16),
        VMEM((fs, hidden // fs, d), BF16),
        pltpu.SemaphoreType.DMA((2,)),
        pltpu.SemaphoreType.DMA((SEQ_N,)),
    ]


def ffn(ids, blocks, packed, vec, hidden, fs):
    rows, d = blocks[0].shape
    total = SEQ_N * rows
    outs = (struct((rows, d), BF16),) * SEQ_N + (struct((total, hidden), BF16),) * 2
    return call(
        ffn_kernel,
        outs,
        (ids, blocks[0], *(hbm(b) for b in blocks[1:]), vec, hbm(packed)),
        name="ffn",
        in_specs=[whole(pltpu.SMEM), whole()] + [whole(HBM)] * 3 + [whole(), whole(HBM)],
        scratch=[VMEM((total, d), BF16)] * 2 + weight_scratch(fs, d, hidden),
        flops=4 * total * d * hidden,
        trans=2 * total * hidden,
    )


def ffn_back_kernel(ids, d0, d1, d2, d3, slope, packed, q0, q1, q2, q3, up_low, sums,
                    held, made, up, down, sems, row_sems):
    rows, d = d0.shape
    held[2 * rows : 3 * rows, :] = d0[...]
    blocks = row_copies((d1, d3, None, d2), held, row_sems)
    n = up.shape[1]
    up_copies = [pltpu.make_async_copy(packed.at[:, pl.ds(0, n), :], up, sems.at[0])]
    down_copies = [pltpu.make_async_copy(packed.at[:, pl.ds(n, down.shape[1]), :], down, sems.at[1])]
    for copy in blocks + down_copies + up_copies:
        copy.start()
    hidden = up_low.shape[1]
    half = 2 * rows
    per = TILE // up.shape[1]
    sums[...] = jnp.zeros_like(sums)
    for copy in blocks + down_copies + up_copies:
        copy.wait()

    def step(part, carry):
        at = pl.ds(pl.multiple_of(part * half, half), half)
        for t in range(hidden // TILE):
            cols = slice(t * TILE, (t + 1) * TILE)
            rhs = down[t * per : (t + 1) * per].reshape(TILE, d)
            u = (dot_nt(held[at, :], rhs) * slope[at, cols].astype(F32)).astype(BF16)
            up_low[at, cols] = u
            sums[0:1, cols] += jnp.sum(u.astype(F32), 0, keepdims=True)
        for t in range(d // TILE):
            cols = slice(t * TILE, (t + 1) * TILE)
            rhs = up[t * per : (t + 1) * per].reshape(TILE, hidden)
            made[at, cols] = dot_nt(up_low[at, :], rhs).astype(BF16)
        return carry

    lax.fori_loop(0, 2, step, 0)
    for i, out in enumerate((q1, q3, q0, q2)):
        out[...] = made[i * rows : (i + 1) * rows, :]


def ffn_back(ids, blocks, packed, slope, fs):
    rows, d = blocks[0].shape
    total, hidden = slope.shape
    outs = (struct((rows, d), BF16),) * SEQ_N + (
        struct((total, hidden), BF16),
        struct((8, hidden), F32),
    )
    return call(
        ffn_back_kernel,
        outs,
        (ids, *blocks, slope, packed),
        name="ffn_back",
        in_specs=[whole(pltpu.SMEM), whole()] + [whole(HBM)] * 3 + [whole(), whole(HBM)],
        scratch=[VMEM((total, d), BF16)] * 2 + weight_scratch(fs, d, hidden),
        flops=4 * total * d * hidden,
    )


def down_grads_kernel(gelu, d0, d1, d2, d3, out, right, made, sems, out_sems):
    rows, e = d0.shape
    copies = row_copies((d1, d3, None, d2), right, sems)
    for copy in copies:
        copy.start()
    right[2 * rows : 3 * rows, :] = d0[...]
    for copy in copies:
        copy.wait()
    results = []
    for t in range(gelu.shape[1] // TILE):
        at = slice(t * TILE, (t + 1) * TILE)
        made[at, :] = dot_tn(gelu[:, at], right[...]).astype(BF16)
        at = pl.ds(t * TILE, TILE)
        copy = pltpu.make_async_copy(made.at[at, :], out.at[at, :], out_sems.at[t])
        copy.start()
        results.append(copy)
    for copy in results:
        copy.wait()


def down_grads(gelu, lows):
    rows, d = lows[0].shape
    total, hidden = gelu.shape
    return call(
        down_grads_kernel,
        struct((hidden, d), BF16),
        (gelu, *lows),
        name="down_grads",
        light=32,
        in_specs=[whole()] * 2 + [whole(HBM)] * 3,
        out_specs=whole(HBM),
        scratch=[
            VMEM((total, d), BF16),
            VMEM((hidden, d), BF16),
            pltpu.SemaphoreType.DMA((SEQ_N,)),
            pltpu.SemaphoreType.DMA((hidden // TILE,)),
        ],
        flops=2 * total * d * hidden,
    )


def up_grads_kernel(ids, f0, f1, f2, f3, up_low, keep, send, left, turn, sems):
    copies = row_copies((f1, f3, f0, f2), left, sems)
    for copy in copies:
        copy.start()
    n = keep.shape[1]
    per = TILE // (2 * n)
    y = ids[1] & 1
    for copy in copies:
        copy.wait()
    for t in range(left.shape[1] // TILE):
        turn[...] = dot_tn(left[:, t * TILE : (t + 1) * TILE], up_low[...]).astype(BF16)
        for j in range(per):
            for out, side in ((keep, y), (send, 1 - y)):
                out[t * per + j] = turn[pl.ds(pl.multiple_of((2 * j + side) * n, n), n), :]


def up_grads(ids, firsts, up_low, fs):
    rows, d = firsts[0].shape
    total, hidden = up_low.shape
    return call(
        up_grads_kernel,
        (struct((fs // 2, d // fs, hidden), BF16),) * 2,
        (ids, *(hbm(f) for f in firsts), up_low),
        name="up_grads",
        light=32,
        in_specs=[whole(pltpu.SMEM)] + [whole(HBM)] * SEQ_N + [whole()],
        scratch=[VMEM((total, d), BF16), VMEM((TILE, hidden), BF16), pltpu.SemaphoreType.DMA((SEQ_N,))],
        flops=2 * total * d * hidden,
    )


def add(a, b):
    return (a.astype(F32) + b.astype(F32)).astype(BF16)


def sum_z(terms):
    return jnp.sum(turn_z(terms).astype(F32), 0).astype(BF16)


def scatter_fsdp(keep, came, *others):
    if isinstance(keep, (list, tuple)):
        total = None
        for k in (1, 2, 3, 0):
            here = keep[k].astype(F32) + came[k].astype(F32)
            if k:
                here = swap_z(here.astype(BF16), k, len(keep)).astype(F32)
            total = here if total is None else total + here
        return total.astype(BF16)
    return sum_z(after(add(keep, came), *others))


def fill_vectors(s, vec, back_sums, first_sums, second_sums, up_sums):
    c = vec.shape[1] // SEQ_N
    vec[...] = jnp.zeros_like(vec)
    cols = pl.ds(pl.multiple_of(s * c, c), c)
    vec[ROW_QB : ROW_QB + 1, cols] = back_sums[0:1, 0:c]
    vec[ROW_VB : ROW_VB + 1, cols] = back_sums[0:1, 2 * c : 3 * c]
    vec[ROW_OB : ROW_OB + 1, :] = first_sums[2:3, :]
    vec[ROW_DB : ROW_DB + 1, :] = second_sums[2:3, :]
    vec[ROW_G1 : ROW_G1 + 1, :] = first_sums[0:1, :]
    vec[ROW_S1 : ROW_S1 + 1, :] = first_sums[1:2, :]
    vec[ROW_G2 : ROW_G2 + 1, :] = second_sums[0:1, :]
    vec[ROW_S2 : ROW_S2 + 1, :] = second_sums[1:2, :]
    vec[pl.ds(ROW_UB + s, 1), :] = up_sums[0:1, :]


def qkvo_grads_kernel(ids, x0, x1, x2, x3, back, o0, o1, o2, s0, s1, s2, s3, *refs):
    outs, (held, vec, turn, sems) = refs[:-4], refs[-4:]
    s, f = ids[0], ids[1]
    nb, block, d = x0.shape
    e = back.shape[1]
    n = outs[0].shape[-2] - VEC
    zs = d // (2 * n)
    per = TILE // (2 * n)
    y = f & 1
    copies = row_copies([x.at[b] for b in range(nb) for x in (x0, x1, x2, x3)], held, sems)
    for copy in copies:
        copy.start()
    fill_vectors(s, vec, s0, s1, s2, s3)
    for copy in copies:
        copy.wait()
    if len(outs) > 2:
        for k in (1, 2, 3, 0):
            z = (f >> 1) ^ k
            rows = pl.ds(pl.multiple_of(z * TILE, TILE), TILE)
            turn[:, 0:e] = dot_tn(held[:, rows], back[...]).astype(BF16)
            turn[:, e:] = (
                o0[rows, :].astype(F32) + o1[rows, :].astype(F32) + o2[rows, :].astype(F32)
            ).astype(BF16)
            for out, side in ((outs[k], y), (outs[zs + k], 1 - y)):
                out[0:n, :] = turn[pl.ds(pl.multiple_of(side * n, n), n), :]
                out[n:, :] = jnp.zeros((VEC, out.shape[1]), BF16)
                cols = pl.ds(pl.multiple_of((2 * z + side) * n, n), n)
                out[n:, 0:n] = vec[:, cols].astype(BF16)
        return
    keep, send = outs
    for t in range(d // TILE):
        rows = slice(t * TILE, (t + 1) * TILE)
        turn[:, 0:e] = dot_tn(held[:, rows], back[...]).astype(BF16)
        turn[:, e:] = (
            o0[rows, :].astype(F32) + o1[rows, :].astype(F32) + o2[rows, :].astype(F32)
        ).astype(BF16)
        for j in range(per):
            z = t * per + j
            for out, side in ((keep, y), (send, 1 - y)):
                out[z, 0:n, :] = turn[pl.ds(pl.multiple_of((2 * j + side) * n, n), n), :]
    low = vec[...].astype(BF16)
    for z in range(zs):
        first, second = (low[:, (2 * z + i) * n : (2 * z + i + 1) * n] for i in range(2))
        for out, pick in ((keep, y == 0), (send, y != 0)):
            out[z, n:, :] = jnp.zeros((VEC, out.shape[2]), BF16)
            out[z, n:, 0:n] = jnp.where(pick, first, second)


def qkvo_grads(ids, blocks, back, out_parts, sums, fs):
    nb, block, d = blocks[0].shape
    total, e = back.shape
    n = d // fs
    wide = e + out_parts[0].shape[1]
    if fs == 8 and fits(n):
        outs = (struct((n + VEC, wide), BF16),) * 8
    else:
        outs = (struct((fs // 2, n + VEC, wide), BF16),) * 2
    return call(
        qkvo_grads_kernel,
        outs,
        (ids, *(hbm(b) for b in blocks), back, *out_parts, *sums),
        name="qkvo_grads",
        in_specs=[whole(pltpu.SMEM)] + [whole(HBM)] * SEQ_N + [whole()] * 8,
        scratch=[
            VMEM((total, d), BF16),
            VMEM((VEC, d), F32),
            VMEM((TILE, wide), BF16),
            pltpu.SemaphoreType.DMA((nb * SEQ_N,)),
        ],
        flops=2 * total * d * e,
    )


def finish_ffn_kernel(fs, ids, *refs):
    ups, downs, (up, down) = refs[:4], refs[4:8], refs[8:]
    s = ids[0]
    w = up.shape[1] // fs // SEQ_N
    for r in range(SEQ_N):
        at = s ^ r
        for j in range(fs):
            place = pl.ds(pl.multiple_of((j * SEQ_N + at) * w, w), w)
            up[:, place] = ups[r][:, j * w : (j + 1) * w].astype(F32)
        down[pl.ds(pl.multiple_of(at * w, w), w), :] = downs[r][...].astype(F32)


def finish_qkvo_kernel(ids, c0, c1, c2, c3, wq, wk, wv, wo, *vectors):
    s = ids[0]
    n = wq.shape[0]
    c = wq.shape[1] // SEQ_N
    total = 0.0
    for r, small in enumerate((c0, c1, c2, c3)):
        cols = pl.ds(pl.multiple_of((s ^ r) * c, c), c)
        for i, out in enumerate((wq, wk, wv, wo)):
            out[:, cols] = small[0:n, i * c : (i + 1) * c].astype(F32)
        total = total + small[n:, 0:n].astype(F32)
    for row, out in enumerate(vectors[:ROW_UB]):
        out[...] = total[row : row + 1, :].reshape(n)
    for j in range(SEQ_N):
        vectors[ROW_UB][j * n : (j + 1) * n] = total[ROW_UB + j : ROW_UB + j + 1, :].reshape(n)


def finish_ffn(ids, s, ups, downs, fs):
    n = ups[0].shape[0]
    w, d = downs[0].shape
    hidden = SEQ_N * fs * w
    if fits(n):
        return call(
            functools.partial(finish_ffn_kernel, fs),
            (struct((n, hidden), F32), struct((SEQ_N * w, d), F32)),
            (ids, *ups, *downs),
            name="finish_ffn",
            in_specs=[whole(pltpu.SMEM)] + [whole()] * 8,
        )
    order = jnp.arange(SEQ_N) ^ s
    up, down = (jnp.stack(v)[order].astype(F32) for v in (ups, downs))
    return (
        up.reshape(SEQ_N, n, fs, w).transpose(1, 2, 0, 3).reshape(n, hidden),
        down.reshape(SEQ_N * w, d),
    )


def finish_qkvo(ids, s, small):
    n = small[0].shape[0] - VEC
    d = small[0].shape[1]
    c = d // SEQ_N
    if fits(n):
        outs = (struct((n, d), F32),) * 4 + (struct((n,), F32),) * ROW_UB + (struct((SEQ_N * n,), F32),)
        done = call(
            finish_qkvo_kernel,
            outs,
            (ids, *small),
            name="finish_qkvo",
            in_specs=[whole(pltpu.SMEM)] + [whole()] * 4,
        )
        return done[:4], done[4:]
    small = jnp.stack(small)[jnp.arange(SEQ_N) ^ s].astype(F32)
    four = small[:, :n].reshape(SEQ_N, n, 4, c).transpose(2, 1, 0, 3).reshape(4, n, d)
    total = jnp.sum(small[:, n:, :n], 0)
    vectors = [total[row] for row in range(ROW_UB)]
    vectors.append(total[ROW_UB : ROW_UB + SEQ_N].reshape(SEQ_N * n))
    return [four[i] for i in range(4)], vectors


def body(fs, tokens_in, cotangent, query_weight, key_weight, value_weight, out_weight, up_weight,
         down_weight, query_bias, value_bias, out_bias, up_bias, down_bias, first_gain, first_shift,
         second_gain, second_shift):
    nb, block, d = tokens_in.shape
    rows = nb * block
    s = lax.axis_index(SEQ)
    f = lax.axis_index(FSDP)
    ids = jnp.stack([s, f]).astype(jnp.int32)
    flat = lambda a: a.reshape(rows, a.shape[-1])
    deep = lambda a: a.reshape(nb, block, a.shape[-1])

    scope = jax.named_scope
    early = pack_early(
        ids, s, query_weight, key_weight, value_weight, out_weight,
        [query_bias, value_bias, out_bias, down_bias, first_gain, first_shift, second_gain, second_shift],
        up_bias,
    )
    packed = pack_late(ids, s, fs, up_weight, down_weight)
    hidden = up_weight.shape[1] // SEQ_N
    with scope("tok"):
        tokens = gather_seq(tokens_in)
    with scope("wqkv"):
        wqkv = gather_early(early, fs)
    with scope("ffnw"):
        packed = lax.all_gather(after(packed, wqkv[0], *wqkv[3:5]), FSDP)
    with scope("wo"):
        n = d // fs
        wo = jnp.stack([p[..., :n, 3 * (d // SEQ_N) :] for p in wqkv])
        wo = [wo, seq_swap(wo, 1), seq_swap(wo, 2)]
    qkv, lse, *mixtures, wqkv, vec = attend(ids, tokens, wqkv, fs)
    with scope("wo"):
        wo.append(seq_swap(after(wo[2], vec), 1))
    with scope("mix"):
        mixtures = exchange_seq([flat(m) for m in mixtures])
    attn_sum, normed, first_low, mix, wo = out_project(ids, mixtures, wo, flat(tokens_in), vec)
    with scope("first"):
        firsts = gather_seq(first_low)
    *parts, gelu, slope = ffn(ids, firsts, packed, vec, hidden, fs)
    with scope("ffn"):
        parts, _ = reduce_seq(parts)
    layer_out, ffn_grad, down_low, second_sums = second_norm(normed, parts, flat(cotangent), vec)
    with scope("low"):
        lows = gather_seq(down_low)
    down_full = down_grads(gelu, lows)
    with scope("gdown"):
        down_grad = lax.psum_scatter(down_full, FSDP, scatter_dimension=0, tiled=True)
    slope = after(slope, down_full)
    *parts, up_low, up_sums = ffn_back(ids, lows, packed, slope, fs)
    with scope("ffnback"):
        parts, onward = reduce_seq(parts)
    keep_up, send_up = up_grads(ids, firsts, after(up_low, parts[1]), fs)
    with scope("gup"):
        came_up = swap_y(send_up)
    parts[0] = after(parts[0], keep_up)
    attn_grad, first_sums, *pieces, out_low = first_norm(ids, ffn_grad, parts, attn_sum, vec, wo)
    with scope("mixback"):
        grads = exchange_seq(pieces)
    out_parts = out_grads(ids, mix, out_low)
    with scope("outs"):
        out_parts, onward = reduce_seq(out_parts, *grads[2:])
    grads[0] = after(grads[0], onward, keep_up)
    back, back_sums, *parts = attend_back(qkv, lse, [deep(g) for g in grads], wqkv.reshape(d, -1))
    with scope("gup"):
        up_terms = add(keep_up, after(came_up, back))
        up_grad = sum_z(up_terms)
    back = after(back, up_terms, down_grad)
    pieces = qkvo_grads(
        ids, tokens, back.reshape(-1, back.shape[-1]), out_parts,
        (back_sums, first_sums, second_sums, up_sums), fs,
    )
    with scope("gqkvo"):
        half = len(pieces) // 2
        keep, send = pieces[:half], pieces[half:]
        if half == 1:
            small = scatter_fsdp(keep[0], swap_y(send[0]))
        else:
            came = {k: swap_y(send[k]) for k in (1, 2, 3, 0)}
            small = scatter_fsdp(keep, came)
    with scope("input"):
        terms, _ = reduce_seq([flat(p) for p in parts])
    input_grad = attn_grad + (
        terms[0].astype(F32) + terms[1].astype(F32) + terms[2].astype(F32)
    )
    with scope("fdown"):
        downs = gather_seq(after(down_grad, terms[2]))
    with scope("fup"):
        ups = gather_seq(after(up_grad, downs[2]))
    up, down = finish_ffn(ids, s, ups, downs, fs)
    with scope("small"):
        small = gather_seq(small, up)
    four, vecs = finish_qkvo(ids, s, small)
    return (
        deep(layer_out), deep(input_grad), *four, up, down,
        vecs[ROW_QB], vecs[ROW_VB], vecs[ROW_OB], vecs[ROW_UB], vecs[ROW_DB],
        vecs[ROW_G1], vecs[ROW_S1], vecs[ROW_G2], vecs[ROW_S2],
    )


def solution(mesh):
    count, fs = mesh.shape["seq"], mesh.shape["fsdp"]
    assert count == SEQ_N and fs % 4 == 0
    inner = Mesh(mesh.devices.reshape(2, 2, fs // 2, 2), SEQ + FSDP)
    rows, matrix, vector = P(FSDP, SEQ, None), P(FSDP, None), P(FSDP)
    in_specs = (rows,) * 2 + (matrix,) * 6 + (vector,) * 9
    return jax.shard_map(
        functools.partial(body, fs), mesh=inner, in_specs=in_specs, out_specs=in_specs, check_vma=False
    )
```
